128 devices in a mesh: ty: 4 (over y), tx: 32 (over z, x, core).
Axes of the slice: x: 4, y: 4, z: 4, core: 2. Of those that a mesh axis runs over, the one named last changes fastest.
Arguments:
- block_sums: float32 [16384, 1, 1024], P(('ty', 'tx')), may hold values from -6 to 6
- block_weights: float32 [16384, 1, 1024], P(('ty', 'tx')), may hold values from 0.1 to 2
- block_tile: int32 [16384, 1], P(('ty', 'tx')), may hold values from 0 to 127; in each aligned block of 128 rows (0 to 127, 128 to 255, ...) at most 2 rows name the same one
- block_row: int32 [16384], P(('ty', 'tx')), may hold values from 0 to 127
- prior_weight: float32 [512, 32768], P('ty', 'tx'), may hold values from 0.1 to 1
Outputs:
- solution_field: float32 [512, 32768], P('ty', 'tx')
- residual: float32 [512, 32768], P('ty', 'tx')
The draws below stay inside these ranges and needn't reach their ends.
Inputs may be any that keep to these rules, and one draw needn't show every extreme that they name: `block_tile`: among the 128 blocks of one log shard no tile is named more than 2 times, a bound that some block reaches.
All inputs are finite; a program needn't handle non-finite values.
Results may differ from the reference program's by a relative error of at most 0.0003.
Values sent between devices are 32-bit elements; how exact they have to be, the bound alone decides.
No kernel may reach another device: no remote copies, remote signals or barrier semaphores. Data moves between devices by JAX's collectives and lax.ppermute only.
A program may use at most 64 MiB of HBM per device.

```python
import math
import jax
import jax.numpy as jnp
import numpy as np
from jax import lax

ROWS = 128
COLS = 1024
HALF = 32
ITERS = 2
BLK_DEV = 128
BAND = 1
CAP = 2
BLOCKS = 16384
NY = 512
NX = 32768
N_TX = 32
DEVICES = 128


def set_ends(drawn, rng, least, top_value):
    extent = drawn.shape
    index_at = [jax.random.randint(jax.random.fold_in(rng, axis), (), 0, extent[axis]) for axis in range(len(extent))]
    drawn = drawn.at[tuple(index_at)].set(least)
    longest = extent.index(max(extent))
    index_at[longest] = (index_at[longest] + 1) % extent[longest]
    return drawn.at[tuple(index_at)].set(top_value)


def steps_of(stream_key, shape, cuts, smallest, top_value):
    level = 1.0
    for axis_at, parts in cuts:
        heights = jax.random.uniform(jax.random.fold_in(jax.random.fold_in(stream_key, 6), axis_at), (parts,), jnp.float32, smallest / len(cuts), top_value / len(cuts))
        level = level * jnp.repeat(jnp.exp(heights), shape[axis_at] // parts).reshape((-1,) + (1,) * (len(shape) - 1 - axis_at))
    return level


def assign_block(rng, own, number, rows, count, top, limit, slope):
    sequence = jax.random.permutation(rng, count)
    packed, ordinary = portions_of(count, rows * top, limit, slope, True), portions_of(count, rows * top, limit, slope, False)
    places = jnp.arange(count)

    def named(sizes, rotation):
        used = int((sizes > 0).sum())
        fixed = max(1, used // 4)
        passed = fixed + (places - fixed + rotation * (used - fixed)) % max(1, count - fixed)
        return jnp.zeros((count,), jnp.int32).at[sequence[jnp.where(places < fixed, places, passed)]].set(jnp.asarray(sizes, jnp.int32))

    sizes = jnp.where(number % 4 == 0, named(packed, number // 4), named(ordinary, number - number // 4 - 1))
    mixed = jax.random.permutation(jax.random.fold_in(own, 3), count)
    giver, receiver = mixed[0:count // 2 * 2:2], mixed[1:count // 2 * 2:2]
    slack = jnp.minimum(sizes[giver] - 1, limit - sizes[receiver]) // 2
    slack = jnp.where((giver == sequence[0]) | (receiver == sequence[0]) | (sizes[receiver] == 0), 0, jnp.maximum(slack, 0))
    passed = jax.random.randint(jax.random.fold_in(own, 4), (count // 2,), 0, 1 << 20) % (slack + 1)
    sizes = sizes.at[giver].add(-passed).at[receiver].add(passed)
    members = jnp.searchsorted(jnp.cumsum(sizes), jnp.arange(rows * top), side="right").astype(jnp.int32)
    listing = members.reshape(top, rows).T
    listing = listing[jax.random.permutation(jax.random.fold_in(own, 1), rows)]
    rotation = jax.random.randint(jax.random.fold_in(own, 2), (rows, 1), 0, top)
    return jnp.take_along_axis(listing, (jnp.arange(top)[None, :] + rotation) % top, axis=1)


def portions_of(number_of, total, reach, slope, full):
    portions = [(1 << 20) // math.isqrt(rank ** slope) + 1 for rank in range(1, number_of + 1)]
    largest = reach if full else min(reach, max(-(-total // number_of), total * portions[0] // sum(portions)))
    least = 1 if total - largest >= number_of - 1 else 0
    holding, surplus = [largest] + [least] * (number_of - 1), total - largest - least * (number_of - 1)
    while surplus > 0:
        candidates = [i for i in range(1, number_of) if holding[i] < largest] or [i for i in range(1, number_of) if holding[i] < reach]
        whole, remaining = sum([portions[i] for i in candidates]), surplus
        for i in candidates:
            more = min(reach - holding[i], max(1, remaining * portions[i] // whole), surplus)
            holding[i] = holding[i] + more
            surplus = surplus - more
    return np.array(holding)


def noise(key, shape, scale, limit, pieces=(), held_as=jnp.bfloat16):
    array = scale * jax.random.normal(key, shape, jnp.float32)
    if pieces:
        array = array * steps_of(key, shape, pieces, -0.22, 0.18)
    return jnp.clip(array, -limit, limit).astype(held_as)


def setup_inputs(seed: int = 0) -> dict:
    streams_of = jax.random.split(jax.random.key(seed), 6)
    block_sums = noise(streams_of[0], (BLOCKS, BAND, COLS), 1.0, 6.0, ((0, 128),), jnp.float32)
    block_weights = jnp.clip(jnp.exp(math.log(2.0) - 2.9957323 * jax.random.uniform(streams_of[1], (BLOCKS, BAND, COLS), jnp.float32) ** steps_of(streams_of[1], (BLOCKS, BAND, COLS), ((0, 128),), -0.2, 0.2)), 0.1, 2.0)
    block_tile_keys = jax.random.split(jax.random.fold_in(streams_of[2], 1), BLOCKS // BLK_DEV)
    block_tile_turns = jax.random.permutation(jax.random.fold_in(streams_of[2], 3), BLOCKS // BLK_DEV)
    block_tile = jax.vmap(lambda own, number: assign_block(jax.random.fold_in(streams_of[2], 2), own, number, BLK_DEV, DEVICES, 1, CAP, 2))(block_tile_keys, block_tile_turns).reshape((BLOCKS, 1))
    block_row = set_ends(jax.random.randint(streams_of[3], (BLOCKS,), 0, BLK_DEV), jax.random.fold_in(streams_of[3], 1), 0, BLK_DEV - 1).astype(jnp.int32)
    prior_weight = jnp.clip(jnp.exp(math.log(1.0) - 2.3025851 * jax.random.uniform(streams_of[4], (NY, NX), jnp.float32) ** steps_of(streams_of[4], (NY, NX), ((0, 4), (1, 32)), -0.2, 0.2)), 0.1, 1.0)
    return dict(block_sums=block_sums, block_weights=block_weights, block_tile=block_tile, block_row=block_row, prior_weight=prior_weight)


def kernel_taps():
    dist = jnp.abs(jnp.arange(-HALF, HALF + 1).astype(jnp.float32))
    scaled = dist / (HALF + 1.0)
    taps = (1.0 - scaled) ** 4 * (1.0 + 4.0 * scaled)
    return taps / jnp.sum(taps)

def smooth(field, taps):
    image = field[None, None]
    image = lax.conv_general_dilated(image, taps[None, None, :, None], (1, 1), [(HALF, HALF), (0, 0)], precision=lax.Precision.HIGHEST)
    image = lax.conv_general_dilated(image, taps[None, None, None, :], (1, 1), [(0, 0), (HALF, HALF)], precision=lax.Precision.HIGHEST)
    return image[0, 0]

def reference(block_sums, block_weights, block_tile, block_row, prior_weight):
    total_blocks = block_sums.shape[0]
    zeros = jnp.zeros((NY, NX), jnp.float32)

    def place(index, carry):
        sums, weights = carry
        target = block_tile[index, 0].astype(jnp.int32)
        top = (target // N_TX * ROWS + block_row[index] * BAND).astype(jnp.int32)
        left = (target % N_TX * COLS).astype(jnp.int32)
        old_sums = lax.dynamic_slice(sums, (top, left), (BAND, COLS))
        old_weights = lax.dynamic_slice(weights, (top, left), (BAND, COLS))
        sums = lax.dynamic_update_slice(sums, old_sums + block_sums[index], (top, left))
        weights = lax.dynamic_update_slice(weights, old_weights + block_weights[index], (top, left))
        return (sums, weights)
    cell_sums, cell_weights = lax.fori_loop(0, total_blocks, place, (zeros, zeros))
    root = jnp.sqrt(prior_weight + cell_weights)
    right_side = cell_sums / root
    taps = kernel_taps()

    def operate(field):
        return 0.5 * field + root * smooth(root * field, taps)
    solution_field = jnp.zeros_like(right_side)
    residual, direction = (right_side, right_side)
    norm_now = jnp.sum(residual * residual)
    for step in range(ITERS):
        image = operate(direction)
        alpha = norm_now / jnp.sum(direction * image)
        solution_field = solution_field + alpha * direction
        residual = residual - alpha * image
        norm_next = jnp.sum(residual * residual)
        direction = residual + norm_next / norm_now * direction
        norm_now = norm_next
    return (solution_field, residual)
```

```python
import functools

import jax
import jax.numpy as jnp
import numpy as np
from jax import lax
from jax.experimental import pallas as pl
from jax.experimental.pallas import tpu as pltpu
from jax.sharding import Mesh
from jax.sharding import PartitionSpec as P

HALF = 32
LANES = 128
SLOTS = 2
TY_TX = ("ty", "tx_0", "tx_1", "tx_2")
TX = ("tx_0", "tx_1", "tx_2")
F32 = jnp.float32
BF16 = jnp.bfloat16


def taps(offset):
    def raw(d):
        scaled = np.abs(d) / (HALF + 1.0)
        return np.where(np.abs(d) <= HALF, (1.0 - scaled) ** 4 * (1.0 + 4.0 * scaled), 0.0)

    values = raw(offset) / raw(np.arange(-HALF, HALF + 1)).sum()
    head = values.astype(BF16)
    tail = (values - head.astype(np.float64)).astype(BF16)
    return jnp.asarray(head), jnp.asarray(tail)


def split2(x):
    head = x.astype(BF16)
    return head, (x - head.astype(F32)).astype(BF16)


def split3(x):
    head = x.astype(BF16)
    rest = x - head.astype(F32)
    mid = rest.astype(BF16)
    return head, mid, (rest - mid.astype(F32)).astype(BF16)


def mm(a, b):
    return jnp.dot(a, b, preferred_element_type=F32)


def pick(select, x):
    head, mid, tail = split3(x)
    return mm(select, tail) + mm(select, mid) + mm(select, head)


def smooth3(left, right):
    (lh, ll), (rh, rl) = left, right
    return mm(ll, rh) + mm(lh, rl) + mm(lh, rh)


def iota(shape, dim):
    return lax.broadcasted_iota(jnp.int32, shape, dim)


def pack_kernel(n_tx, parts, length, tile_ref, row_ref, sums_ref, weights_ref, out_ref):
    count = tile_ref.shape[1]
    devices = out_ref.shape[0] // length
    tile = tile_ref[...]
    t = iota((devices, count), 0)
    same = tile == t
    earlier = iota((count, count), 0) < iota((count, count), 1)
    before = mm(same.astype(F32).astype(BF16), earlier.astype(F32).astype(BF16))
    rank = jnp.sum(jnp.where(same, before, 0.0), axis=0, keepdims=True)
    column = lax.rem(t, n_tx)
    from_left = (tile + 1 == t) & (column != 0)
    from_right = (tile - 1 == t) & (column != n_tx - 1)

    def onehot(mask, k):
        return jnp.where(mask & (rank == float(k)), 1.0, 0.0)

    own = [onehot(same, k) for k in range(SLOTS)]
    own_all = jnp.concatenate(own, axis=0).astype(BF16)
    left_all = jnp.concatenate([onehot(from_left, k) for k in range(SLOTS)], axis=0).astype(BF16)
    right_all = jnp.concatenate(
        [jnp.concatenate([onehot(from_right, k), own[k]], axis=1) for k in range(SLOTS)], axis=0
    ).astype(BF16)

    for which, ref in enumerate((sums_ref, weights_ref)):
        for c in range(0, parts, 2):
            x = jnp.concatenate(
                [ref[pl.ds(c + i, count, stride=parts), :] for i in range(2)], axis=1
            )
            y = pick(own_all, x)
            for k in range(SLOTS):
                for i in range(2):
                    at = (which * SLOTS + k) * parts + c + i
                    out_ref[pl.ds(at, devices, stride=length), :] = y[
                        k * devices : (k + 1) * devices, i * LANES : (i + 1) * LANES
                    ]

    lane = iota((count, LANES), 1)
    number = jnp.transpose(
        jnp.broadcast_to(row_ref[...].astype(F32) + 1.0, (count, count))
    )
    last = parts - 1
    s_last = sums_ref[pl.ds(last, count, stride=parts), :]
    w_last = pltpu.roll(weights_ref[pl.ds(last, count, stride=parts), :], 64, 1)
    s_first = sums_ref[pl.ds(0, count, stride=parts), :]
    w_first = pltpu.roll(weights_ref[pl.ds(0, count, stride=parts), :], 64, 1)
    left_rows = jnp.where(
        lane >= 64, s_last, jnp.where(lane >= 32, w_last, jnp.where(lane == 0, number, 0.0))
    )
    right_rows = jnp.where(
        lane < 64, s_first, jnp.where(lane < 96, w_first, jnp.where(lane == 96, number, 0.0))
    )
    own_rows = jnp.where(lane == 97, number, 0.0)
    to_left = pick(left_all, left_rows)
    to_right = pick(right_all, jnp.concatenate([right_rows, own_rows], axis=0))
    base = 2 * SLOTS * parts
    for k in range(SLOTS):
        part = slice(k * devices, (k + 1) * devices)
        out_ref[pl.ds(base + k, devices, stride=length), :] = to_left[part]
        out_ref[pl.ds(base + SLOTS + k, devices, stride=length), :] = to_right[part]


def select_kernel(
    parts, length, got_ref, prior_ref, prior_right_ref, prior_left_ref, s_ref, w_ref, up_ref, down_ref
):
    rows, cols = prior_ref.shape
    devices = got_ref.shape[0] // length
    base = 2 * SLOTS * parts
    from_left = [got_ref[pl.ds(base + k, devices, stride=length), :] for k in range(SLOTS)]
    from_right = [got_ref[pl.ds(base + SLOTS + k, devices, stride=length), :] for k in range(SLOTS)]
    left_t = [jnp.transpose(x) for x in from_left]
    right_t = [jnp.transpose(x) for x in from_right]
    wanted = (iota((rows, devices), 0) + 1).astype(F32)

    def chooser(lists, at):
        return jnp.concatenate(
            [jnp.where(x[at : at + 1, :] == wanted, 1.0, 0.0) for x in lists], axis=1
        ).astype(BF16)

    own = chooser(right_t, 97)
    for which, dst in enumerate((s_ref, w_ref)):
        for c in range(0, parts, 2):
            x = jnp.concatenate(
                [
                    jnp.concatenate(
                        [
                            got_ref[
                                pl.ds((which * SLOTS + k) * parts + c + i, devices, stride=length), :
                            ]
                            for i in range(2)
                        ],
                        axis=1,
                    )
                    for k in range(SLOTS)
                ],
                axis=0,
            )
            y = pick(own, x)
            at = slice(c * LANES, (c + 2) * LANES)
            if which == 1:
                y = y + prior_ref[:, at]
            dst[:, at] = y
    left = pick(chooser(left_t, 0), jnp.concatenate(from_left, axis=0))
    right = pick(chooser(right_t, 96), jnp.concatenate(from_right, axis=0))
    lane = iota((rows, LANES), 1)
    s_ref[:, cols:] = jnp.where(lane < 64, right, left)
    w_ref[:, cols:] = jnp.where(
        lane < 32,
        pltpu.roll(right, 64, 1) + prior_right_ref[...],
        jnp.where(lane >= 96, pltpu.roll(left, 64, 1) + prior_left_ref[...], 0.0),
    )
    up_ref[: 2 * HALF, :] = s_ref[: 2 * HALF, :]
    up_ref[2 * HALF :, :] = w_ref[:HALF, :]
    down_ref[: 2 * HALF, :] = s_ref[rows - 2 * HALF :, :]
    down_ref[2 * HALF :, :] = w_ref[rows - HALF :, :]


def conv_kernel(
    s_ref,
    w_ref,
    above_ref,
    below_ref,
    row_h_ref,
    row_l_ref,
    col_h_ref,
    col_l_ref,
    edge_h_ref,
    edge_l_ref,
    y0_ref,
    y1_ref,
    moments_ref,
    mid_ref,
    z_ref,
):
    rows, wide = s_ref.shape
    cols = wide - LANES
    tall = rows + 2 * HALF
    col = (col_h_ref[...], col_l_ref[...])
    edge = (edge_h_ref[...], edge_l_ref[...])

    def block(ref, c, height):
        lo, hi = (c - 1) * LANES, (c + 3) * LANES
        if c == 0:
            x = jnp.concatenate([ref[:height, cols:], ref[:height, :hi]], axis=1)
        else:
            x = ref[:height, lo:hi]
        return smooth3(split2(x), col)

    row = (row_h_ref[...], row_l_ref[...])
    for c in range(0, wide, LANES * 3):
        at = slice(c, c + LANES * 3)
        full = jnp.concatenate(
            [above_ref[: 2 * HALF, at], s_ref[:, at], below_ref[: 2 * HALF, at]], axis=0
        )
        mid_ref[:, at] = smooth3(row, split2(full))
    total_sy = jnp.zeros((rows, 2 * LANES), F32)
    total_zy = jnp.zeros((rows, 2 * LANES), F32)
    total_ss = jnp.zeros((rows, 2 * LANES), F32)
    for c in range(0, cols // LANES, 2):
        at = slice(c * LANES, (c + 2) * LANES)
        y = block(mid_ref, c, tall)
        w = jnp.concatenate([above_ref[2 * HALF :, at], w_ref[:, at], below_ref[2 * HALF :, at]], axis=0)
        z = w * y
        z_ref[:, at] = z
        inner = y[HALF : HALF + rows]
        y0_ref[:, at] = inner
        s = s_ref[:, at]
        total_sy += s * inner
        total_zy += z[HALF : HALF + rows] * inner
        total_ss += s * s / w_ref[:, at]
    x = jnp.concatenate([mid_ref[:, cols - LANES :], mid_ref[:, :LANES]], axis=1)
    y = smooth3(split2(x), edge)
    w = jnp.concatenate([above_ref[2 * HALF :, cols:], w_ref[:, cols:], below_ref[2 * HALF :, cols:]], axis=0)
    z_ref[:, cols:] = w * y

    row = (row_h_ref[:rows, :tall], row_l_ref[:rows, :tall])
    for c in range(0, wide, LANES * 3):
        at = slice(c, c + LANES * 3)
        mid_ref[:rows, at] = smooth3(row, split2(z_ref[:, at]))
    total_zz = jnp.zeros((rows, 2 * LANES), F32)
    for c in range(0, cols // LANES, 2):
        at = slice(c * LANES, (c + 2) * LANES)
        y = block(mid_ref, c, rows)
        y1_ref[:, at] = y
        total_zz += z_ref[HALF : HALF + rows, at] * y
    lane = iota((1, LANES), 1)
    packed = jnp.zeros((1, LANES), F32)
    for i, total in enumerate((total_ss, total_sy, total_zy, total_zz)):
        value = jnp.sum(jnp.sum(total, axis=0, keepdims=True), axis=1, keepdims=True)
        packed = jnp.where(lane == i, value, packed)
    moments_ref[...] = jnp.broadcast_to(packed, moments_ref.shape)


def final_kernel(moments_ref, s_ref, w_ref, y0_ref, y1_ref, x_ref, r_ref):
    totals = jnp.sum(moments_ref[...], axis=0, keepdims=True)
    lane = iota(totals.shape, 1)
    m0, n1, n2, n3 = (
        jnp.sum(jnp.where(lane == i, totals, 0.0), axis=1, keepdims=True) for i in range(4)
    )
    mu = n1 / m0
    a = m0 / (0.5 * m0 + n1)
    vv = n2 - mu * n1
    vbv = n3 - 2.0 * mu * n2 + mu * mu * n1
    beta = a * a * vv / m0
    step = vv / (0.5 * vv + vbv - a * vv * vv / m0)
    x_r0 = a + step * beta + step * a * mu
    x_b0 = -step * a
    r_r0 = a * mu - step * (0.5 * a * mu + 0.5 * beta)
    r_b0 = -a - step * (a * mu - 0.5 * a + beta)
    r_b1 = step * a
    w = w_ref[...]
    root = jnp.sqrt(w)
    r0 = s_ref[...] / w
    y0 = y0_ref[...]
    x_ref[...] = root * (x_r0 * r0 + x_b0 * y0)
    r_ref[...] = root * (r_r0 * r0 + r_b0 * y0 + r_b1 * y1_ref[...])


def vmem(count):
    return [pl.BlockSpec(memory_space=pltpu.VMEM)] * count


def call(kernel, shapes, *args, scratch=(), name, flops=0):
    moved = sum(int(np.prod(x.shape)) * x.dtype.itemsize for x in args)
    return pl.pallas_call(
        kernel,
        out_shape=[jax.ShapeDtypeStruct(s, F32) for s in shapes],
        in_specs=vmem(len(args)),
        out_specs=vmem(len(shapes)),
        scratch_shapes=list(scratch),
        compiler_params=pltpu.CompilerParams(vmem_limit_bytes=40 << 20),
        cost_estimate=pl.CostEstimate(flops=flops, bytes_accessed=moved, transcendentals=0),
        name=name,
    )(*args)


def neighbours(axes, step):
    count = int(np.prod([lax.axis_size(a) for a in axes]))
    pairs = [(i, i + 1) for i in range(count - 1)]
    return pairs if step > 0 else [(b, a) for a, b in pairs]


def shards(block_sums, block_weights, block_tile, block_row, prior_weight):
    devices = lax.axis_size(TY_TX)
    n_tx = lax.axis_size(TX)
    blocks, _, cols = block_sums.shape
    rows = prior_weight.shape[0]
    parts = cols // LANES
    length = 2 * SLOTS * parts + 2 * SLOTS
    wide = cols + LANES
    slab = (3 * HALF, wide)

    prior_right = lax.ppermute(prior_weight[:, :LANES], TX, neighbours(TX, -1))
    prior_left = lax.ppermute(prior_weight[:, cols - LANES :], TX, neighbours(TX, 1))

    (message,) = call(
        functools.partial(pack_kernel, n_tx, parts, length),
        [(devices * length, LANES)],
        block_tile.reshape(1, blocks),
        block_row.reshape(1, blocks),
        block_sums.reshape(blocks * parts, LANES),
        block_weights.reshape(blocks * parts, LANES),
        name="pack",
    )
    got = lax.all_to_all(
        message.reshape(devices, 1, length * LANES), TY_TX, split_axis=0, concat_axis=0, tiled=True
    ).reshape(devices * length, LANES)
    s, w, up, down = call(
        functools.partial(select_kernel, parts, length),
        [(rows, wide), (rows, wide), slab, slab],
        got,
        prior_weight,
        prior_right,
        prior_left,
        name="select",
    )
    above = lax.ppermute(down, "ty", neighbours(("ty",), 1))
    below = lax.ppermute(up, "ty", neighbours(("ty",), -1))

    tall = rows + 2 * HALF
    row_taps = taps(np.arange(tall)[:, None] - np.arange(rows + 4 * HALF)[None, :] + HALF)
    col_taps = taps(np.arange(2 * LANES)[None, :] - np.arange(4 * LANES)[:, None] + LANES)
    ring = np.where(np.arange(LANES) < 64, cols, -LANES) + np.arange(LANES)
    near = np.concatenate([np.arange(cols - LANES, cols), ring, np.arange(LANES)])
    edge_taps = taps(ring[None, :] - near[:, None])
    y0, y1, moments = call(
        conv_kernel,
        [(rows, cols), (rows, cols), (devices, LANES)],
        s,
        w,
        above,
        below,
        *row_taps,
        *col_taps,
        *edge_taps,
        scratch=[pltpu.VMEM((tall, wide), F32), pltpu.VMEM((tall, wide), F32)],
        name="smooth",
    )
    moments = lax.all_to_all(
        moments.reshape(devices, 1, LANES), TY_TX, split_axis=0, concat_axis=0, tiled=True
    ).reshape(devices, LANES)
    whole = lambda shape: pl.BlockSpec(shape, lambda i: (0, 0))
    return tuple(
        pl.pallas_call(
            final_kernel,
            grid=(1,),
            out_shape=[jax.ShapeDtypeStruct((rows, cols), F32)] * 2,
            in_specs=[whole((devices, LANES))] + [whole((rows, cols))] * 4,
            out_specs=[whole((rows, cols))] * 2,
            compiler_params=pltpu.CompilerParams(vmem_limit_bytes=40 << 20),
            name="combine",
        )(moments, s, w, y0, y1)
    )


def solution(mesh):
    split = Mesh(mesh.devices.reshape(mesh.shape["ty"], 4, 4, 2), ("ty", "tx_0", "tx_1", "tx_2"))
    in_specs = (P(TY_TX, None, None), P(TY_TX, None, None), P(TY_TX, None), P(TY_TX), P("ty", TX))
    out_specs = (P("ty", TX), P("ty", TX))
    return jax.shard_map(
        shards, mesh=split, in_specs=in_specs, out_specs=out_specs, check_vma=False
    )
```

```python
import functools

import jax
import jax.numpy as jnp
import numpy as np
from jax import lax
from jax.experimental import pallas as pl
from jax.experimental.pallas import tpu as pltpu
from jax.sharding import Mesh
from jax.sharding import PartitionSpec as P

HALF = 32
LANES = 128
SLOTS = 2
GROUPS = 2
CHUNKS = 4
TY_TX = ("ty", "tx_0", "tx_1", "tx_2")
TX = ("tx_0", "tx_1", "tx_2")
F32 = jnp.float32
BF16 = jnp.bfloat16


def taps(offset):
    def raw(d):
        scaled = np.abs(d) / (HALF + 1.0)
        return np.where(np.abs(d) <= HALF, (1.0 - scaled) ** 4 * (1.0 + 4.0 * scaled), 0.0)

    values = raw(offset) / raw(np.arange(-HALF, HALF + 1)).sum()
    head = values.astype(BF16)
    tail = (values - head.astype(np.float64)).astype(BF16)
    return jnp.asarray(head), jnp.asarray(tail)


def split2(x):
    head = x.astype(BF16)
    return head, (x - head.astype(F32)).astype(BF16)


def split3(x):
    head = x.astype(BF16)
    rest = x - head.astype(F32)
    mid = rest.astype(BF16)
    return head, mid, (rest - mid.astype(F32)).astype(BF16)


def mm(a, b):
    return jnp.dot(a, b, preferred_element_type=F32)


def pick(select, x):
    head, mid, tail = split3(x)
    return mm(select, tail) + mm(select, mid) + mm(select, head)


def smooth3(left, right):
    (lh, ll), (rh, rl) = left, right
    return mm(ll, rh) + mm(lh, rl) + mm(lh, rh)


def iota(shape, dim):
    return lax.broadcasted_iota(jnp.int32, shape, dim)


def pack_kernel(
    n_tx, parts, length, tile_hbm, row_hbm, sums_hbm, weights_hbm, out_hbm,
    tile_ref, row_ref, sums_ref, weights_ref, split_ref, out_ref, in_sem, out_sem
):
    fetches = [
        pltpu.make_async_copy(src, dst, in_sem.at[i])
        for i, (src, dst) in enumerate(
            (
                (tile_hbm, tile_ref),
                (row_hbm, row_ref),
                (sums_hbm, sums_ref),
                (weights_hbm, weights_ref),
            )
        )
    ]
    for fetch in fetches:
        fetch.start()
    fetches[0].wait()
    fetches[1].wait()
    count = tile_ref.shape[1]
    devices = out_ref.shape[0] // length
    group = devices // GROUPS
    tile = tile_ref[...]
    t = iota((devices, count), 0)
    same = tile == t
    earlier = iota((count, count), 0) < iota((count, count), 1)
    before = mm(same.astype(F32).astype(BF16), earlier.astype(F32).astype(BF16))
    rank = jnp.sum(jnp.where(same, before, 0.0), axis=0, keepdims=True)
    column = lax.rem(t, n_tx)
    from_left = (tile + 1 == t) & (column != 0)
    from_right = (tile - 1 == t) & (column != n_tx - 1)

    def onehot(mask, k):
        return jnp.where(mask & (rank == float(k)), 1.0, 0.0)

    own = [onehot(same, k) for k in range(SLOTS)]
    left = [onehot(from_left, k) for k in range(SLOTS)]
    right = [
        jnp.concatenate([onehot(from_right, k), own[k]], axis=1) for k in range(SLOTS)
    ]

    def of_group(masks, g):
        part = slice(g * group, (g + 1) * group)
        return jnp.concatenate([m[part] for m in masks], axis=0).astype(BF16)

    lane = iota((count, LANES), 1)
    number = jnp.transpose(jnp.broadcast_to(row_ref[...].astype(F32) + 1.0, (count, count)))
    for which, ref in enumerate((sums_ref, weights_ref)):
        fetches[2 + which].wait()
        for c in range(parts):
            at = slice((which * parts + c) * LANES, (which * parts + c + 1) * LANES)
            for i, piece in enumerate(split3(ref[pl.ds(c, count, stride=parts), :])):
                split_ref[i, :, at] = piece

    last = parts - 1
    s_last = sums_ref[pl.ds(last, count, stride=parts), :]
    w_last = pltpu.roll(weights_ref[pl.ds(last, count, stride=parts), :], 64, 1)
    s_first = sums_ref[pl.ds(0, count, stride=parts), :]
    w_first = pltpu.roll(weights_ref[pl.ds(0, count, stride=parts), :], 64, 1)
    left_rows = jnp.where(
        lane >= 64, s_last, jnp.where(lane >= 32, w_last, jnp.where(lane == 0, number, 0.0))
    )
    right_rows = jnp.where(
        lane < 64, s_first, jnp.where(lane < 96, w_first, jnp.where(lane == 96, number, 0.0))
    )
    own_rows = jnp.where(lane == 97, number, 0.0)
    both_rows = jnp.concatenate([right_rows, own_rows], axis=0)

    base = 2 * SLOTS * parts
    sends = []
    for g in range(GROUPS):
        first = g * group * length
        own_all = of_group(own, g)
        for c in range(0, 2 * parts, 2):
            at = slice(c * LANES, (c + 2) * LANES)
            y = (
                mm(own_all, split_ref[2, :, at])
                + mm(own_all, split_ref[1, :, at])
                + mm(own_all, split_ref[0, :, at])
            )
            which, chunk = divmod(c, parts)
            for k in range(SLOTS):
                for i in range(2):
                    to = first + (which * SLOTS + k) * parts + chunk + i
                    out_ref[pl.ds(to, group, stride=length), :] = y[
                        k * group : (k + 1) * group, i * LANES : (i + 1) * LANES
                    ]
        to_left = pick(of_group(left, g), left_rows)
        to_right = pick(of_group(right, g), both_rows)
        for k in range(SLOTS):
            part = slice(k * group, (k + 1) * group)
            out_ref[pl.ds(first + base + k, group, stride=length), :] = to_left[part]
            out_ref[pl.ds(first + base + SLOTS + k, group, stride=length), :] = to_right[part]
        span = pl.ds(first, group * length)
        send = pltpu.make_async_copy(out_ref.at[span], out_hbm.at[span], out_sem.at[g])
        send.start()
        sends.append(send)
    for send in sends:
        send.wait()


def select_kernel(
    parts, length, got_ref, prior_ref, prior_halo_ref, s_ref, w_ref, up_ref, down_ref
):
    rows, cols = prior_ref.shape
    devices = got_ref.shape[0] // length
    base = 2 * SLOTS * parts
    from_left = [got_ref[pl.ds(base + k, devices, stride=length), :] for k in range(SLOTS)]
    from_right = [got_ref[pl.ds(base + SLOTS + k, devices, stride=length), :] for k in range(SLOTS)]
    left_t = [jnp.transpose(x) for x in from_left]
    right_t = [jnp.transpose(x) for x in from_right]
    wanted = (iota((rows, devices), 0) + 1).astype(F32)

    def chooser(lists, at):
        return jnp.concatenate(
            [jnp.where(x[at : at + 1, :] == wanted, 1.0, 0.0) for x in lists], axis=1
        ).astype(BF16)

    own = chooser(right_t, 97)
    for which, dst in enumerate((s_ref, w_ref)):
        for c in range(0, parts, 2):
            x = jnp.concatenate(
                [
                    jnp.concatenate(
                        [
                            got_ref[
                                pl.ds((which * SLOTS + k) * parts + c + i, devices, stride=length), :
                            ]
                            for i in range(2)
                        ],
                        axis=1,
                    )
                    for k in range(SLOTS)
                ],
                axis=0,
            )
            y = pick(own, x)
            at = slice(c * LANES, (c + 2) * LANES)
            if which == 1:
                y = y + prior_ref[:, at]
            dst[:, at] = y
    left = pick(chooser(left_t, 0), jnp.concatenate(from_left, axis=0))
    right = pick(chooser(right_t, 96), jnp.concatenate(from_right, axis=0))
    lane = iota((rows, LANES), 1)
    s_ref[:, cols:] = jnp.where(lane < 64, right, left)
    w_ref[:, cols:] = prior_halo_ref[...] + jnp.where(
        lane < 32,
        pltpu.roll(right, 64, 1),
        jnp.where(lane >= 96, pltpu.roll(left, 64, 1), 0.0),
    )
    up_ref[: 2 * HALF, :] = s_ref[: 2 * HALF, :]
    up_ref[2 * HALF :, :] = w_ref[:HALF, :]
    down_ref[: 2 * HALF, :] = s_ref[rows - 2 * HALF :, :]
    down_ref[2 * HALF :, :] = w_ref[rows - HALF :, :]


def conv_kernel(
    s_ref,
    w_ref,
    above_ref,
    below_ref,
    row_h_ref,
    row_l_ref,
    col_h_ref,
    col_l_ref,
    edge_h_ref,
    edge_l_ref,
    y0_ref,
    y1_ref,
    moments_ref,
    mid_ref,
    z_ref,
):
    rows, wide = s_ref.shape
    cols = wide - LANES
    tall = rows + 2 * HALF
    col = (col_h_ref[...], col_l_ref[...])
    edge = (edge_h_ref[...], edge_l_ref[...])

    def block(ref, c, height):
        lo, hi = (c - 1) * LANES, (c + 3) * LANES
        if c == 0:
            x = jnp.concatenate([ref[:height, cols:], ref[:height, :hi]], axis=1)
        else:
            x = ref[:height, lo:hi]
        return smooth3(split2(x), col)

    row = (row_h_ref[...], row_l_ref[...])
    for c in range(0, wide, LANES * 3):
        at = slice(c, c + LANES * 3)
        full = jnp.concatenate(
            [above_ref[: 2 * HALF, at], s_ref[:, at], below_ref[: 2 * HALF, at]], axis=0
        )
        mid_ref[:, at] = smooth3(row, split2(full))
    total_sy = jnp.zeros((rows, 2 * LANES), F32)
    total_zy = jnp.zeros((rows, 2 * LANES), F32)
    total_ss = jnp.zeros((rows, 2 * LANES), F32)
    for c in range(0, cols // LANES, 2):
        at = slice(c * LANES, (c + 2) * LANES)
        y = block(mid_ref, c, tall)
        w = jnp.concatenate([above_ref[2 * HALF :, at], w_ref[:, at], below_ref[2 * HALF :, at]], axis=0)
        z = w * y
        z_ref[:, at] = z
        inner = y[HALF : HALF + rows]
        y0_ref[:, at] = inner
        s = s_ref[:, at]
        total_sy += s * inner
        total_zy += z[HALF : HALF + rows] * inner
        total_ss += s * s / w_ref[:, at]
    x = jnp.concatenate([mid_ref[:, cols - LANES :], mid_ref[:, :LANES]], axis=1)
    y = smooth3(split2(x), edge)
    w = jnp.concatenate([above_ref[2 * HALF :, cols:], w_ref[:, cols:], below_ref[2 * HALF :, cols:]], axis=0)
    z_ref[:, cols:] = w * y

    row = (row_h_ref[:rows, :tall], row_l_ref[:rows, :tall])
    for c in range(0, wide, LANES * 3):
        at = slice(c, c + LANES * 3)
        mid_ref[:rows, at] = smooth3(row, split2(z_ref[:, at]))
    total_zz = jnp.zeros((rows, 2 * LANES), F32)
    for c in range(0, cols // LANES, 2):
        at = slice(c * LANES, (c + 2) * LANES)
        y = block(mid_ref, c, rows)
        y1_ref[:, at] = y
        total_zz += z_ref[HALF : HALF + rows, at] * y
    lane = iota((1, LANES), 1)
    packed = jnp.zeros((1, LANES), F32)
    for i, total in enumerate((total_ss, total_sy, total_zy, total_zz)):
        value = jnp.sum(jnp.sum(total, axis=0, keepdims=True), axis=1, keepdims=True)
        packed = jnp.where(lane == i, value, packed)
    moments_ref[...] = jnp.broadcast_to(packed, moments_ref.shape)


def final_kernel(
    moments_ref, s_ref, w_ref, y0_ref, y1_ref, x_hbm, r_hbm, x_ref, r_ref, sem
):
    totals = jnp.sum(moments_ref[...], axis=0, keepdims=True)
    lane = iota(totals.shape, 1)
    m0, n1, n2, n3 = (
        jnp.sum(jnp.where(lane == i, totals, 0.0), axis=1, keepdims=True) for i in range(4)
    )
    mu = n1 / m0
    a = m0 / (0.5 * m0 + n1)
    vv = n2 - mu * n1
    vbv = n3 - 2.0 * mu * n2 + mu * mu * n1
    beta = a * a * vv / m0
    step = vv / (0.5 * vv + vbv - a * vv * vv / m0)
    x_r0 = a + step * beta + step * a * mu
    x_b0 = -step * a
    r_r0 = a * mu - step * (0.5 * a * mu + 0.5 * beta)
    r_b0 = -a - step * (a * mu - 0.5 * a + beta)
    r_b1 = step * a
    sends = []
    rows, cols = y0_ref.shape
    step_rows = rows // CHUNKS
    for c in range(CHUNKS):
        at = slice(c * step_rows, (c + 1) * step_rows)
        w = w_ref[at, :cols]
        root = jnp.sqrt(w)
        r0 = s_ref[at, :cols] / w
        y0 = y0_ref[at, :]
        x_ref[at, :] = root * (x_r0 * r0 + x_b0 * y0)
        r_ref[at, :] = root * (r_r0 * r0 + r_b0 * y0 + r_b1 * y1_ref[at, :])
        for i, (src, dst) in enumerate(((x_ref, x_hbm), (r_ref, r_hbm))):
            send = pltpu.make_async_copy(src.at[at], dst.at[at], sem.at[c, i])
            send.start()
            sends.append(send)
    for send in sends:
        send.wait()


VMEM = pl.BlockSpec(memory_space=pltpu.VMEM)
ANY = pl.BlockSpec(memory_space=pl.ANY)
HBM = pl.BlockSpec(memory_space=pltpu.HBM)


def call(kernel, shapes, *args, ins=None, outs=None, scratch=(), name, limit=24, flops=0):
    moved = sum(int(np.prod(x.shape)) * x.dtype.itemsize for x in args)
    return pl.pallas_call(
        kernel,
        out_shape=[jax.ShapeDtypeStruct(s, F32) for s in shapes],
        in_specs=ins or [VMEM] * len(args),
        out_specs=outs or [VMEM] * len(shapes),
        scratch_shapes=list(scratch),
        compiler_params=pltpu.CompilerParams(vmem_limit_bytes=limit << 20),
        cost_estimate=pl.CostEstimate(flops=flops, bytes_accessed=moved, transcendentals=0),
        name=name,
    )(*args)


def neighbours(axes, step):
    count = int(np.prod([lax.axis_size(a) for a in axes]))
    pairs = [(i, i + 1) for i in range(count - 1)]
    return pairs if step > 0 else [(b, a) for a, b in pairs]


def shards(block_sums, block_weights, block_tile, block_row, prior_weight):
    devices = lax.axis_size(TY_TX)
    n_tx = lax.axis_size(TX)
    blocks, _, cols = block_sums.shape
    rows = prior_weight.shape[0]
    parts = cols // LANES
    length = 2 * SLOTS * parts + 2 * SLOTS
    wide = cols + LANES
    slab = (3 * HALF, wide)

    prior_right = lax.ppermute(prior_weight[:, :LANES], TX, neighbours(TX, -1))
    prior_left = lax.ppermute(prior_weight[:, cols - LANES :], TX, neighbours(TX, 1))
    lane = jnp.arange(LANES)[None, :]
    prior_halo = jnp.where(lane < HALF, prior_right, jnp.where(lane >= LANES - HALF, prior_left, 0.0))

    (message,) = call(
        functools.partial(pack_kernel, n_tx, parts, length),
        [(devices * length, LANES)],
        block_tile.reshape(1, blocks),
        block_row.reshape(1, blocks),
        block_sums.reshape(blocks * parts, LANES),
        block_weights.reshape(blocks * parts, LANES),
        ins=[HBM] * 4,
        outs=[HBM],
        scratch=[
            pltpu.VMEM((1, blocks), jnp.int32),
            pltpu.VMEM((1, blocks), jnp.int32),
            pltpu.VMEM((blocks * parts, LANES), F32),
            pltpu.VMEM((blocks * parts, LANES), F32),
            pltpu.VMEM((3, blocks, 2 * cols), BF16),
            pltpu.VMEM((devices * length, LANES), F32),
            pltpu.SemaphoreType.DMA((4,)),
            pltpu.SemaphoreType.DMA((GROUPS,)),
        ],
        name="pack",
        limit=63,
    )
    got = lax.all_to_all(
        message.reshape(devices, 1, length * LANES), TY_TX, split_axis=0, concat_axis=0, tiled=True
    ).reshape(devices * length, LANES)
    s, w, up, down = call(
        functools.partial(select_kernel, parts, length),
        [(rows, wide), (rows, wide), slab, slab],
        got,
        prior_weight,
        prior_halo,
        name="select",
    )
    above = lax.ppermute(down, "ty", neighbours(("ty",), 1))
    below = lax.ppermute(up, "ty", neighbours(("ty",), -1))

    tall = rows + 2 * HALF
    row_taps = taps(np.arange(tall)[:, None] - np.arange(rows + 4 * HALF)[None, :] + HALF)
    col_taps = taps(np.arange(2 * LANES)[None, :] - np.arange(4 * LANES)[:, None] + LANES)
    ring = np.where(np.arange(LANES) < 64, cols, -LANES) + np.arange(LANES)
    near = np.concatenate([np.arange(cols - LANES, cols), ring, np.arange(LANES)])
    edge_taps = taps(ring[None, :] - near[:, None])
    y0, y1, moments = call(
        conv_kernel,
        [(rows, cols), (rows, cols), (devices, LANES)],
        s,
        w,
        above,
        below,
        *row_taps,
        *col_taps,
        *edge_taps,
        scratch=[pltpu.VMEM((tall, wide), F32), pltpu.VMEM((tall, wide), F32)],
        name="smooth",
    )
    moments = lax.all_to_all(
        moments.reshape(devices, 1, LANES), TY_TX, split_axis=0, concat_axis=0, tiled=True
    ).reshape(devices, LANES)
    return tuple(
        call(
            final_kernel,
            [(rows, cols), (rows, cols)],
            moments,
            s,
            w,
            y0,
            y1,
            outs=[HBM, HBM],
            scratch=[
                pltpu.VMEM((rows, cols), F32),
                pltpu.VMEM((rows, cols), F32),
                pltpu.SemaphoreType.DMA((CHUNKS, 2)),
            ],
            name="combine",
        )
    )


def solution(mesh):
    split = Mesh(mesh.devices.reshape(mesh.shape["ty"], 4, 4, 2), ("ty", "tx_0", "tx_1", "tx_2"))
    in_specs = (P(TY_TX, None, None), P(TY_TX, None, None), P(TY_TX, None), P(TY_TX), P("ty", TX))
    out_specs = (P("ty", TX), P("ty", TX))
    return jax.shard_map(
        shards, mesh=split, in_specs=in_specs, out_specs=out_specs, check_vma=False
    )
```

```python
import functools

import jax
import jax.numpy as jnp
import numpy as np
from jax import lax
from jax.experimental import pallas as pl
from jax.experimental.pallas import tpu as pltpu
from jax.sharding import Mesh
from jax.sharding import PartitionSpec as P

HALF = 32
LANES = 128
SLOTS = 2
GROUPS = 2
CHUNKS = 4
TY_TX = ("ty", "tx_0", "tx_1", "tx_2")
TX = ("tx_0", "tx_1", "tx_2")
F32 = jnp.float32
BF16 = jnp.bfloat16


def taps(offset):
    def raw(d):
        scaled = np.abs(d) / (HALF + 1.0)
        return np.where(np.abs(d) <= HALF, (1.0 - scaled) ** 4 * (1.0 + 4.0 * scaled), 0.0)

    values = raw(offset) / raw(np.arange(-HALF, HALF + 1)).sum()
    head = values.astype(BF16)
    tail = (values - head.astype(np.float64)).astype(BF16)
    return jnp.asarray(head), jnp.asarray(tail)


def split2(x):
    head = x.astype(BF16)
    return head, (x - head.astype(F32)).astype(BF16)


def split3(x):
    head = x.astype(BF16)
    rest = x - head.astype(F32)
    mid = rest.astype(BF16)
    return head, mid, (rest - mid.astype(F32)).astype(BF16)


def mm(a, b):
    return jnp.dot(a, b, preferred_element_type=F32)


def pick(select, x):
    head, mid, tail = split3(x)
    return mm(select, tail) + mm(select, mid) + mm(select, head)


def smooth3(left, right):
    (lh, ll), (rh, rl) = left, right
    return mm(ll, rh) + mm(lh, rl) + mm(lh, rh)


def iota(shape, dim):
    return lax.broadcasted_iota(jnp.int32, shape, dim)


def pack_kernel(
    n_tx, parts, length, tile_hbm, row_hbm, sums_hbm, weights_hbm, out_hbm,
    tile_ref, row_ref, sums_ref, weights_ref, split_ref, out_ref, in_sem, out_sem
):
    fetches = [
        pltpu.make_async_copy(src, dst, in_sem.at[i])
        for i, (src, dst) in enumerate(
            (
                (tile_hbm, tile_ref),
                (row_hbm, row_ref),
                (sums_hbm, sums_ref),
                (weights_hbm, weights_ref),
            )
        )
    ]
    for fetch in fetches:
        fetch.start()
    fetches[0].wait()
    fetches[1].wait()
    count = tile_ref.shape[1]
    devices = out_ref.shape[0] // length
    group = devices // GROUPS
    tile = tile_ref[...]
    t = iota((devices, count), 0)
    same = tile == t
    earlier = iota((count, count), 0) < iota((count, count), 1)
    before = mm(same.astype(F32).astype(BF16), earlier.astype(F32).astype(BF16))
    rank = jnp.sum(jnp.where(same, before, 0.0), axis=0, keepdims=True)
    column = lax.rem(t, n_tx)
    from_left = (tile + 1 == t) & (column != 0)
    from_right = (tile - 1 == t) & (column != n_tx - 1)

    def onehot(mask, k):
        return jnp.where(mask & (rank == float(k)), 1.0, 0.0)

    own = [onehot(same, k) for k in range(SLOTS)]
    left = [onehot(from_left, k) for k in range(SLOTS)]
    right = [
        jnp.concatenate([onehot(from_right, k), own[k]], axis=1) for k in range(SLOTS)
    ]

    def of_group(masks, g):
        part = slice(g * group, (g + 1) * group)
        return jnp.concatenate([m[part] for m in masks], axis=0).astype(BF16)

    lane = iota((count, LANES), 1)
    number = jnp.transpose(jnp.broadcast_to(row_ref[...].astype(F32) + 1.0, (count, count)))
    for which, ref in enumerate((sums_ref, weights_ref)):
        fetches[2 + which].wait()
        for c in range(parts):
            at = slice((which * parts + c) * LANES, (which * parts + c + 1) * LANES)
            for i, piece in enumerate(split3(ref[pl.ds(c, count, stride=parts), :])):
                split_ref[i, :, at] = piece

    last = parts - 1
    s_last = sums_ref[pl.ds(last, count, stride=parts), :]
    w_last = pltpu.roll(weights_ref[pl.ds(last, count, stride=parts), :], 64, 1)
    s_first = sums_ref[pl.ds(0, count, stride=parts), :]
    w_first = pltpu.roll(weights_ref[pl.ds(0, count, stride=parts), :], 64, 1)
    left_rows = jnp.where(
        lane >= 64, s_last, jnp.where(lane >= 32, w_last, jnp.where(lane == 0, number, 0.0))
    )
    right_rows = jnp.where(
        lane < 64, s_first, jnp.where(lane < 96, w_first, jnp.where(lane == 96, number, 0.0))
    )
    own_rows = jnp.where(lane == 97, number, 0.0)
    both_rows = jnp.concatenate([right_rows, own_rows], axis=0)

    base = 2 * SLOTS * parts
    sends = []
    for g in range(GROUPS):
        first = g * group * length
        own_all = of_group(own, g)
        for c in range(0, 2 * parts, 2):
            at = slice(c * LANES, (c + 2) * LANES)
            y = (
                mm(own_all, split_ref[2, :, at])
                + mm(own_all, split_ref[1, :, at])
                + mm(own_all, split_ref[0, :, at])
            )
            which, chunk = divmod(c, parts)
            for k in range(SLOTS):
                for i in range(2):
                    to = first + (which * SLOTS + k) * parts + chunk + i
                    out_ref[pl.ds(to, group, stride=length), :] = y[
                        k * group : (k + 1) * group, i * LANES : (i + 1) * LANES
                    ]
        to_left = pick(of_group(left, g), left_rows)
        to_right = pick(of_group(right, g), both_rows)
        for k in range(SLOTS):
            part = slice(k * group, (k + 1) * group)
            out_ref[pl.ds(first + base + k, group, stride=length), :] = to_left[part]
            out_ref[pl.ds(first + base + SLOTS + k, group, stride=length), :] = to_right[part]
        span = pl.ds(first, group * length)
        send = pltpu.make_async_copy(out_ref.at[span], out_hbm.at[span], out_sem.at[g])
        send.start()
        sends.append(send)
    for send in sends:
        send.wait()


def select_kernel(
    parts, length, got_ref, prior_ref, prior_halo_ref, s_ref, w_ref, up_ref, down_ref
):
    rows, cols = prior_ref.shape
    devices = got_ref.shape[0] // length
    base = 2 * SLOTS * parts
    from_left = [got_ref[pl.ds(base + k, devices, stride=length), :] for k in range(SLOTS)]
    from_right = [got_ref[pl.ds(base + SLOTS + k, devices, stride=length), :] for k in range(SLOTS)]
    left_t = [jnp.transpose(x) for x in from_left]
    right_t = [jnp.transpose(x) for x in from_right]
    wanted = (iota((rows, devices), 0) + 1).astype(F32)

    def chooser(lists, at):
        return jnp.concatenate(
            [jnp.where(x[at : at + 1, :] == wanted, 1.0, 0.0) for x in lists], axis=1
        ).astype(BF16)

    own = chooser(right_t, 97)
    for which, dst in enumerate((s_ref, w_ref)):
        for c in range(0, parts, 2):
            x = jnp.concatenate(
                [
                    jnp.concatenate(
                        [
                            got_ref[
                                pl.ds((which * SLOTS + k) * parts + c + i, devices, stride=length), :
                            ]
                            for i in range(2)
                        ],
                        axis=1,
                    )
                    for k in range(SLOTS)
                ],
                axis=0,
            )
            y = pick(own, x)
            at = slice(c * LANES, (c + 2) * LANES)
            if which == 1:
                y = y + prior_ref[:, at]
            dst[:, at] = y
    left = pick(chooser(left_t, 0), jnp.concatenate(from_left, axis=0))
    right = pick(chooser(right_t, 96), jnp.concatenate(from_right, axis=0))
    lane = iota((rows, LANES), 1)
    s_ref[:, cols:] = jnp.where(lane < 64, right, left)
    column = lax.axis_index(TX)
    has_left = jnp.where(column > 0, 1.0, 0.0)
    has_right = jnp.where(column < lax.axis_size(TX) - 1, 1.0, 0.0)
    prior_halo = prior_halo_ref[...]
    w_ref[:, cols:] = jnp.where(
        lane < 32,
        prior_halo * has_right + pltpu.roll(right, 64, 1),
        jnp.where(lane >= 96, prior_halo * has_left + pltpu.roll(left, 64, 1), 0.0),
    )
    up_ref[: 2 * HALF, :] = s_ref[: 2 * HALF, :]
    up_ref[2 * HALF :, :] = w_ref[:HALF, :]
    down_ref[: 2 * HALF, :] = s_ref[rows - 2 * HALF :, :]
    down_ref[2 * HALF :, :] = w_ref[rows - HALF :, :]


def conv_kernel(
    n_ty,
    s_ref,
    w_ref,
    above_ref,
    below_ref,
    row_h_ref,
    row_l_ref,
    col_h_ref,
    col_l_ref,
    edge_h_ref,
    edge_l_ref,
    y0_ref,
    y1_ref,
    moments_ref,
    mid_ref,
    z_ref,
):
    rows, wide = s_ref.shape
    cols = wide - LANES
    tall = rows + 2 * HALF
    col = (col_h_ref[...], col_l_ref[...])
    edge = (edge_h_ref[...], edge_l_ref[...])
    row_at = lax.axis_index("ty")
    has_above = jnp.where(row_at > 0, 1.0, 0.0)
    has_below = jnp.where(row_at < n_ty - 1, 1.0, 0.0)

    def with_halo(part, at, ref):
        above = above_ref[part, at] * has_above
        below = below_ref[part, at] * has_below
        return jnp.concatenate([above, ref[:, at], below], axis=0)

    sums, weights = slice(0, 2 * HALF), slice(2 * HALF, 3 * HALF)

    def block(ref, c, height):
        lo, hi = (c - 1) * LANES, (c + 3) * LANES
        if c == 0:
            x = jnp.concatenate([ref[:height, cols:], ref[:height, :hi]], axis=1)
        else:
            x = ref[:height, lo:hi]
        return smooth3(split2(x), col)

    row = (row_h_ref[...], row_l_ref[...])
    for c in range(0, wide, LANES * 3):
        at = slice(c, c + LANES * 3)
        mid_ref[:, at] = smooth3(row, split2(with_halo(sums, at, s_ref)))
    total_sy = jnp.zeros((rows, 2 * LANES), F32)
    total_zy = jnp.zeros((rows, 2 * LANES), F32)
    total_ss = jnp.zeros((rows, 2 * LANES), F32)
    for c in range(0, cols // LANES, 2):
        at = slice(c * LANES, (c + 2) * LANES)
        y = block(mid_ref, c, tall)
        z = with_halo(weights, at, w_ref) * y
        z_ref[:, at] = z
        inner = y[HALF : HALF + rows]
        y0_ref[:, at] = inner
        s = s_ref[:, at]
        total_sy += s * inner
        total_zy += z[HALF : HALF + rows] * inner
        total_ss += s * s / w_ref[:, at]
    x = jnp.concatenate([mid_ref[:, cols - LANES :], mid_ref[:, :LANES]], axis=1)
    y = smooth3(split2(x), edge)
    z_ref[:, cols:] = with_halo(weights, slice(cols, wide), w_ref) * y

    row = (row_h_ref[:rows, :tall], row_l_ref[:rows, :tall])
    for c in range(0, wide, LANES * 3):
        at = slice(c, c + LANES * 3)
        mid_ref[:rows, at] = smooth3(row, split2(z_ref[:, at]))
    total_zz = jnp.zeros((rows, 2 * LANES), F32)
    for c in range(0, cols // LANES, 2):
        at = slice(c * LANES, (c + 2) * LANES)
        y = block(mid_ref, c, rows)
        y1_ref[:, at] = y
        total_zz += z_ref[HALF : HALF + rows, at] * y
    lane = iota((1, LANES), 1)
    packed = jnp.zeros((1, LANES), F32)
    for i, total in enumerate((total_ss, total_sy, total_zy, total_zz)):
        value = jnp.sum(jnp.sum(total, axis=0, keepdims=True), axis=1, keepdims=True)
        packed = jnp.where(lane == i, value, packed)
    moments_ref[...] = jnp.broadcast_to(packed, moments_ref.shape)


def final_kernel(
    moments_ref, s_ref, w_ref, y0_ref, y1_ref, x_hbm, r_hbm, x_ref, r_ref, sem
):
    totals = jnp.sum(moments_ref[...], axis=0, keepdims=True)
    lane = iota(totals.shape, 1)
    m0, n1, n2, n3 = (
        jnp.sum(jnp.where(lane == i, totals, 0.0), axis=1, keepdims=True) for i in range(4)
    )
    mu = n1 / m0
    a = m0 / (0.5 * m0 + n1)
    vv = n2 - mu * n1
    vbv = n3 - 2.0 * mu * n2 + mu * mu * n1
    beta = a * a * vv / m0
    step = vv / (0.5 * vv + vbv - a * vv * vv / m0)
    x_r0 = a + step * beta + step * a * mu
    x_b0 = -step * a
    r_r0 = a * mu - step * (0.5 * a * mu + 0.5 * beta)
    r_b0 = -a - step * (a * mu - 0.5 * a + beta)
    r_b1 = step * a
    sends = []
    rows, cols = y0_ref.shape
    step_rows = rows // CHUNKS
    for c in range(CHUNKS):
        at = slice(c * step_rows, (c + 1) * step_rows)
        w = w_ref[at, :cols]
        root = jnp.sqrt(w)
        r0 = s_ref[at, :cols] / w
        y0 = y0_ref[at, :]
        x_ref[at, :] = root * (x_r0 * r0 + x_b0 * y0)
        r_ref[at, :] = root * (r_r0 * r0 + r_b0 * y0 + r_b1 * y1_ref[at, :])
        for i, (src, dst) in enumerate(((x_ref, x_hbm), (r_ref, r_hbm))):
            send = pltpu.make_async_copy(src.at[at], dst.at[at], sem.at[c, i])
            send.start()
            sends.append(send)
    for send in sends:
        send.wait()


VMEM = pl.BlockSpec(memory_space=pltpu.VMEM)
ANY = pl.BlockSpec(memory_space=pl.ANY)
HBM = pl.BlockSpec(memory_space=pltpu.HBM)


def call(kernel, shapes, *args, ins=None, outs=None, scratch=(), name, limit=24, flops=0):
    moved = sum(int(np.prod(x.shape)) * x.dtype.itemsize for x in args)
    return pl.pallas_call(
        kernel,
        out_shape=[jax.ShapeDtypeStruct(s, F32) for s in shapes],
        in_specs=ins or [VMEM] * len(args),
        out_specs=outs or [VMEM] * len(shapes),
        scratch_shapes=list(scratch),
        compiler_params=pltpu.CompilerParams(vmem_limit_bytes=limit << 20),
        cost_estimate=pl.CostEstimate(flops=flops, bytes_accessed=moved, transcendentals=0),
        name=name,
    )(*args)


def neighbours(axes, step):
    count = int(np.prod([lax.axis_size(a) for a in axes]))
    return [(i, (i + step) % count) for i in range(count)]


def shards(block_sums, block_weights, block_tile, block_row, prior_weight):
    devices = lax.axis_size(TY_TX)
    n_tx = lax.axis_size(TX)
    blocks, _, cols = block_sums.shape
    rows = prior_weight.shape[0]
    parts = cols // LANES
    length = 2 * SLOTS * parts + 2 * SLOTS
    wide = cols + LANES
    slab = (3 * HALF, wide)

    prior_right = lax.ppermute(prior_weight[:, :LANES], TX, neighbours(TX, -1))
    prior_left = lax.ppermute(prior_weight[:, cols - LANES :], TX, neighbours(TX, 1))
    lane = jnp.arange(LANES)[None, :]
    prior_halo = jnp.where(lane < HALF, prior_right, jnp.where(lane >= LANES - HALF, prior_left, 0.0))

    (message,) = call(
        functools.partial(pack_kernel, n_tx, parts, length),
        [(devices * length, LANES)],
        block_tile.reshape(1, blocks),
        block_row.reshape(1, blocks),
        block_sums.reshape(blocks * parts, LANES),
        block_weights.reshape(blocks * parts, LANES),
        ins=[HBM] * 4,
        outs=[HBM],
        scratch=[
            pltpu.VMEM((1, blocks), jnp.int32),
            pltpu.VMEM((1, blocks), jnp.int32),
            pltpu.VMEM((blocks * parts, LANES), F32),
            pltpu.VMEM((blocks * parts, LANES), F32),
            pltpu.VMEM((3, blocks, 2 * cols), BF16),
            pltpu.VMEM((devices * length, LANES), F32),
            pltpu.SemaphoreType.DMA((4,)),
            pltpu.SemaphoreType.DMA((GROUPS,)),
        ],
        name="pack",
        limit=63,
    )
    got = lax.all_to_all(
        message.reshape(devices, 1, length * LANES), TY_TX, split_axis=0, concat_axis=0, tiled=True
    ).reshape(devices * length, LANES)
    s, w, up, down = call(
        functools.partial(select_kernel, parts, length),
        [(rows, wide), (rows, wide), slab, slab],
        got,
        prior_weight,
        prior_halo,
        name="select",
    )
    above = lax.ppermute(down, "ty", neighbours(("ty",), 1))
    below = lax.ppermute(up, "ty", neighbours(("ty",), -1))

    tall = rows + 2 * HALF
    row_taps = taps(np.arange(tall)[:, None] - np.arange(rows + 4 * HALF)[None, :] + HALF)
    col_taps = taps(np.arange(2 * LANES)[None, :] - np.arange(4 * LANES)[:, None] + LANES)
    ring = np.where(np.arange(LANES) < 64, cols, -LANES) + np.arange(LANES)
    near = np.concatenate([np.arange(cols - LANES, cols), ring, np.arange(LANES)])
    edge_taps = taps(ring[None, :] - near[:, None])
    y0, y1, moments = call(
        functools.partial(conv_kernel, lax.axis_size("ty")),
        [(rows, cols), (rows, cols), (devices, LANES)],
        s,
        w,
        above,
        below,
        *row_taps,
        *col_taps,
        *edge_taps,
        scratch=[pltpu.VMEM((tall, wide), F32), pltpu.VMEM((tall, wide), F32)],
        name="smooth",
    )
    moments = lax.all_to_all(
        moments.reshape(devices, 1, LANES), TY_TX, split_axis=0, concat_axis=0, tiled=True
    ).reshape(devices, LANES)
    return tuple(
        call(
            final_kernel,
            [(rows, cols), (rows, cols)],
            moments,
            s,
            w,
            y0,
            y1,
            outs=[HBM, HBM],
            scratch=[
                pltpu.VMEM((rows, cols), F32),
                pltpu.VMEM((rows, cols), F32),
                pltpu.SemaphoreType.DMA((CHUNKS, 2)),
            ],
            name="combine",
        )
    )


def solution(mesh):
    split = Mesh(mesh.devices.reshape(mesh.shape["ty"], 4, 4, 2), ("ty", "tx_0", "tx_1", "tx_2"))
    in_specs = (P(TY_TX, None, None), P(TY_TX, None, None), P(TY_TX, None), P(TY_TX), P("ty", TX))
    out_specs = (P("ty", TX), P("ty", TX))
    return jax.shard_map(
        shards, mesh=split, in_specs=in_specs, out_specs=out_specs, check_vma=False
    )
```

```python
import functools

import jax
import jax.numpy as jnp
import numpy as np
from jax import lax
from jax.experimental import pallas as pl
from jax.experimental.pallas import tpu as pltpu
from jax.sharding import Mesh
from jax.sharding import PartitionSpec as P

HALF = 32
LANES = 128
SLOTS = 2
GROUPS = 2
CHUNKS = 4
TY_TX = ("ty", "tx_0", "tx_1", "tx_2")
TX = ("tx_0", "tx_1", "tx_2")
F32 = jnp.float32
BF16 = jnp.bfloat16


def taps(offset):
    def raw(d):
        scaled = np.abs(d) / (HALF + 1.0)
        return np.where(np.abs(d) <= HALF, (1.0 - scaled) ** 4 * (1.0 + 4.0 * scaled), 0.0)

    values = raw(offset) / raw(np.arange(-HALF, HALF + 1)).sum()
    head = values.astype(BF16)
    tail = (values - head.astype(np.float64)).astype(BF16)
    return jnp.asarray(head), jnp.asarray(tail)


def split2(x):
    head = x.astype(BF16)
    return head, (x - head.astype(F32)).astype(BF16)


def split3(x):
    head = x.astype(BF16)
    rest = x - head.astype(F32)
    mid = rest.astype(BF16)
    return head, mid, (rest - mid.astype(F32)).astype(BF16)


def mm(a, b):
    return jnp.dot(a, b, preferred_element_type=F32)


def pick(select, x):
    head, mid, tail = split3(x)
    return mm(select, tail) + mm(select, mid) + mm(select, head)


def smooth3(left, right):
    (lh, ll), (rh, rl) = left, right
    return mm(ll, rh) + mm(lh, rl) + mm(lh, rh)


def iota(shape, dim):
    return lax.broadcasted_iota(jnp.int32, shape, dim)


def pack_kernel(
    n_tx, parts, length, tile_hbm, row_hbm, sums_hbm, weights_hbm, out_hbm,
    tile_ref, row_ref, sums_ref, weights_ref, split_ref, out_ref, in_sem, out_sem
):
    fetches = [
        pltpu.make_async_copy(src, dst, in_sem.at[i])
        for i, (src, dst) in enumerate(
            (
                (tile_hbm, tile_ref),
                (row_hbm, row_ref),
                (sums_hbm, sums_ref),
                (weights_hbm, weights_ref),
            )
        )
    ]
    for fetch in fetches:
        fetch.start()
    fetches[0].wait()
    fetches[1].wait()
    count = tile_ref.shape[1]
    devices = out_ref.shape[0] // length
    group = devices // GROUPS
    tile = tile_ref[...]
    t = iota((devices, count), 0)
    same = tile == t
    earlier = iota((count, count), 0) < iota((count, count), 1)
    before = mm(same.astype(F32).astype(BF16), earlier.astype(F32).astype(BF16))
    rank = jnp.sum(jnp.where(same, before, 0.0), axis=0, keepdims=True)
    column = lax.rem(t, n_tx)
    from_left = (tile + 1 == t) & (column != 0)
    from_right = (tile - 1 == t) & (column != n_tx - 1)

    def onehot(mask, k):
        return jnp.where(mask & (rank == float(k)), 1.0, 0.0)

    own = [onehot(same, k) for k in range(SLOTS)]
    left = [onehot(from_left, k) for k in range(SLOTS)]
    right = [
        jnp.concatenate([onehot(from_right, k), own[k]], axis=1) for k in range(SLOTS)
    ]

    def of_group(masks, g):
        part = slice(g * group, (g + 1) * group)
        return jnp.concatenate([m[part] for m in masks], axis=0).astype(BF16)

    lane = iota((count, LANES), 1)
    number = jnp.transpose(jnp.broadcast_to(row_ref[...].astype(F32) + 1.0, (count, count)))
    for which, ref in enumerate((sums_ref, weights_ref)):
        fetches[2 + which].wait()
        for c in range(parts):
            at = slice((which * parts + c) * LANES, (which * parts + c + 1) * LANES)
            for i, piece in enumerate(split3(ref[pl.ds(c, count, stride=parts), :])):
                split_ref[i, :, at] = piece

    last = parts - 1
    s_last = sums_ref[pl.ds(last, count, stride=parts), :]
    w_last = pltpu.roll(weights_ref[pl.ds(last, count, stride=parts), :], 64, 1)
    s_first = sums_ref[pl.ds(0, count, stride=parts), :]
    w_first = pltpu.roll(weights_ref[pl.ds(0, count, stride=parts), :], 64, 1)
    left_rows = jnp.where(
        lane >= 64, s_last, jnp.where(lane >= 32, w_last, jnp.where(lane == 0, number, 0.0))
    )
    right_rows = jnp.where(
        lane < 64, s_first, jnp.where(lane < 96, w_first, jnp.where(lane == 96, number, 0.0))
    )
    own_rows = jnp.where(lane == 97, number, 0.0)
    both_rows = jnp.concatenate([right_rows, own_rows], axis=0)

    base = 2 * SLOTS * parts
    sends = []
    for g in range(GROUPS):
        first = g * group * length
        own_all = of_group(own, g)
        for c in range(0, 2 * parts, 2):
            at = slice(c * LANES, (c + 2) * LANES)
            y = (
                mm(own_all, split_ref[2, :, at])
                + mm(own_all, split_ref[1, :, at])
                + mm(own_all, split_ref[0, :, at])
            )
            which, chunk = divmod(c, parts)
            for k in range(SLOTS):
                for i in range(2):
                    to = first + (which * SLOTS + k) * parts + chunk + i
                    out_ref[pl.ds(to, group, stride=length), :] = y[
                        k * group : (k + 1) * group, i * LANES : (i + 1) * LANES
                    ]
        to_left = pick(of_group(left, g), left_rows)
        to_right = pick(of_group(right, g), both_rows)
        for k in range(SLOTS):
            part = slice(k * group, (k + 1) * group)
            out_ref[pl.ds(first + base + k, group, stride=length), :] = to_left[part]
            out_ref[pl.ds(first + base + SLOTS + k, group, stride=length), :] = to_right[part]
        span = pl.ds(first, group * length)
        send = pltpu.make_async_copy(out_ref.at[span], out_hbm.at[span], out_sem.at[g])
        send.start()
        sends.append(send)
    for send in sends:
        send.wait()


def select_kernel(
    parts, length, got_ref, prior_ref, prior_halo_ref, s_ref, w_ref, s_up_ref, s_down_ref,
    w_up_ref, w_down_ref
):
    rows, cols = prior_ref.shape
    devices = got_ref.shape[0] // length
    base = 2 * SLOTS * parts
    from_left = [got_ref[pl.ds(base + k, devices, stride=length), :] for k in range(SLOTS)]
    from_right = [got_ref[pl.ds(base + SLOTS + k, devices, stride=length), :] for k in range(SLOTS)]
    left_t = [jnp.transpose(x) for x in from_left]
    right_t = [jnp.transpose(x) for x in from_right]
    wanted = (iota((rows, devices), 0) + 1).astype(F32)

    def chooser(lists, at):
        return jnp.concatenate(
            [jnp.where(x[at : at + 1, :] == wanted, 1.0, 0.0) for x in lists], axis=1
        ).astype(BF16)

    own = chooser(right_t, 97)
    for which, dst in enumerate((s_ref, w_ref)):
        for c in range(0, parts, 2):
            x = jnp.concatenate(
                [
                    jnp.concatenate(
                        [
                            got_ref[
                                pl.ds((which * SLOTS + k) * parts + c + i, devices, stride=length), :
                            ]
                            for i in range(2)
                        ],
                        axis=1,
                    )
                    for k in range(SLOTS)
                ],
                axis=0,
            )
            y = pick(own, x)
            at = slice(c * LANES, (c + 2) * LANES)
            if which == 1:
                y = y + prior_ref[:, at]
            dst[:, at] = y
    left = pick(chooser(left_t, 0), jnp.concatenate(from_left, axis=0))
    right = pick(chooser(right_t, 96), jnp.concatenate(from_right, axis=0))
    lane = iota((rows, LANES), 1)
    s_ref[:, cols:] = jnp.where(lane < 64, right, left)
    column = lax.axis_index(TX)
    has_left = jnp.where(column > 0, 1.0, 0.0)
    has_right = jnp.where(column < lax.axis_size(TX) - 1, 1.0, 0.0)
    prior_halo = prior_halo_ref[...]
    w_ref[:, cols:] = jnp.where(
        lane < 32,
        prior_halo * has_right + pltpu.roll(right, 64, 1),
        jnp.where(lane >= 96, prior_halo * has_left + pltpu.roll(left, 64, 1), 0.0),
    )
    s_up_ref[...] = s_ref[: 2 * HALF, :]
    s_down_ref[...] = s_ref[rows - 2 * HALF :, :]
    w_up_ref[...] = w_ref[:HALF, :]
    w_down_ref[...] = w_ref[rows - HALF :, :]


def with_halo(n_ty, above_ref, ref, below_ref, at):
    row_at = lax.axis_index("ty")
    above = above_ref[:, at] * jnp.where(row_at > 0, 1.0, 0.0)
    below = below_ref[:, at] * jnp.where(row_at < n_ty - 1, 1.0, 0.0)
    return jnp.concatenate([above, ref[:, at], below], axis=0)


def along_columns(mid_ref, c, height, col):
    cols = mid_ref.shape[1] - LANES
    lo, hi = (c - 1) * LANES, (c + 3) * LANES
    if c == 0:
        x = jnp.concatenate([mid_ref[:height, cols:], mid_ref[:height, :hi]], axis=1)
    else:
        x = mid_ref[:height, lo:hi]
    return smooth3(split2(x), col)


def first_kernel(
    n_ty,
    s_ref,
    w_ref,
    above_ref,
    below_ref,
    row_h_ref,
    row_l_ref,
    col_h_ref,
    col_l_ref,
    edge_h_ref,
    edge_l_ref,
    y0_ref,
    root_ref,
    r0_ref,
    m0_ref,
    mid_ref,
):
    rows, wide = s_ref.shape
    cols = wide - LANES
    tall = rows + 2 * HALF
    row = (row_h_ref[...], row_l_ref[...])
    col = (col_h_ref[...], col_l_ref[...])
    for c in range(0, wide, LANES * 3):
        at = slice(c, c + LANES * 3)
        mid_ref[:, at] = smooth3(row, split2(with_halo(n_ty, above_ref, s_ref, below_ref, at)))
    for c in range(0, cols // LANES, 2):
        at = slice(c * LANES, (c + 2) * LANES)
        y0_ref[:, at] = along_columns(mid_ref, c, tall, col)
    x = jnp.concatenate([mid_ref[:, cols - LANES :], mid_ref[:, :LANES]], axis=1)
    y0_ref[:, cols:] = smooth3(split2(x), (edge_h_ref[...], edge_l_ref[...]))
    total = jnp.zeros((8, cols), F32)
    for r in range(0, rows, 8):
        at = slice(r, r + 8)
        root = jnp.sqrt(w_ref[at, :cols])
        r0 = s_ref[at, :cols] / root
        root_ref[at, :] = root
        r0_ref[at, :] = r0
        total += r0 * r0
    m0_ref[...] = sum(total[:, c : c + LANES] for c in range(0, cols, LANES))


def second_kernel(
    n_ty,
    s_ref,
    w_ref,
    above_ref,
    below_ref,
    y0_ref,
    root_ref,
    m0_ref,
    row_h_ref,
    row_l_ref,
    col_h_ref,
    col_l_ref,
    b0_ref,
    b1_ref,
    moments_ref,
    mid_ref,
    z_ref,
):
    rows, wide = s_ref.shape
    cols = wide - LANES
    tall = rows + 2 * HALF
    row = (row_h_ref[:rows, :tall], row_l_ref[:rows, :tall])
    col = (col_h_ref[...], col_l_ref[...])
    for c in range(0, wide, LANES * 3):
        at = slice(c, c + LANES * 3)
        z = with_halo(n_ty, above_ref, w_ref, below_ref, at) * y0_ref[:, at]
        z_ref[:, at] = z[HALF : HALF + rows]
        mid_ref[:, at] = smooth3(row, split2(z))
    total_sy = jnp.zeros((rows, 2 * LANES), F32)
    total_zy = jnp.zeros((rows, 2 * LANES), F32)
    total_zz = jnp.zeros((rows, 2 * LANES), F32)
    for c in range(0, cols // LANES, 2):
        at = slice(c * LANES, (c + 2) * LANES)
        y1 = along_columns(mid_ref, c, rows, col)
        y0 = y0_ref[HALF : HALF + rows, at]
        z = z_ref[:, at]
        root = root_ref[:, at]
        b0_ref[:, at] = root * y0
        b1_ref[:, at] = root * y1
        total_sy += s_ref[:, at] * y0
        total_zy += z * y0
        total_zz += z * y1
    lane = iota((1, LANES), 1)
    packed = jnp.zeros((1, LANES), F32)
    for i, total in enumerate((m0_ref[...], total_sy, total_zy, total_zz)):
        value = jnp.sum(jnp.sum(total, axis=0, keepdims=True), axis=1, keepdims=True)
        packed = jnp.where(lane == i, value, packed)
    moments_ref[...] = jnp.broadcast_to(packed, moments_ref.shape)


def final_kernel(moments_ref, r0_ref, b0_ref, b1_ref, x_hbm, r_hbm, x_ref, r_ref, sem):
    totals = jnp.sum(moments_ref[...], axis=0, keepdims=True)
    lane = iota(totals.shape, 1)
    m0, n1, n2, n3 = (
        jnp.sum(jnp.where(lane == i, totals, 0.0), axis=1, keepdims=True) for i in range(4)
    )
    mu = n1 / m0
    a = m0 / (0.5 * m0 + n1)
    vv = n2 - mu * n1
    vbv = n3 - 2.0 * mu * n2 + mu * mu * n1
    beta = a * a * vv / m0
    step = vv / (0.5 * vv + vbv - a * vv * vv / m0)
    x_r0 = a + step * beta + step * a * mu
    x_b0 = -step * a
    r_r0 = a * mu - step * (0.5 * a * mu + 0.5 * beta)
    r_b0 = -a - step * (a * mu - 0.5 * a + beta)
    r_b1 = step * a
    sends = []
    step_rows = r0_ref.shape[0] // CHUNKS
    for c in range(CHUNKS):
        at = slice(c * step_rows, (c + 1) * step_rows)
        r0 = r0_ref[at, :]
        b0 = b0_ref[at, :]
        x_ref[at, :] = x_r0 * r0 + x_b0 * b0
        r_ref[at, :] = r_r0 * r0 + r_b0 * b0 + r_b1 * b1_ref[at, :]
        for i, (src, dst) in enumerate(((x_ref, x_hbm), (r_ref, r_hbm))):
            send = pltpu.make_async_copy(src.at[at], dst.at[at], sem.at[c, i])
            send.start()
            sends.append(send)
    for send in sends:
        send.wait()


VMEM = pl.BlockSpec(memory_space=pltpu.VMEM)
ANY = pl.BlockSpec(memory_space=pl.ANY)
HBM = pl.BlockSpec(memory_space=pltpu.HBM)


def call(kernel, shapes, *args, ins=None, outs=None, scratch=(), name, limit=24, flops=0):
    moved = sum(int(np.prod(x.shape)) * x.dtype.itemsize for x in args)
    return pl.pallas_call(
        kernel,
        out_shape=[jax.ShapeDtypeStruct(s, F32) for s in shapes],
        in_specs=ins or [VMEM] * len(args),
        out_specs=outs or [VMEM] * len(shapes),
        scratch_shapes=list(scratch),
        compiler_params=pltpu.CompilerParams(vmem_limit_bytes=limit << 20),
        cost_estimate=pl.CostEstimate(flops=flops, bytes_accessed=moved, transcendentals=0),
        name=name,
    )(*args)


def neighbours(axes, step):
    count = int(np.prod([lax.axis_size(a) for a in axes]))
    return [(i, (i + step) % count) for i in range(count)]


def shards(block_sums, block_weights, block_tile, block_row, prior_weight):
    devices = lax.axis_size(TY_TX)
    n_tx = lax.axis_size(TX)
    blocks, _, cols = block_sums.shape
    rows = prior_weight.shape[0]
    parts = cols // LANES
    length = 2 * SLOTS * parts + 2 * SLOTS
    wide = cols + LANES

    prior_right = lax.ppermute(prior_weight[:, :LANES], TX, neighbours(TX, -1))
    prior_left = lax.ppermute(prior_weight[:, cols - LANES :], TX, neighbours(TX, 1))
    lane = jnp.arange(LANES)[None, :]
    prior_halo = jnp.where(lane < HALF, prior_right, jnp.where(lane >= LANES - HALF, prior_left, 0.0))

    (message,) = call(
        functools.partial(pack_kernel, n_tx, parts, length),
        [(devices * length, LANES)],
        block_tile.reshape(1, blocks),
        block_row.reshape(1, blocks),
        block_sums.reshape(blocks * parts, LANES),
        block_weights.reshape(blocks * parts, LANES),
        ins=[HBM] * 4,
        outs=[HBM],
        scratch=[
            pltpu.VMEM((1, blocks), jnp.int32),
            pltpu.VMEM((1, blocks), jnp.int32),
            pltpu.VMEM((blocks * parts, LANES), F32),
            pltpu.VMEM((blocks * parts, LANES), F32),
            pltpu.VMEM((3, blocks, 2 * cols), BF16),
            pltpu.VMEM((devices * length, LANES), F32),
            pltpu.SemaphoreType.DMA((4,)),
            pltpu.SemaphoreType.DMA((GROUPS,)),
        ],
        name="pack",
        limit=63,
    )
    got = lax.all_to_all(
        message.reshape(devices, 1, length * LANES), TY_TX, split_axis=0, concat_axis=0, tiled=True
    ).reshape(devices * length, LANES)
    s_slab, w_slab = (2 * HALF, wide), (HALF, wide)
    s, w, s_up, s_down, w_up, w_down = call(
        functools.partial(select_kernel, parts, length),
        [(rows, wide), (rows, wide), s_slab, s_slab, w_slab, w_slab],
        got,
        prior_weight,
        prior_halo,
        name="select",
    )
    n_ty = lax.axis_size("ty")
    downward, upward = neighbours(("ty",), 1), neighbours(("ty",), -1)
    s_above, s_below = lax.ppermute(s_down, "ty", downward), lax.ppermute(s_up, "ty", upward)
    w_above, w_below = lax.ppermute(w_down, "ty", downward), lax.ppermute(w_up, "ty", upward)

    tall = rows + 2 * HALF
    row_taps = taps(np.arange(tall)[:, None] - np.arange(rows + 4 * HALF)[None, :] + HALF)
    col_taps = taps(np.arange(2 * LANES)[None, :] - np.arange(4 * LANES)[:, None] + LANES)
    ring = np.where(np.arange(LANES) < 64, cols, -LANES) + np.arange(LANES)
    near = np.concatenate([np.arange(cols - LANES, cols), ring, np.arange(LANES)])
    edge_taps = taps(ring[None, :] - near[:, None])
    tile = (rows, cols)
    y0, root, r0, m0 = call(
        functools.partial(first_kernel, n_ty),
        [(tall, wide), tile, tile, (8, LANES)],
        s,
        w,
        s_above,
        s_below,
        *row_taps,
        *col_taps,
        *edge_taps,
        scratch=[pltpu.VMEM((tall, wide), F32)],
        flops=3 * 2 * tall * wide * (2 * LANES + 4 * LANES),
        name="first",
    )
    b0, b1, moments = call(
        functools.partial(second_kernel, n_ty),
        [tile, tile, (devices, LANES)],
        s,
        w,
        w_above,
        w_below,
        y0,
        root,
        m0,
        *row_taps,
        *col_taps,
        scratch=[pltpu.VMEM((rows, wide), F32), pltpu.VMEM((rows, wide), F32)],
        flops=3 * 2 * rows * wide * (2 * LANES + 4 * LANES),
        name="second",
    )
    moments = lax.all_to_all(
        moments.reshape(devices, 1, LANES), TY_TX, split_axis=0, concat_axis=0, tiled=True
    ).reshape(devices, LANES)
    return tuple(
        call(
            final_kernel,
            [tile, tile],
            moments,
            r0,
            b0,
            b1,
            outs=[HBM, HBM],
            scratch=[
                pltpu.VMEM(tile, F32),
                pltpu.VMEM(tile, F32),
                pltpu.SemaphoreType.DMA((CHUNKS, 2)),
            ],
            name="combine",
        )
    )


def solution(mesh):
    split = Mesh(mesh.devices.reshape(mesh.shape["ty"], 4, 4, 2), ("ty", "tx_0", "tx_1", "tx_2"))
    in_specs = (P(TY_TX, None, None), P(TY_TX, None, None), P(TY_TX, None), P(TY_TX), P("ty", TX))
    out_specs = (P("ty", TX), P("ty", TX))
    return jax.shard_map(
        shards, mesh=split, in_specs=in_specs, out_specs=out_specs, check_vma=False
    )
```

```python
import functools

import jax
import jax.numpy as jnp
import numpy as np
from jax import lax
from jax.experimental import pallas as pl
from jax.experimental.pallas import tpu as pltpu
from jax.sharding import Mesh
from jax.sharding import PartitionSpec as P

HALF = 32
LANES = 128
SLOTS = 2
GROUPS = 2
CHUNKS = 4
TY_TX = ("ty", "tx_0", "tx_1", "tx_2")
TX = ("tx_0", "tx_1", "tx_2")
F32 = jnp.float32
BF16 = jnp.bfloat16


def taps(offset):
    def raw(d):
        scaled = np.abs(d) / (HALF + 1.0)
        return np.where(np.abs(d) <= HALF, (1.0 - scaled) ** 4 * (1.0 + 4.0 * scaled), 0.0)

    values = raw(offset) / raw(np.arange(-HALF, HALF + 1)).sum()
    head = values.astype(BF16)
    tail = (values - head.astype(np.float64)).astype(BF16)
    return jnp.asarray(head), jnp.asarray(tail)


def split2(x):
    head = x.astype(BF16)
    return head, (x - head.astype(F32)).astype(BF16)


def split3(x):
    head = x.astype(BF16)
    rest = x - head.astype(F32)
    mid = rest.astype(BF16)
    return head, mid, (rest - mid.astype(F32)).astype(BF16)


def mm(a, b):
    return jnp.dot(a, b, preferred_element_type=F32)


def pick(select, x):
    head, mid, tail = split3(x)
    return mm(select, tail) + mm(select, mid) + mm(select, head)


def smooth3(left, right):
    (lh, ll), (rh, rl) = left, right
    return mm(ll, rh) + mm(lh, rl) + mm(lh, rh)


def iota(shape, dim):
    return lax.broadcasted_iota(jnp.int32, shape, dim)


def pack_kernel(
    n_tx, parts, length, tile_hbm, row_hbm, sums_hbm, weights_hbm, out_hbm,
    tile_ref, row_ref, sums_ref, weights_ref, split_ref, out_ref, in_sem, out_sem
):
    fetches = [
        pltpu.make_async_copy(src, dst, in_sem.at[i])
        for i, (src, dst) in enumerate(
            (
                (tile_hbm, tile_ref),
                (row_hbm, row_ref),
                (sums_hbm, sums_ref),
                (weights_hbm, weights_ref),
            )
        )
    ]
    for fetch in fetches:
        fetch.start()
    fetches[0].wait()
    fetches[1].wait()
    count = tile_ref.shape[1]
    devices = out_ref.shape[0] // length
    group = devices // GROUPS
    tile = tile_ref[...]
    t = iota((devices, count), 0)
    same = tile == t
    earlier = iota((count, count), 0) < iota((count, count), 1)
    before = mm(same.astype(F32).astype(BF16), earlier.astype(F32).astype(BF16))
    rank = jnp.sum(jnp.where(same, before, 0.0), axis=0, keepdims=True)
    column = lax.rem(t, n_tx)
    from_left = (tile + 1 == t) & (column != 0)
    from_right = (tile - 1 == t) & (column != n_tx - 1)

    def onehot(mask, k):
        return jnp.where(mask & (rank == float(k)), 1.0, 0.0)

    own = [onehot(same, k) for k in range(SLOTS)]
    left = [onehot(from_left, k) for k in range(SLOTS)]
    right = [
        jnp.concatenate([onehot(from_right, k), own[k]], axis=1) for k in range(SLOTS)
    ]

    def of_group(masks, g):
        part = slice(g * group, (g + 1) * group)
        return jnp.concatenate([m[part] for m in masks], axis=0).astype(BF16)

    lane = iota((count, LANES), 1)
    number = jnp.transpose(jnp.broadcast_to(row_ref[...].astype(F32) + 1.0, (count, count)))
    for which, ref in enumerate((sums_ref, weights_ref)):
        fetches[2 + which].wait()
        for c in range(parts):
            at = slice((which * parts + c) * LANES, (which * parts + c + 1) * LANES)
            for i, piece in enumerate(split3(ref[pl.ds(c, count, stride=parts), :])):
                split_ref[i, :, at] = piece

    last = parts - 1
    s_last = sums_ref[pl.ds(last, count, stride=parts), :]
    w_last = pltpu.roll(weights_ref[pl.ds(last, count, stride=parts), :], 64, 1)
    s_first = sums_ref[pl.ds(0, count, stride=parts), :]
    w_first = pltpu.roll(weights_ref[pl.ds(0, count, stride=parts), :], 64, 1)
    left_rows = jnp.where(
        lane >= 64, s_last, jnp.where(lane >= 32, w_last, jnp.where(lane == 0, number, 0.0))
    )
    right_rows = jnp.where(
        lane < 64, s_first, jnp.where(lane < 96, w_first, jnp.where(lane == 96, number, 0.0))
    )
    own_rows = jnp.where(lane == 97, number, 0.0)
    both_rows = jnp.concatenate([right_rows, own_rows], axis=0)

    base = 2 * SLOTS * parts
    sends = []
    for g in range(GROUPS):
        first = g * group * length
        own_all = of_group(own, g)
        for c in range(0, 2 * parts, 2):
            at = slice(c * LANES, (c + 2) * LANES)
            y = (
                mm(own_all, split_ref[2, :, at])
                + mm(own_all, split_ref[1, :, at])
                + mm(own_all, split_ref[0, :, at])
            )
            which, chunk = divmod(c, parts)
            for k in range(SLOTS):
                for i in range(2):
                    to = first + (which * SLOTS + k) * parts + chunk + i
                    out_ref[pl.ds(to, group, stride=length), :] = y[
                        k * group : (k + 1) * group, i * LANES : (i + 1) * LANES
                    ]
        to_left = pick(of_group(left, g), left_rows)
        to_right = pick(of_group(right, g), both_rows)
        for k in range(SLOTS):
            part = slice(k * group, (k + 1) * group)
            out_ref[pl.ds(first + base + k, group, stride=length), :] = to_left[part]
            out_ref[pl.ds(first + base + SLOTS + k, group, stride=length), :] = to_right[part]
        span = pl.ds(first, group * length)
        send = pltpu.make_async_copy(out_ref.at[span], out_hbm.at[span], out_sem.at[g])
        send.start()
        sends.append(send)
    for send in sends:
        send.wait()


def slot_rows(got_ref, length, at, devices):
    return got_ref[pl.ds(at, devices, stride=length), :]


def gather_tile(got_ref, parts, length, which, select, dst, extra):
    devices = got_ref.shape[0] // length
    for c in range(0, parts, 2):
        x = jnp.concatenate(
            [
                jnp.concatenate(
                    [
                        slot_rows(got_ref, length, (which * SLOTS + k) * parts + c + i, devices)
                        for i in range(2)
                    ],
                    axis=1,
                )
                for k in range(SLOTS)
            ],
            axis=0,
        )
        at = slice(c * LANES, (c + 2) * LANES)
        y = pick(select, x)
        dst[:, at] = y if extra is None else y + extra[:, at]


def sums_kernel(parts, length, got_ref, s_ref, up_ref, down_ref, select_ref, strip_ref):
    rows, wide = s_ref.shape
    cols = wide - LANES
    devices = got_ref.shape[0] // length
    base = 2 * SLOTS * parts
    from_left = [slot_rows(got_ref, length, base + k, devices) for k in range(SLOTS)]
    from_right = [slot_rows(got_ref, length, base + SLOTS + k, devices) for k in range(SLOTS)]
    left_t = [jnp.transpose(x) for x in from_left]
    right_t = [jnp.transpose(x) for x in from_right]
    wanted = (iota((rows, devices), 0) + 1).astype(F32)

    def chooser(lists, at):
        return jnp.concatenate(
            [jnp.where(x[at : at + 1, :] == wanted, 1.0, 0.0) for x in lists], axis=1
        ).astype(BF16)

    own = chooser(right_t, 97)
    select_ref[...] = own
    gather_tile(got_ref, parts, length, 0, own, s_ref, None)
    left = pick(chooser(left_t, 0), jnp.concatenate(from_left, axis=0))
    right = pick(chooser(right_t, 96), jnp.concatenate(from_right, axis=0))
    lane = iota((rows, LANES), 1)
    s_ref[:, cols:] = jnp.where(lane < 64, right, left)
    strip_ref[...] = jnp.where(lane < 64, pltpu.roll(right, 64, 1), pltpu.roll(left, 64, 1))
    up_ref[...] = s_ref[: 2 * HALF, :]
    down_ref[...] = s_ref[rows - 2 * HALF :, :]


def weights_kernel(
    parts, length, n_tx, got_ref, prior_ref, prior_halo_ref, select_ref, strip_ref,
    w_ref, up_ref, down_ref
):
    rows, wide = w_ref.shape
    cols = wide - LANES
    gather_tile(got_ref, parts, length, 1, select_ref[...], w_ref, prior_ref)
    lane = iota((rows, LANES), 1)
    column = lax.axis_index(TX)
    has_left = jnp.where(column > 0, 1.0, 0.0)
    has_right = jnp.where(column < n_tx - 1, 1.0, 0.0)
    prior_halo = prior_halo_ref[...]
    strip = strip_ref[...]
    w_ref[:, cols:] = jnp.where(
        lane < HALF,
        prior_halo * has_right + strip,
        jnp.where(lane >= LANES - HALF, prior_halo * has_left + strip, 0.0),
    )
    up_ref[...] = w_ref[:HALF, :]
    down_ref[...] = w_ref[rows - HALF :, :]


def with_halo(n_ty, above_ref, ref, below_ref, at):
    row_at = lax.axis_index("ty")
    above = above_ref[:, at] * jnp.where(row_at > 0, 1.0, 0.0)
    below = below_ref[:, at] * jnp.where(row_at < n_ty - 1, 1.0, 0.0)
    return jnp.concatenate([above, ref[:, at], below], axis=0)


def along_columns(mid_ref, c, height, col):
    cols = mid_ref.shape[1] - LANES
    lo, hi = (c - 1) * LANES, (c + 3) * LANES
    if c == 0:
        x = jnp.concatenate([mid_ref[:height, cols:], mid_ref[:height, :hi]], axis=1)
    else:
        x = mid_ref[:height, lo:hi]
    return smooth3(split2(x), col)


def first_kernel(
    n_ty,
    s_ref,
    w_ref,
    above_ref,
    below_ref,
    row_h_ref,
    row_l_ref,
    col_h_ref,
    col_l_ref,
    edge_h_ref,
    edge_l_ref,
    y0_ref,
    root_ref,
    r0_ref,
    m0_ref,
    mid_ref,
):
    rows, wide = s_ref.shape
    cols = wide - LANES
    tall = rows + 2 * HALF
    row = (row_h_ref[...], row_l_ref[...])
    col = (col_h_ref[...], col_l_ref[...])
    for c in range(0, wide, LANES * 3):
        at = slice(c, c + LANES * 3)
        mid_ref[:, at] = smooth3(row, split2(with_halo(n_ty, above_ref, s_ref, below_ref, at)))
    for c in range(0, cols // LANES, 2):
        at = slice(c * LANES, (c + 2) * LANES)
        y0_ref[:, at] = along_columns(mid_ref, c, tall, col)
    x = jnp.concatenate([mid_ref[:, cols - LANES :], mid_ref[:, :LANES]], axis=1)
    y0_ref[:, cols:] = smooth3(split2(x), (edge_h_ref[...], edge_l_ref[...]))
    total = jnp.zeros((8, cols), F32)
    for r in range(0, rows, 8):
        at = slice(r, r + 8)
        root = jnp.sqrt(w_ref[at, :cols])
        r0 = s_ref[at, :cols] / root
        root_ref[at, :] = root
        r0_ref[at, :] = r0
        total += r0 * r0
    m0_ref[...] = sum(total[:, c : c + LANES] for c in range(0, cols, LANES))


def folded(total):
    rows, cols = total.shape
    total = sum(total[r : r + 8] for r in range(0, rows, 8))
    return sum(total[:, c : c + LANES] for c in range(0, cols, LANES))


def second_kernel(
    s_ref,
    w_ref,
    y0_ref,
    root_ref,
    m0_ref,
    own_h_ref,
    own_l_ref,
    col_h_ref,
    col_l_ref,
    b0_ref,
    inner_ref,
    z_ref,
    mid_ref,
    sums_ref,
    deep_ref,
):
    rows, wide = s_ref.shape
    cols = wide - LANES
    tile = slice(HALF, HALF + rows)
    deep = slice(HALF, rows - HALF)
    row = (own_h_ref[...], own_l_ref[...])
    col = (col_h_ref[...], col_l_ref[...])
    for c in range(0, wide, LANES * 3):
        at = slice(c, c + LANES * 3)
        z = w_ref[:, at] * y0_ref[tile, at]
        z_ref[:, at] = z
        mid = smooth3(row, split2(z))
        mid_ref[:, at] = mid
        deep_ref[:, at] = mid[deep]
    total_sy = total_zy = total_zz = jnp.zeros((8, LANES), F32)
    for c in range(0, cols // LANES, 2):
        at = slice(c * LANES, (c + 2) * LANES)
        y0 = y0_ref[tile, at]
        b0_ref[:, at] = root_ref[:, at] * y0
        total_sy += folded(s_ref[:, at] * y0)
        total_zy += folded(z_ref[:, at] * y0)
        y1 = along_columns(deep_ref, c, rows - 2 * HALF, col)
        inner_ref[:, at] = root_ref[deep, at] * y1
        total_zz += folded(z_ref[deep, at] * y1)
    for i, total in enumerate((m0_ref[...], total_sy, total_zy, total_zz)):
        sums_ref[8 * i : 8 * i + 8, :] = total


def third_kernel(
    n_ty,
    above_ref,
    below_ref,
    y0_ref,
    root_ref,
    z_ref,
    part_ref,
    inner_ref,
    sums_ref,
    halo_h_ref,
    halo_l_ref,
    col_h_ref,
    col_l_ref,
    b1_ref,
    moments_ref,
    mid_ref,
):
    rows, wide = z_ref.shape
    cols = wide - LANES
    row_at = lax.axis_index("ty")
    has_above = jnp.where(row_at > 0, 1.0, 0.0)
    has_below = jnp.where(row_at < n_ty - 1, 1.0, 0.0)
    row = (halo_h_ref[...], halo_l_ref[...])
    col = (col_h_ref[...], col_l_ref[...])
    top, bottom = slice(0, HALF), slice(rows - HALF, rows)
    b1_ref[HALF : rows - HALF, :] = inner_ref[...]

    def border(ref, at):
        return jnp.concatenate([ref[top, at], ref[bottom, at]], axis=0)

    for c in range(0, wide, LANES * 3):
        at = slice(c, c + LANES * 3)
        z = jnp.concatenate(
            [
                above_ref[:, at] * has_above * y0_ref[:HALF, at],
                below_ref[:, at] * has_below * y0_ref[rows + HALF :, at],
            ],
            axis=0,
        )
        mid_ref[:, at] = border(part_ref, at) + smooth3(row, split2(z))
    total_zz = sums_ref[24:32, :]
    for c in range(0, cols // LANES, 2):
        at = slice(c * LANES, (c + 2) * LANES)
        y1 = along_columns(mid_ref, c, 2 * HALF, col)
        b1 = border(root_ref, at) * y1
        b1_ref[top, at] = b1[:HALF]
        b1_ref[bottom, at] = b1[HALF:]
        total_zz += folded(border(z_ref, at) * y1)
    lane = iota((1, LANES), 1)
    packed = jnp.zeros((1, LANES), F32)
    for i, total in enumerate((sums_ref[0:8, :], sums_ref[8:16, :], sums_ref[16:24, :], total_zz)):
        value = jnp.sum(jnp.sum(total, axis=0, keepdims=True), axis=1, keepdims=True)
        packed = jnp.where(lane == i, value, packed)
    moments_ref[...] = jnp.broadcast_to(packed, moments_ref.shape)


def final_kernel(moments_ref, r0_ref, b0_ref, b1_ref, x_hbm, r_hbm, x_ref, r_ref, sem):
    totals = jnp.sum(moments_ref[...], axis=0, keepdims=True)
    lane = iota(totals.shape, 1)
    m0, n1, n2, n3 = (
        jnp.sum(jnp.where(lane == i, totals, 0.0), axis=1, keepdims=True) for i in range(4)
    )
    mu = n1 / m0
    a = m0 / (0.5 * m0 + n1)
    vv = n2 - mu * n1
    vbv = n3 - 2.0 * mu * n2 + mu * mu * n1
    beta = a * a * vv / m0
    step = vv / (0.5 * vv + vbv - a * vv * vv / m0)
    x_r0 = a + step * beta + step * a * mu
    x_b0 = -step * a
    r_r0 = a * mu - step * (0.5 * a * mu + 0.5 * beta)
    r_b0 = -a - step * (a * mu - 0.5 * a + beta)
    r_b1 = step * a
    sends = []
    step_rows = r0_ref.shape[0] // CHUNKS
    for c in range(CHUNKS):
        at = slice(c * step_rows, (c + 1) * step_rows)
        r0 = r0_ref[at, :]
        b0 = b0_ref[at, :]
        x_ref[at, :] = x_r0 * r0 + x_b0 * b0
        r_ref[at, :] = r_r0 * r0 + r_b0 * b0 + r_b1 * b1_ref[at, :]
        for i, (src, dst) in enumerate(((x_ref, x_hbm), (r_ref, r_hbm))):
            send = pltpu.make_async_copy(src.at[at], dst.at[at], sem.at[c, i])
            send.start()
            sends.append(send)
    for send in sends:
        send.wait()


VMEM = pl.BlockSpec(memory_space=pltpu.VMEM)
ANY = pl.BlockSpec(memory_space=pl.ANY)
HBM = pl.BlockSpec(memory_space=pltpu.HBM)


def call(kernel, shapes, *args, ins=None, outs=None, scratch=(), name, limit=24, flops=0):
    moved = sum(int(np.prod(x.shape)) * x.dtype.itemsize for x in args)
    return pl.pallas_call(
        kernel,
        out_shape=[
            jax.ShapeDtypeStruct(s, F32) if isinstance(s, tuple) else s for s in shapes
        ],
        in_specs=ins or [VMEM] * len(args),
        out_specs=outs or [VMEM] * len(shapes),
        scratch_shapes=list(scratch),
        compiler_params=pltpu.CompilerParams(vmem_limit_bytes=limit << 20),
        cost_estimate=pl.CostEstimate(flops=flops, bytes_accessed=moved, transcendentals=0),
        name=name,
    )(*args)


def neighbours(axes, step):
    count = int(np.prod([lax.axis_size(a) for a in axes]))
    return [(i, (i + step) % count) for i in range(count)]


def shards(block_sums, block_weights, block_tile, block_row, prior_weight):
    devices = lax.axis_size(TY_TX)
    n_tx = lax.axis_size(TX)
    blocks, _, cols = block_sums.shape
    rows = prior_weight.shape[0]
    parts = cols // LANES
    length = 2 * SLOTS * parts + 2 * SLOTS
    wide = cols + LANES

    prior_right = lax.ppermute(prior_weight[:, :LANES], TX, neighbours(TX, -1))
    prior_left = lax.ppermute(prior_weight[:, cols - LANES :], TX, neighbours(TX, 1))
    lane = jnp.arange(LANES)[None, :]
    prior_halo = jnp.where(lane < HALF, prior_right, jnp.where(lane >= LANES - HALF, prior_left, 0.0))

    (message,) = call(
        functools.partial(pack_kernel, n_tx, parts, length),
        [(devices * length, LANES)],
        block_tile.reshape(1, blocks),
        block_row.reshape(1, blocks),
        block_sums.reshape(blocks * parts, LANES),
        block_weights.reshape(blocks * parts, LANES),
        ins=[HBM] * 4,
        outs=[HBM],
        scratch=[
            pltpu.VMEM((1, blocks), jnp.int32),
            pltpu.VMEM((1, blocks), jnp.int32),
            pltpu.VMEM((blocks * parts, LANES), F32),
            pltpu.VMEM((blocks * parts, LANES), F32),
            pltpu.VMEM((3, blocks, 2 * cols), BF16),
            pltpu.VMEM((devices * length, LANES), F32),
            pltpu.SemaphoreType.DMA((4,)),
            pltpu.SemaphoreType.DMA((GROUPS,)),
        ],
        name="pack",
        limit=63,
    )
    got = lax.all_to_all(
        message.reshape(devices, 1, length * LANES), TY_TX, split_axis=0, concat_axis=0, tiled=True
    ).reshape(devices * length, LANES)
    s_slab, w_slab = (2 * HALF, wide), (HALF, wide)
    s, s_up, s_down, chosen, strip = call(
        functools.partial(sums_kernel, parts, length),
        [
            (rows, wide),
            s_slab,
            s_slab,
            jax.ShapeDtypeStruct((rows, SLOTS * devices), BF16),
            (rows, LANES),
        ],
        got,
        flops=3 * 2 * rows * wide * SLOTS * devices,
        name="sums",
    )
    w, w_up, w_down = call(
        functools.partial(weights_kernel, parts, length, n_tx),
        [(rows, wide), w_slab, w_slab],
        got,
        prior_weight,
        prior_halo,
        chosen,
        strip,
        flops=3 * 2 * rows * wide * SLOTS * devices,
        name="weights",
    )
    n_ty = lax.axis_size("ty")
    downward, upward = neighbours(("ty",), 1), neighbours(("ty",), -1)
    s_above, s_below = lax.ppermute(s_down, "ty", downward), lax.ppermute(s_up, "ty", upward)
    w_above, w_below = lax.ppermute(w_down, "ty", downward), lax.ppermute(w_up, "ty", upward)

    tall = rows + 2 * HALF
    row_taps = taps(np.arange(tall)[:, None] - np.arange(rows + 4 * HALF)[None, :] + HALF)
    col_taps = taps(np.arange(2 * LANES)[None, :] - np.arange(4 * LANES)[:, None] + LANES)
    ring = np.where(np.arange(LANES) < 64, cols, -LANES) + np.arange(LANES)
    near = np.concatenate([np.arange(cols - LANES, cols), ring, np.arange(LANES)])
    edge_taps = taps(ring[None, :] - near[:, None])
    tile = (rows, cols)
    y0, root, r0, m0 = call(
        functools.partial(first_kernel, n_ty),
        [(tall, wide), tile, tile, (8, LANES)],
        s,
        w,
        s_above,
        s_below,
        *row_taps,
        *col_taps,
        *edge_taps,
        scratch=[pltpu.VMEM((tall, wide), F32)],
        flops=3 * 2 * tall * wide * (2 * LANES + 4 * LANES),
        name="first",
    )
    inside = np.arange(rows)
    own_taps = taps(inside[:, None] - inside[None, :])
    border = np.concatenate([inside[:HALF], inside[rows - HALF :]])
    outside = np.concatenate([np.arange(-HALF, 0), np.arange(rows, rows + HALF)])
    halo_taps = taps(border[:, None] - outside[None, :])
    b0, inner, z, part, sums = call(
        second_kernel,
        [tile, (rows - 2 * HALF, cols), (rows, wide), (rows, wide), (32, LANES)],
        s,
        w,
        y0,
        root,
        m0,
        *own_taps,
        *col_taps,
        scratch=[pltpu.VMEM((rows - 2 * HALF, wide), F32)],
        flops=3 * 2 * rows * wide * 3 * LANES,
        name="second",
    )
    b1, moments = call(
        functools.partial(third_kernel, n_ty),
        [tile, (devices, LANES)],
        w_above,
        w_below,
        y0,
        root,
        z,
        part,
        inner,
        sums,
        *halo_taps,
        *col_taps,
        scratch=[pltpu.VMEM((2 * HALF, wide), F32)],
        flops=3 * 2 * rows * wide * 3 * LANES,
        name="third",
    )
    moments = lax.all_to_all(
        moments.reshape(devices, 1, LANES), TY_TX, split_axis=0, concat_axis=0, tiled=True
    ).reshape(devices, LANES)
    return tuple(
        call(
            final_kernel,
            [tile, tile],
            moments,
            r0,
            b0,
            b1,
            outs=[HBM, HBM],
            scratch=[
                pltpu.VMEM(tile, F32),
                pltpu.VMEM(tile, F32),
                pltpu.SemaphoreType.DMA((CHUNKS, 2)),
            ],
            name="combine",
        )
    )


def solution(mesh):
    split = Mesh(mesh.devices.reshape(mesh.shape["ty"], 4, 4, 2), ("ty", "tx_0", "tx_1", "tx_2"))
    in_specs = (P(TY_TX, None, None), P(TY_TX, None, None), P(TY_TX, None), P(TY_TX), P("ty", TX))
    out_specs = (P("ty", TX), P("ty", TX))
    return jax.shard_map(
        shards, mesh=split, in_specs=in_specs, out_specs=out_specs, check_vma=False
    )
```

```python
import functools

import jax
import jax.numpy as jnp
import numpy as np
from jax import lax
from jax.experimental import pallas as pl
from jax.experimental.pallas import tpu as pltpu
from jax.sharding import Mesh
from jax.sharding import PartitionSpec as P

HALF = 32
LANES = 128
SLOTS = 2
GROUPS = 2
CHUNKS = 4
TY_TX = ("ty", "tx_0", "tx_1", "tx_2")
TX = ("tx_0", "tx_1", "tx_2")
F32 = jnp.float32
BF16 = jnp.bfloat16


def taps(offset, axis):
    def raw(d):
        scaled = np.abs(d) / (HALF + 1.0)
        return np.where(np.abs(d) <= HALF, (1.0 - scaled) ** 4 * (1.0 + 4.0 * scaled), 0.0)

    values = raw(offset) / raw(np.arange(-HALF, HALF + 1)).sum()
    head = values.astype(BF16)
    tail = (values - head.astype(np.float64)).astype(BF16)
    return jnp.asarray(np.concatenate([head, tail], axis=axis))


def split3(x):
    head = x.astype(BF16)
    rest = x - head.astype(F32)
    mid = rest.astype(BF16)
    return head, mid, (rest - mid.astype(F32)).astype(BF16)


def mm(a, b):
    return jnp.dot(a, b, preferred_element_type=F32)


def pick(select, x):
    head, mid, tail = split3(x)
    return mm(select, tail) + mm(select, mid) + mm(select, head)


def taps_times(taps_ref, x):
    rows = taps_ref.shape[0] // 2
    xh, xm, xl = split3(x)
    low = mm(taps_ref[:rows, :], xl)
    mid = mm(taps_ref[...], xm)
    high = mm(taps_ref[...], xh)
    return low + mid[rows:] + high[rows:] + mid[:rows] + high[:rows]


def times_taps(pieces, taps_ref):
    xh, xm, xl = pieces
    depth = taps_ref.shape[0] // 2
    head, tail = taps_ref[:depth, :], taps_ref[depth:, :]
    return mm(xl, head) + mm(xm, tail) + mm(xh, tail) + mm(xm, head) + mm(xh, head)


def spans(wide):
    cols = wide - LANES
    return [slice(c, c + 2 * LANES) for c in range(0, cols, 2 * LANES)] + [slice(cols, wide)]


def iota(shape, dim):
    return lax.broadcasted_iota(jnp.int32, shape, dim)


def pack_kernel(
    n_tx, parts, length, tile_hbm, row_hbm, sums_hbm, weights_hbm, out_hbm,
    tile_ref, row_ref, sums_ref, weights_ref, split_ref, out_ref, in_sem, out_sem
):
    fetches = [
        pltpu.make_async_copy(src, dst, in_sem.at[i])
        for i, (src, dst) in enumerate(
            (
                (tile_hbm, tile_ref),
                (row_hbm, row_ref),
                (sums_hbm, sums_ref),
                (weights_hbm, weights_ref),
            )
        )
    ]
    for fetch in fetches:
        fetch.start()
    fetches[0].wait()
    fetches[1].wait()
    count = tile_ref.shape[1]
    devices = out_ref.shape[0] // length
    group = devices // GROUPS
    tile = tile_ref[...]
    t = iota((devices, count), 0)
    same = tile == t
    earlier = iota((count, count), 0) < iota((count, count), 1)
    before = mm(same.astype(F32).astype(BF16), earlier.astype(F32).astype(BF16))
    rank = jnp.sum(jnp.where(same, before, 0.0), axis=0, keepdims=True)
    column = lax.rem(t, n_tx)
    from_left = (tile + 1 == t) & (column != 0)
    from_right = (tile - 1 == t) & (column != n_tx - 1)

    def onehot(mask, k):
        return jnp.where(mask & (rank == float(k)), 1.0, 0.0)

    own = [onehot(same, k) for k in range(SLOTS)]
    left = [onehot(from_left, k) for k in range(SLOTS)]
    right = [
        jnp.concatenate([onehot(from_right, k), own[k]], axis=1) for k in range(SLOTS)
    ]

    def of_group(masks, g):
        part = slice(g * group, (g + 1) * group)
        return jnp.concatenate([m[part] for m in masks], axis=0).astype(BF16)

    lane = iota((count, LANES), 1)
    number = jnp.transpose(jnp.broadcast_to(row_ref[...].astype(F32) + 1.0, (count, count)))
    for which, ref in enumerate((sums_ref, weights_ref)):
        fetches[2 + which].wait()
        for c in range(parts):
            at = slice((which * parts + c) * LANES, (which * parts + c + 1) * LANES)
            for i, piece in enumerate(split3(ref[pl.ds(c, count, stride=parts), :])):
                split_ref[i, :, at] = piece

    last = parts - 1
    s_last = sums_ref[pl.ds(last, count, stride=parts), :]
    w_last = pltpu.roll(weights_ref[pl.ds(last, count, stride=parts), :], 64, 1)
    s_first = sums_ref[pl.ds(0, count, stride=parts), :]
    w_first = pltpu.roll(weights_ref[pl.ds(0, count, stride=parts), :], 64, 1)
    left_rows = jnp.where(
        lane >= 64, s_last, jnp.where(lane >= 32, w_last, jnp.where(lane == 0, number, 0.0))
    )
    right_rows = jnp.where(
        lane < 64, s_first, jnp.where(lane < 96, w_first, jnp.where(lane == 96, number, 0.0))
    )
    own_rows = jnp.where(lane == 97, number, 0.0)
    both_rows = jnp.concatenate([right_rows, own_rows], axis=0)

    base = 2 * SLOTS * parts
    sends = []
    for g in range(GROUPS):
        first = g * group * length
        own_all = of_group(own, g)
        for c in range(0, 2 * parts, 2):
            at = slice(c * LANES, (c + 2) * LANES)
            y = (
                mm(own_all, split_ref[2, :, at])
                + mm(own_all, split_ref[1, :, at])
                + mm(own_all, split_ref[0, :, at])
            )
            which, chunk = divmod(c, parts)
            for k in range(SLOTS):
                for i in range(2):
                    to = first + (which * SLOTS + k) * parts + chunk + i
                    out_ref[pl.ds(to, group, stride=length), :] = y[
                        k * group : (k + 1) * group, i * LANES : (i + 1) * LANES
                    ]
        to_left = pick(of_group(left, g), left_rows)
        to_right = pick(of_group(right, g), both_rows)
        for k in range(SLOTS):
            part = slice(k * group, (k + 1) * group)
            out_ref[pl.ds(first + base + k, group, stride=length), :] = to_left[part]
            out_ref[pl.ds(first + base + SLOTS + k, group, stride=length), :] = to_right[part]
        span = pl.ds(first, group * length)
        send = pltpu.make_async_copy(out_ref.at[span], out_hbm.at[span], out_sem.at[g])
        send.start()
        sends.append(send)
    for send in sends:
        send.wait()


def slot_rows(got_ref, length, at, devices):
    return got_ref[pl.ds(at, devices, stride=length), :]


def gather_tile(got_ref, parts, length, which, select, dst, extra):
    devices = got_ref.shape[0] // length
    for c in range(0, parts, 2):
        x = jnp.concatenate(
            [
                jnp.concatenate(
                    [
                        slot_rows(got_ref, length, (which * SLOTS + k) * parts + c + i, devices)
                        for i in range(2)
                    ],
                    axis=1,
                )
                for k in range(SLOTS)
            ],
            axis=0,
        )
        at = slice(c * LANES, (c + 2) * LANES)
        y = pick(select, x)
        dst[:, at] = y if extra is None else y + extra[:, at]


def sums_kernel(parts, length, got_ref, s_ref, up_ref, down_ref, select_ref, strip_ref):
    rows, wide = s_ref.shape
    cols = wide - LANES
    devices = got_ref.shape[0] // length
    base = 2 * SLOTS * parts
    from_left = [slot_rows(got_ref, length, base + k, devices) for k in range(SLOTS)]
    from_right = [slot_rows(got_ref, length, base + SLOTS + k, devices) for k in range(SLOTS)]
    left_t = [jnp.transpose(x) for x in from_left]
    right_t = [jnp.transpose(x) for x in from_right]
    wanted = (iota((rows, devices), 0) + 1).astype(F32)

    def chooser(lists, at):
        return jnp.concatenate(
            [jnp.where(x[at : at + 1, :] == wanted, 1.0, 0.0) for x in lists], axis=1
        ).astype(BF16)

    own = chooser(right_t, 97)
    select_ref[...] = own
    gather_tile(got_ref, parts, length, 0, own, s_ref, None)
    left = pick(chooser(left_t, 0), jnp.concatenate(from_left, axis=0))
    right = pick(chooser(right_t, 96), jnp.concatenate(from_right, axis=0))
    lane = iota((rows, LANES), 1)
    s_ref[:, cols:] = jnp.where(lane < 64, right, left)
    strip_ref[...] = jnp.where(lane < 64, pltpu.roll(right, 64, 1), pltpu.roll(left, 64, 1))
    up_ref[...] = s_ref[: 2 * HALF, :]
    down_ref[...] = s_ref[rows - 2 * HALF :, :]


def weights_kernel(
    parts, length, n_tx, got_ref, prior_ref, prior_halo_ref, select_ref, strip_ref,
    w_ref, up_ref, down_ref
):
    rows, wide = w_ref.shape
    cols = wide - LANES
    gather_tile(got_ref, parts, length, 1, select_ref[...], w_ref, prior_ref)
    lane = iota((rows, LANES), 1)
    column = lax.axis_index(TX)
    has_left = jnp.where(column > 0, 1.0, 0.0)
    has_right = jnp.where(column < n_tx - 1, 1.0, 0.0)
    prior_halo = prior_halo_ref[...]
    strip = strip_ref[...]
    w_ref[:, cols:] = jnp.where(
        lane < HALF,
        prior_halo * has_right + strip,
        jnp.where(lane >= LANES - HALF, prior_halo * has_left + strip, 0.0),
    )
    up_ref[...] = w_ref[:HALF, :]
    down_ref[...] = w_ref[rows - HALF :, :]


def with_halo(n_ty, above_ref, ref, below_ref, at):
    row_at = lax.axis_index("ty")
    above = above_ref[:, at] * jnp.where(row_at > 0, 1.0, 0.0)
    below = below_ref[:, at] * jnp.where(row_at < n_ty - 1, 1.0, 0.0)
    return jnp.concatenate([above, ref[:, at], below], axis=0)


def along_columns(pieces, taps_ref):
    height, wide = pieces[0].shape
    cols = wide - LANES

    def stacked(x):
        first = jnp.concatenate([x[:, cols:], x[:, : 3 * LANES]], axis=1)
        rest = [
            x[:, (c - 1) * LANES : (c + 3) * LANES] for c in range(2, cols // LANES, 2)
        ]
        return jnp.concatenate([first] + rest, axis=0)

    half = [stacked(x) for x in pieces]
    out = []
    for r in range(0, half[0].shape[0], 2 * height):
        y = times_taps([x[r : r + 2 * height] for x in half], taps_ref)
        out += [y[:height], y[height:]]
    return out


def first_kernel(
    n_ty,
    s_ref,
    w_ref,
    above_ref,
    below_ref,
    row_ref,
    col_ref,
    edge_ref,
    y0_ref,
    root_ref,
    r0_ref,
    sums_ref,
    mid_ref,
):
    rows, wide = s_ref.shape
    cols = wide - LANES
    for at in spans(wide):
        mid_ref[:, at] = taps_times(row_ref, with_halo(n_ty, above_ref, s_ref, below_ref, at))
    pieces = split3(mid_ref[...])
    for c, y in enumerate(along_columns(pieces, col_ref)):
        y0_ref[:, 2 * c * LANES : 2 * (c + 1) * LANES] = y
    near = [jnp.concatenate([x[:, cols - LANES :], x[:, :LANES]], axis=1) for x in pieces]
    y0_ref[:, cols:] = times_taps(near, edge_ref)
    total_rr = total_rb = jnp.zeros((8, cols), F32)
    for r in range(0, rows, 8):
        at = slice(r, r + 8)
        root = jnp.sqrt(w_ref[at, :cols])
        s = s_ref[at, :cols]
        r0 = s / root
        root_ref[at, :] = root
        r0_ref[at, :] = r0
        total_rr += r0 * r0
        total_rb += s * y0_ref[HALF + r : HALF + r + 8, :cols]
    for i, total in enumerate((total_rr, total_rb)):
        sums_ref[8 * i : 8 * i + 8, :] = sum(
            total[:, c : c + LANES] for c in range(0, cols, LANES)
        )


def folded(total):
    rows, cols = total.shape
    total = sum(total[r : r + 8] for r in range(0, rows, 8))
    return sum(total[:, c : c + LANES] for c in range(0, cols, LANES))


def whole(total):
    return jnp.sum(jnp.sum(total, axis=0, keepdims=True), axis=1, keepdims=True)


def centred(r0, b0, b1, c):
    v, q = b0 - c * r0, b1 - c * b0
    return v * q, v * b0 + r0 * q


def second_kernel(
    w_ref,
    y0_ref,
    root_ref,
    r0_ref,
    first_ref,
    own_ref,
    col_ref,
    b0_ref,
    inner_ref,
    mid_ref,
    sums_ref,
):
    rows, wide = w_ref.shape
    cols = wide - LANES
    tile = slice(HALF, HALF + rows)
    deep = slice(HALF, rows - HALF)
    m0, n1 = whole(first_ref[0:8, :]), whole(first_ref[8:16, :])
    c0 = n1 / jnp.where(m0 > 0.0, m0, 1.0)
    for at in spans(wide):
        mid_ref[:, at] = taps_times(own_ref, w_ref[:, at] * y0_ref[tile, at])
    total_vv = total_rv = total_vq = total_mix = jnp.zeros((8, LANES), F32)
    for c, y1 in enumerate(along_columns(split3(mid_ref[deep, :]), col_ref)):
        at = slice(2 * c * LANES, 2 * (c + 1) * LANES)
        r0 = r0_ref[:, at]
        b0 = root_ref[:, at] * y0_ref[tile, at]
        b0_ref[:, at] = b0
        v = b0 - c0 * r0
        total_vv += folded(v * v)
        total_rv += folded(r0 * v)
        b1 = root_ref[deep, at] * y1
        inner_ref[:, at] = b1
        vq, mix = centred(r0[deep], b0[deep], b1, c0)
        total_vq += folded(vq)
        total_mix += folded(mix)
    lane = iota((8, LANES), 1)
    known = jnp.zeros((8, LANES), F32)
    for i, value in enumerate((m0, n1, c0, whole(total_vv), whole(total_rv))):
        known = jnp.where(lane == i, value, known)
    sums_ref[0:8, :] = known
    sums_ref[8:16, :] = total_vq
    sums_ref[16:24, :] = total_mix


def third_kernel(
    n_ty,
    above_ref,
    below_ref,
    y0_ref,
    root_ref,
    r0_ref,
    b0_ref,
    part_ref,
    inner_ref,
    sums_ref,
    halo_ref,
    col_ref,
    b1_ref,
    moments_ref,
    mid_ref,
):
    rows, wide = part_ref.shape
    cols = wide - LANES
    row_at = lax.axis_index("ty")
    has_above = jnp.where(row_at > 0, 1.0, 0.0)
    has_below = jnp.where(row_at < n_ty - 1, 1.0, 0.0)
    top, bottom = slice(0, HALF), slice(rows - HALF, rows)
    b1_ref[HALF : rows - HALF, :] = inner_ref[...]
    known = sums_ref[0:1, :]
    lane = iota(known.shape, 1)
    c0 = jnp.sum(jnp.where(lane == 2, known, 0.0), axis=1, keepdims=True)

    def border(ref, at):
        return jnp.concatenate([ref[top, at], ref[bottom, at]], axis=0)

    for at in spans(wide):
        z = jnp.concatenate(
            [
                above_ref[:, at] * has_above * y0_ref[:HALF, at],
                below_ref[:, at] * has_below * y0_ref[rows + HALF :, at],
            ],
            axis=0,
        )
        mid_ref[:, at] = border(part_ref, at) + taps_times(halo_ref, z)
    total_vq, total_mix = sums_ref[8:16, :], sums_ref[16:24, :]
    for c, y1 in enumerate(along_columns(split3(mid_ref[...]), col_ref)):
        at = slice(2 * c * LANES, 2 * (c + 1) * LANES)
        b1 = border(root_ref, at) * y1
        b1_ref[top, at] = b1[:HALF]
        b1_ref[bottom, at] = b1[HALF:]
        vq, mix = centred(border(r0_ref, at), border(b0_ref, at), b1, c0)
        total_vq += folded(vq)
        total_mix += folded(mix)
    known = jnp.where(lane == 5, whole(total_vq), known)
    known = jnp.where(lane == 6, whole(total_mix), known)
    moments_ref[...] = jnp.broadcast_to(known, moments_ref.shape)


def final_kernel(moments_ref, r0_ref, b0_ref, b1_ref, x_hbm, r_hbm, x_ref, r_ref, sem):
    parts = jnp.transpose(moments_ref[...])
    m0_at, n1_at, c_at, vv_at, rv_at, vq_at, mix_at = (parts[i : i + 1, :] for i in range(7))

    def total(x):
        return jnp.sum(x, axis=1, keepdims=True)

    m0, n1 = total(m0_at), total(n1_at)
    mu = n1 / m0
    shift = c_at - mu
    vv = total(vv_at + shift * (2.0 * rv_at + shift * m0_at))
    vbv = total(vq_at + shift * (mix_at + shift * n1_at))
    a = m0 / (0.5 * m0 + n1)
    ratio = vv / m0
    beta = a * a * ratio
    step = vv / (0.5 * vv + vbv - a * vv * ratio)
    x_r0 = a + step * beta + step * a * mu
    x_b0 = -step * a
    r_r0 = a * mu - step * (0.5 * a * mu + 0.5 * beta)
    r_b0 = -a - step * (a * mu - 0.5 * a + beta)
    r_b1 = step * a
    sends = []
    step_rows = r0_ref.shape[0] // CHUNKS
    for c in range(CHUNKS):
        at = slice(c * step_rows, (c + 1) * step_rows)
        r0 = r0_ref[at, :]
        b0 = b0_ref[at, :]
        x_ref[at, :] = x_r0 * r0 + x_b0 * b0
        r_ref[at, :] = r_r0 * r0 + r_b0 * b0 + r_b1 * b1_ref[at, :]
        for i, (src, dst) in enumerate(((x_ref, x_hbm), (r_ref, r_hbm))):
            send = pltpu.make_async_copy(src.at[at], dst.at[at], sem.at[c, i])
            send.start()
            sends.append(send)
    for send in sends:
        send.wait()


VMEM = pl.BlockSpec(memory_space=pltpu.VMEM)
ANY = pl.BlockSpec(memory_space=pl.ANY)
HBM = pl.BlockSpec(memory_space=pltpu.HBM)


def call(kernel, shapes, *args, ins=None, outs=None, scratch=(), name, limit=24, flops=0):
    moved = sum(int(np.prod(x.shape)) * x.dtype.itemsize for x in args)
    return pl.pallas_call(
        kernel,
        out_shape=[
            jax.ShapeDtypeStruct(s, F32) if isinstance(s, tuple) else s for s in shapes
        ],
        in_specs=ins or [VMEM] * len(args),
        out_specs=outs or [VMEM] * len(shapes),
        scratch_shapes=list(scratch),
        compiler_params=pltpu.CompilerParams(vmem_limit_bytes=limit << 20),
        cost_estimate=pl.CostEstimate(flops=flops, bytes_accessed=moved, transcendentals=0),
        name=name,
    )(*args)


def neighbours(axes, step):
    count = int(np.prod([lax.axis_size(a) for a in axes]))
    return [(i, (i + step) % count) for i in range(count)]


def shards(block_sums, block_weights, block_tile, block_row, prior_weight):
    devices = lax.axis_size(TY_TX)
    n_tx = lax.axis_size(TX)
    blocks, _, cols = block_sums.shape
    rows = prior_weight.shape[0]
    parts = cols // LANES
    length = 2 * SLOTS * parts + 2 * SLOTS
    wide = cols + LANES

    prior_right = lax.ppermute(prior_weight[:, :LANES], TX, neighbours(TX, -1))
    prior_left = lax.ppermute(prior_weight[:, cols - LANES :], TX, neighbours(TX, 1))
    lane = jnp.arange(LANES)[None, :]
    prior_halo = jnp.where(lane < HALF, prior_right, jnp.where(lane >= LANES - HALF, prior_left, 0.0))

    (message,) = call(
        functools.partial(pack_kernel, n_tx, parts, length),
        [(devices * length, LANES)],
        block_tile.reshape(1, blocks),
        block_row.reshape(1, blocks),
        block_sums.reshape(blocks * parts, LANES),
        block_weights.reshape(blocks * parts, LANES),
        ins=[HBM] * 4,
        outs=[HBM],
        scratch=[
            pltpu.VMEM((1, blocks), jnp.int32),
            pltpu.VMEM((1, blocks), jnp.int32),
            pltpu.VMEM((blocks * parts, LANES), F32),
            pltpu.VMEM((blocks * parts, LANES), F32),
            pltpu.VMEM((3, blocks, 2 * cols), BF16),
            pltpu.VMEM((devices * length, LANES), F32),
            pltpu.SemaphoreType.DMA((4,)),
            pltpu.SemaphoreType.DMA((GROUPS,)),
        ],
        name="pack",
        limit=63,
    )
    got = lax.all_to_all(
        message.reshape(devices, 1, length * LANES), TY_TX, split_axis=0, concat_axis=0, tiled=True
    ).reshape(devices * length, LANES)
    s_slab, w_slab = (2 * HALF, wide), (HALF, wide)
    s, s_up, s_down, chosen, strip = call(
        functools.partial(sums_kernel, parts, length),
        [
            (rows, wide),
            s_slab,
            s_slab,
            jax.ShapeDtypeStruct((rows, SLOTS * devices), BF16),
            (rows, LANES),
        ],
        got,
        flops=3 * 2 * rows * wide * SLOTS * devices,
        name="sums",
    )
    w, w_up, w_down = call(
        functools.partial(weights_kernel, parts, length, n_tx),
        [(rows, wide), w_slab, w_slab],
        got,
        prior_weight,
        prior_halo,
        chosen,
        strip,
        flops=3 * 2 * rows * wide * SLOTS * devices,
        name="weights",
    )
    n_ty = lax.axis_size("ty")
    downward, upward = neighbours(("ty",), 1), neighbours(("ty",), -1)
    s_above, s_below = lax.ppermute(s_down, "ty", downward), lax.ppermute(s_up, "ty", upward)
    w_above, w_below = lax.ppermute(w_down, "ty", downward), lax.ppermute(w_up, "ty", upward)

    tall = rows + 2 * HALF
    row_taps = taps(np.arange(tall)[:, None] - np.arange(rows + 4 * HALF)[None, :] + HALF, 0)
    col_taps = taps(np.arange(2 * LANES)[None, :] - np.arange(4 * LANES)[:, None] + LANES, 0)
    ring = np.where(np.arange(LANES) < 64, cols, -LANES) + np.arange(LANES)
    near = np.concatenate([np.arange(cols - LANES, cols), ring, np.arange(LANES)])
    edge_taps = taps(ring[None, :] - near[:, None], 0)
    tile = (rows, cols)
    y0, root, r0, early = call(
        functools.partial(first_kernel, n_ty),
        [(tall, wide), tile, tile, (16, LANES)],
        s,
        w,
        s_above,
        s_below,
        row_taps,
        col_taps,
        edge_taps,
        scratch=[pltpu.VMEM((tall, wide), F32)],
        flops=5 * 2 * tall * wide * (2 * LANES + 4 * LANES),
        name="first",
    )
    inside = np.arange(rows)
    own_taps = taps(inside[:, None] - inside[None, :], 0)
    border = np.concatenate([inside[:HALF], inside[rows - HALF :]])
    outside = np.concatenate([np.arange(-HALF, 0), np.arange(rows, rows + HALF)])
    halo_taps = taps(border[:, None] - outside[None, :], 0)
    b0, inner, part, sums = call(
        second_kernel,
        [tile, (rows - 2 * HALF, cols), (rows, wide), (24, LANES)],
        w,
        y0,
        root,
        r0,
        early,
        own_taps,
        col_taps,
        flops=5 * 2 * rows * wide * 3 * LANES,
        name="second",
    )
    b1, moments = call(
        functools.partial(third_kernel, n_ty),
        [tile, (devices, LANES)],
        w_above,
        w_below,
        y0,
        root,
        r0,
        b0,
        part,
        inner,
        sums,
        halo_taps,
        col_taps,
        scratch=[pltpu.VMEM((2 * HALF, wide), F32)],
        flops=5 * 2 * rows * wide * 3 * LANES,
        name="third",
    )
    moments = lax.all_to_all(
        moments.reshape(devices, 1, LANES), TY_TX, split_axis=0, concat_axis=0, tiled=True
    ).reshape(devices, LANES)
    return tuple(
        call(
            final_kernel,
            [tile, tile],
            moments,
            r0,
            b0,
            b1,
            outs=[HBM, HBM],
            scratch=[
                pltpu.VMEM(tile, F32),
                pltpu.VMEM(tile, F32),
                pltpu.SemaphoreType.DMA((CHUNKS, 2)),
            ],
            name="combine",
        )
    )


def solution(mesh):
    split = Mesh(mesh.devices.reshape(mesh.shape["ty"], 4, 4, 2), ("ty", "tx_0", "tx_1", "tx_2"))
    in_specs = (P(TY_TX, None, None), P(TY_TX, None, None), P(TY_TX, None), P(TY_TX), P("ty", TX))
    out_specs = (P("ty", TX), P("ty", TX))
    return jax.shard_map(
        shards, mesh=split, in_specs=in_specs, out_specs=out_specs, check_vma=False
    )
```

```python
import functools

import jax
import jax.numpy as jnp
import numpy as np
from jax import lax
from jax.experimental import pallas as pl
from jax.experimental.pallas import tpu as pltpu
from jax.sharding import Mesh
from jax.sharding import PartitionSpec as P

HALF = 32
LANES = 128
SLOTS = 2
GROUPS = 2
CHUNKS = 4
TY_TX = ("ty", "tx_0", "tx_1", "tx_2")
TX = ("tx_0", "tx_1", "tx_2")
F32 = jnp.float32
BF16 = jnp.bfloat16


def taps(offset, axis):
    def raw(d):
        scaled = np.abs(d) / (HALF + 1.0)
        return np.where(np.abs(d) <= HALF, (1.0 - scaled) ** 4 * (1.0 + 4.0 * scaled), 0.0)

    values = raw(offset) / raw(np.arange(-HALF, HALF + 1)).sum()
    head = values.astype(BF16)
    tail = (values - head.astype(np.float64)).astype(BF16)
    return jnp.asarray(np.concatenate([head, tail], axis=axis))


def split3(x):
    head = x.astype(BF16)
    rest = x - head.astype(F32)
    mid = rest.astype(BF16)
    return head, mid, (rest - mid.astype(F32)).astype(BF16)


def mm(a, b):
    return jnp.dot(a, b, preferred_element_type=F32)


def pick(select, x):
    head, mid, tail = split3(x)
    return mm(select, tail) + mm(select, mid) + mm(select, head)


def taps_times(taps_ref, x):
    rows = taps_ref.shape[0] // 2
    xh, xm, xl = split3(x)
    low = mm(taps_ref[:rows, :], xl)
    mid = mm(taps_ref[...], xm)
    high = mm(taps_ref[...], xh)
    return low + mid[rows:] + high[rows:] + mid[:rows] + high[:rows]


def times_taps(pieces, taps_ref):
    xh, xm, xl = pieces
    depth = taps_ref.shape[0] // 2
    head, tail = taps_ref[:depth, :], taps_ref[depth:, :]
    return mm(xl, head) + mm(xm, tail) + mm(xh, tail) + mm(xm, head) + mm(xh, head)


def spans(wide):
    cols = wide - LANES
    return [slice(c, c + 2 * LANES) for c in range(0, cols, 2 * LANES)] + [slice(cols, wide)]


def iota(shape, dim):
    return lax.broadcasted_iota(jnp.int32, shape, dim)


def pack_kernel(
    n_tx, parts, length, tile_hbm, row_hbm, sums_hbm, weights_hbm, out_hbm,
    tile_ref, row_ref, sums_ref, weights_ref, split_ref, out_ref, in_sem, out_sem
):
    fetches = [
        pltpu.make_async_copy(src, dst, in_sem.at[i])
        for i, (src, dst) in enumerate(
            (
                (tile_hbm, tile_ref),
                (row_hbm, row_ref),
                (sums_hbm, sums_ref),
                (weights_hbm, weights_ref),
            )
        )
    ]
    for fetch in fetches:
        fetch.start()
    fetches[0].wait()
    fetches[1].wait()
    count = tile_ref.shape[1]
    devices = out_ref.shape[0] // length
    group = devices // GROUPS
    tile = tile_ref[...]
    t = iota((devices, count), 0)
    same = tile == t
    earlier = iota((count, count), 0) < iota((count, count), 1)
    before = mm(same.astype(F32).astype(BF16), earlier.astype(F32).astype(BF16))
    rank = jnp.sum(jnp.where(same, before, 0.0), axis=0, keepdims=True)
    column = lax.rem(t, n_tx)
    from_left = (tile + 1 == t) & (column != 0)
    from_right = (tile - 1 == t) & (column != n_tx - 1)

    def onehot(mask, k):
        return jnp.where(mask & (rank == float(k)), 1.0, 0.0)

    own = [onehot(same, k) for k in range(SLOTS)]
    left = [onehot(from_left, k) for k in range(SLOTS)]
    right = [
        jnp.concatenate([onehot(from_right, k), own[k]], axis=1) for k in range(SLOTS)
    ]

    def of_group(masks, g):
        part = slice(g * group, (g + 1) * group)
        return jnp.concatenate([m[part] for m in masks], axis=0).astype(BF16)

    lane = iota((count, LANES), 1)
    number = jnp.transpose(jnp.broadcast_to(row_ref[...].astype(F32) + 1.0, (count, count)))
    for which, ref in enumerate((sums_ref, weights_ref)):
        fetches[2 + which].wait()
        for c in range(parts):
            at = slice((which * parts + c) * LANES, (which * parts + c + 1) * LANES)
            for i, piece in enumerate(split3(ref[pl.ds(c, count, stride=parts), :])):
                split_ref[i, :, at] = piece

    last = parts - 1
    s_last = sums_ref[pl.ds(last, count, stride=parts), :]
    w_last = pltpu.roll(weights_ref[pl.ds(last, count, stride=parts), :], 64, 1)
    s_first = sums_ref[pl.ds(0, count, stride=parts), :]
    w_first = pltpu.roll(weights_ref[pl.ds(0, count, stride=parts), :], 64, 1)
    left_rows = jnp.where(
        lane >= 64, s_last, jnp.where(lane >= 32, w_last, jnp.where(lane == 0, number, 0.0))
    )
    right_rows = jnp.where(
        lane < 64, s_first, jnp.where(lane < 96, w_first, jnp.where(lane == 96, number, 0.0))
    )
    own_rows = jnp.where(lane == 97, number, 0.0)
    both_rows = jnp.concatenate([right_rows, own_rows], axis=0)

    base = 2 * SLOTS * parts
    sends = []
    for g in range(GROUPS):
        first = g * group * length
        own_all = of_group(own, g)
        for c in range(0, 2 * parts, 2):
            at = slice(c * LANES, (c + 2) * LANES)
            y = (
                mm(own_all, split_ref[2, :, at])
                + mm(own_all, split_ref[1, :, at])
                + mm(own_all, split_ref[0, :, at])
            )
            which, chunk = divmod(c, parts)
            for k in range(SLOTS):
                for i in range(2):
                    to = first + (which * SLOTS + k) * parts + chunk + i
                    out_ref[pl.ds(to, group, stride=length), :] = y[
                        k * group : (k + 1) * group, i * LANES : (i + 1) * LANES
                    ]
        to_left = pick(of_group(left, g), left_rows)
        to_right = pick(of_group(right, g), both_rows)
        for k in range(SLOTS):
            part = slice(k * group, (k + 1) * group)
            out_ref[pl.ds(first + base + k, group, stride=length), :] = to_left[part]
            out_ref[pl.ds(first + base + SLOTS + k, group, stride=length), :] = to_right[part]
        span = pl.ds(first, group * length)
        send = pltpu.make_async_copy(out_ref.at[span], out_hbm.at[span], out_sem.at[g])
        send.start()
        sends.append(send)
    for send in sends:
        send.wait()


def slot_rows(got_ref, length, at, devices):
    return got_ref[pl.ds(at, devices, stride=length), :]


def gather_tile(got_ref, parts, length, which, select, dst, extra):
    devices = got_ref.shape[0] // length
    for c in range(0, parts, 2):
        x = jnp.concatenate(
            [
                jnp.concatenate(
                    [
                        slot_rows(got_ref, length, (which * SLOTS + k) * parts + c + i, devices)
                        for i in range(2)
                    ],
                    axis=1,
                )
                for k in range(SLOTS)
            ],
            axis=0,
        )
        at = slice(c * LANES, (c + 2) * LANES)
        y = pick(select, x)
        dst[:, at] = y if extra is None else y + extra[:, at]


def sums_kernel(parts, length, got_ref, s_ref, up_ref, down_ref, select_ref, strip_ref):
    rows, wide = s_ref.shape
    cols = wide - LANES
    devices = got_ref.shape[0] // length
    base = 2 * SLOTS * parts
    from_left = [slot_rows(got_ref, length, base + k, devices) for k in range(SLOTS)]
    from_right = [slot_rows(got_ref, length, base + SLOTS + k, devices) for k in range(SLOTS)]
    left_t = [jnp.transpose(x) for x in from_left]
    right_t = [jnp.transpose(x) for x in from_right]
    wanted = (iota((rows, devices), 0) + 1).astype(F32)

    def chooser(lists, at):
        return jnp.concatenate(
            [jnp.where(x[at : at + 1, :] == wanted, 1.0, 0.0) for x in lists], axis=1
        ).astype(BF16)

    own = chooser(right_t, 97)
    select_ref[...] = own
    gather_tile(got_ref, parts, length, 0, own, s_ref, None)
    left = pick(chooser(left_t, 0), jnp.concatenate(from_left, axis=0))
    right = pick(chooser(right_t, 96), jnp.concatenate(from_right, axis=0))
    lane = iota((rows, LANES), 1)
    s_ref[:, cols:] = jnp.where(lane < 64, right, left)
    strip_ref[...] = jnp.where(lane < 64, pltpu.roll(right, 64, 1), pltpu.roll(left, 64, 1))
    up_ref[...] = s_ref[: 2 * HALF, :]
    down_ref[...] = s_ref[rows - 2 * HALF :, :]


def weights_kernel(
    parts, length, n_tx, got_ref, prior_ref, prior_halo_ref, select_ref, strip_ref,
    w_ref, up_ref, down_ref
):
    rows, wide = w_ref.shape
    cols = wide - LANES
    gather_tile(got_ref, parts, length, 1, select_ref[...], w_ref, prior_ref)
    lane = iota((rows, LANES), 1)
    column = lax.axis_index(TX)
    has_left = jnp.where(column > 0, 1.0, 0.0)
    has_right = jnp.where(column < n_tx - 1, 1.0, 0.0)
    prior_halo = prior_halo_ref[...]
    strip = strip_ref[...]
    w_ref[:, cols:] = jnp.where(
        lane < HALF,
        prior_halo * has_right + strip,
        jnp.where(lane >= LANES - HALF, prior_halo * has_left + strip, 0.0),
    )
    up_ref[...] = w_ref[:HALF, :]
    down_ref[...] = w_ref[rows - HALF :, :]


def along_columns(pieces, taps_ref):
    height, wide = pieces[0].shape
    cols = wide - LANES

    def stacked(x):
        first = jnp.concatenate([x[:, cols:], x[:, : 3 * LANES]], axis=1)
        rest = [
            x[:, (c - 1) * LANES : (c + 3) * LANES] for c in range(2, cols // LANES, 2)
        ]
        return jnp.concatenate([first] + rest, axis=0)

    half = [stacked(x) for x in pieces]
    out = []
    for r in range(0, half[0].shape[0], 2 * height):
        y = times_taps([x[r : r + 2 * height] for x in half], taps_ref)
        out += [y[:height], y[height:]]
    return out


def all_columns(mid, y0_ref, at, col_ref, edge_ref):
    wide = mid.shape[1]
    cols = wide - LANES
    pieces = split3(mid)
    for c, y in enumerate(along_columns(pieces, col_ref)):
        y0_ref[at, 2 * c * LANES : 2 * (c + 1) * LANES] = y
    near = [jnp.concatenate([x[:, cols - LANES :], x[:, :LANES]], axis=1) for x in pieces]
    y0_ref[at, cols:] = times_taps(near, edge_ref)


def early_kernel(
    s_ref,
    w_ref,
    own_ref,
    col_ref,
    edge_ref,
    part_ref,
    deep_ref,
    root_ref,
    r0_ref,
    sums_ref,
    mid_ref,
):
    rows, wide = s_ref.shape
    cols = wide - LANES
    edge = 4 * HALF
    for at in spans(wide):
        mid = taps_times(own_ref, s_ref[:, at])
        part_ref[:, at] = mid[:edge]
        mid_ref[:, at] = mid[edge:]
    all_columns(mid_ref[...], deep_ref, slice(None), col_ref, edge_ref)
    total_rr = total_rb = jnp.zeros((8, cols), F32)
    for r in range(0, rows, 8):
        at = slice(r, r + 8)
        root = jnp.sqrt(w_ref[at, :cols])
        s = s_ref[at, :cols]
        r0 = s / root
        root_ref[at, :] = root
        r0_ref[at, :] = r0
        total_rr += r0 * r0
        if HALF <= r < rows - HALF:
            total_rb += s * deep_ref[r - HALF : r - HALF + 8, :cols]
    sums_ref[0:8, :] = folded(total_rr)
    sums_ref[8:16, :] = folded(total_rb)


def first_kernel(
    n_ty,
    s_ref,
    above_ref,
    below_ref,
    part_ref,
    deep_ref,
    early_ref,
    halo_ref,
    col_ref,
    edge_ref,
    y0_ref,
    sums_ref,
    mid_ref,
    border_ref,
):
    rows, wide = s_ref.shape
    cols = wide - LANES
    row_at = lax.axis_index("ty")
    has_above = jnp.where(row_at > 0, 1.0, 0.0)
    has_below = jnp.where(row_at < n_ty - 1, 1.0, 0.0)
    for at in spans(wide):
        halo = jnp.concatenate([above_ref[:, at] * has_above, below_ref[:, at] * has_below], axis=0)
        mid_ref[:, at] = part_ref[:, at] + taps_times(halo_ref, halo)
    all_columns(mid_ref[...], border_ref, slice(None), col_ref, edge_ref)
    two = 2 * HALF
    y0_ref[:two, :] = border_ref[:two, :]
    y0_ref[two:rows, :] = deep_ref[...]
    y0_ref[rows:, :] = border_ref[two:, :]
    top = s_ref[:HALF, :cols] * border_ref[HALF:two, :cols]
    bottom = s_ref[rows - HALF :, :cols] * border_ref[two : two + HALF, :cols]
    sums_ref[0:8, :] = early_ref[0:8, :]
    sums_ref[8:16, :] = early_ref[8:16, :] + folded(top) + folded(bottom)


def folded(total):
    rows, cols = total.shape
    total = sum(total[r : r + 8] for r in range(0, rows, 8))
    return sum(total[:, c : c + LANES] for c in range(0, cols, LANES))


def whole(total):
    return jnp.sum(jnp.sum(total, axis=0, keepdims=True), axis=1, keepdims=True)


def centred(r0, b0, b1, c):
    v, q = b0 - c * r0, b1 - c * b0
    return v * q, v * b0 + r0 * q


def second_kernel(
    w_ref,
    y0_ref,
    root_ref,
    r0_ref,
    first_ref,
    own_ref,
    col_ref,
    b0_ref,
    inner_ref,
    mid_ref,
    sums_ref,
):
    rows, wide = w_ref.shape
    cols = wide - LANES
    tile = slice(HALF, HALF + rows)
    deep = slice(HALF, rows - HALF)
    m0, n1 = whole(first_ref[0:8, :]), whole(first_ref[8:16, :])
    c0 = n1 / jnp.where(m0 > 0.0, m0, 1.0)
    for at in spans(wide):
        mid_ref[:, at] = taps_times(own_ref, w_ref[:, at] * y0_ref[tile, at])
    total_vv = total_rv = total_vq = total_mix = jnp.zeros((8, LANES), F32)
    for c, y1 in enumerate(along_columns(split3(mid_ref[deep, :]), col_ref)):
        at = slice(2 * c * LANES, 2 * (c + 1) * LANES)
        r0 = r0_ref[:, at]
        b0 = root_ref[:, at] * y0_ref[tile, at]
        b0_ref[:, at] = b0
        v = b0 - c0 * r0
        total_vv += folded(v * v)
        total_rv += folded(r0 * v)
        b1 = root_ref[deep, at] * y1
        inner_ref[:, at] = b1
        vq, mix = centred(r0[deep], b0[deep], b1, c0)
        total_vq += folded(vq)
        total_mix += folded(mix)
    lane = iota((8, LANES), 1)
    known = jnp.zeros((8, LANES), F32)
    for i, value in enumerate((m0, n1, c0, whole(total_vv), whole(total_rv))):
        known = jnp.where(lane == i, value, known)
    sums_ref[0:8, :] = known
    sums_ref[8:16, :] = total_vq
    sums_ref[16:24, :] = total_mix


def third_kernel(
    n_ty,
    above_ref,
    below_ref,
    y0_ref,
    root_ref,
    r0_ref,
    b0_ref,
    part_ref,
    inner_ref,
    sums_ref,
    halo_ref,
    col_ref,
    b1_ref,
    moments_ref,
    mid_ref,
):
    rows, wide = part_ref.shape
    cols = wide - LANES
    row_at = lax.axis_index("ty")
    has_above = jnp.where(row_at > 0, 1.0, 0.0)
    has_below = jnp.where(row_at < n_ty - 1, 1.0, 0.0)
    top, bottom = slice(0, HALF), slice(rows - HALF, rows)
    b1_ref[HALF : rows - HALF, :] = inner_ref[...]
    known = sums_ref[0:1, :]
    lane = iota(known.shape, 1)
    c0 = jnp.sum(jnp.where(lane == 2, known, 0.0), axis=1, keepdims=True)

    def border(ref, at):
        return jnp.concatenate([ref[top, at], ref[bottom, at]], axis=0)

    for at in spans(wide):
        z = jnp.concatenate(
            [
                above_ref[:, at] * has_above * y0_ref[:HALF, at],
                below_ref[:, at] * has_below * y0_ref[rows + HALF :, at],
            ],
            axis=0,
        )
        mid_ref[:, at] = border(part_ref, at) + taps_times(halo_ref, z)
    total_vq, total_mix = sums_ref[8:16, :], sums_ref[16:24, :]
    for c, y1 in enumerate(along_columns(split3(mid_ref[...]), col_ref)):
        at = slice(2 * c * LANES, 2 * (c + 1) * LANES)
        b1 = border(root_ref, at) * y1
        b1_ref[top, at] = b1[:HALF]
        b1_ref[bottom, at] = b1[HALF:]
        vq, mix = centred(border(r0_ref, at), border(b0_ref, at), b1, c0)
        total_vq += folded(vq)
        total_mix += folded(mix)
    known = jnp.where(lane == 5, whole(total_vq), known)
    known = jnp.where(lane == 6, whole(total_mix), known)
    moments_ref[...] = jnp.broadcast_to(known, moments_ref.shape)


def final_kernel(moments_ref, r0_ref, b0_ref, b1_ref, x_hbm, r_hbm, x_ref, r_ref, sem):
    parts = jnp.transpose(moments_ref[...])
    m0_at, n1_at, c_at, vv_at, rv_at, vq_at, mix_at = (parts[i : i + 1, :] for i in range(7))

    def total(x):
        return jnp.sum(x, axis=1, keepdims=True)

    m0, n1 = total(m0_at), total(n1_at)
    mu = n1 / m0
    shift = c_at - mu
    vv = total(vv_at + shift * (2.0 * rv_at + shift * m0_at))
    vbv = total(vq_at + shift * (mix_at + shift * n1_at))
    a = m0 / (0.5 * m0 + n1)
    ratio = vv / m0
    beta = a * a * ratio
    step = vv / (0.5 * vv + vbv - a * vv * ratio)
    x_r0 = a + step * beta + step * a * mu
    x_b0 = -step * a
    r_r0 = a * mu - step * (0.5 * a * mu + 0.5 * beta)
    r_b0 = -a - step * (a * mu - 0.5 * a + beta)
    r_b1 = step * a
    sends = []
    step_rows = r0_ref.shape[0] // CHUNKS
    for c in range(CHUNKS):
        at = slice(c * step_rows, (c + 1) * step_rows)
        r0 = r0_ref[at, :]
        b0 = b0_ref[at, :]
        x_ref[at, :] = x_r0 * r0 + x_b0 * b0
        r_ref[at, :] = r_r0 * r0 + r_b0 * b0 + r_b1 * b1_ref[at, :]
        for i, (src, dst) in enumerate(((x_ref, x_hbm), (r_ref, r_hbm))):
            send = pltpu.make_async_copy(src.at[at], dst.at[at], sem.at[c, i])
            send.start()
            sends.append(send)
    for send in sends:
        send.wait()


VMEM = pl.BlockSpec(memory_space=pltpu.VMEM)
ANY = pl.BlockSpec(memory_space=pl.ANY)
HBM = pl.BlockSpec(memory_space=pltpu.HBM)


def call(kernel, shapes, *args, ins=None, outs=None, scratch=(), name, limit=24, flops=0):
    moved = sum(int(np.prod(x.shape)) * x.dtype.itemsize for x in args)
    return pl.pallas_call(
        kernel,
        out_shape=[
            jax.ShapeDtypeStruct(s, F32) if isinstance(s, tuple) else s for s in shapes
        ],
        in_specs=ins or [VMEM] * len(args),
        out_specs=outs or [VMEM] * len(shapes),
        scratch_shapes=list(scratch),
        compiler_params=pltpu.CompilerParams(vmem_limit_bytes=limit << 20),
        cost_estimate=pl.CostEstimate(flops=flops, bytes_accessed=moved, transcendentals=0),
        name=name,
    )(*args)


def neighbours(axes, step):
    count = int(np.prod([lax.axis_size(a) for a in axes]))
    return [(i, (i + step) % count) for i in range(count)]


def shards(block_sums, block_weights, block_tile, block_row, prior_weight):
    devices = lax.axis_size(TY_TX)
    n_tx = lax.axis_size(TX)
    blocks, _, cols = block_sums.shape
    rows = prior_weight.shape[0]
    parts = cols // LANES
    length = 2 * SLOTS * parts + 2 * SLOTS
    wide = cols + LANES

    prior_right = lax.ppermute(prior_weight[:, :LANES], TX, neighbours(TX, -1))
    prior_left = lax.ppermute(prior_weight[:, cols - LANES :], TX, neighbours(TX, 1))
    lane = jnp.arange(LANES)[None, :]
    prior_halo = jnp.where(lane < HALF, prior_right, jnp.where(lane >= LANES - HALF, prior_left, 0.0))

    (message,) = call(
        functools.partial(pack_kernel, n_tx, parts, length),
        [(devices * length, LANES)],
        block_tile.reshape(1, blocks),
        block_row.reshape(1, blocks),
        block_sums.reshape(blocks * parts, LANES),
        block_weights.reshape(blocks * parts, LANES),
        ins=[HBM] * 4,
        outs=[HBM],
        scratch=[
            pltpu.VMEM((1, blocks), jnp.int32),
            pltpu.VMEM((1, blocks), jnp.int32),
            pltpu.VMEM((blocks * parts, LANES), F32),
            pltpu.VMEM((blocks * parts, LANES), F32),
            pltpu.VMEM((3, blocks, 2 * cols), BF16),
            pltpu.VMEM((devices * length, LANES), F32),
            pltpu.SemaphoreType.DMA((4,)),
            pltpu.SemaphoreType.DMA((GROUPS,)),
        ],
        name="pack",
        limit=63,
    )
    got = lax.all_to_all(
        message.reshape(devices, 1, length * LANES), TY_TX, split_axis=0, concat_axis=0, tiled=True
    ).reshape(devices * length, LANES)
    s_slab, w_slab = (2 * HALF, wide), (HALF, wide)
    s, s_up, s_down, chosen, strip = call(
        functools.partial(sums_kernel, parts, length),
        [
            (rows, wide),
            s_slab,
            s_slab,
            jax.ShapeDtypeStruct((rows, SLOTS * devices), BF16),
            (rows, LANES),
        ],
        got,
        flops=3 * 2 * rows * wide * SLOTS * devices,
        name="sums",
    )
    w, w_up, w_down = call(
        functools.partial(weights_kernel, parts, length, n_tx),
        [(rows, wide), w_slab, w_slab],
        got,
        prior_weight,
        prior_halo,
        chosen,
        strip,
        flops=3 * 2 * rows * wide * SLOTS * devices,
        name="weights",
    )
    n_ty = lax.axis_size("ty")
    downward, upward = neighbours(("ty",), 1), neighbours(("ty",), -1)
    s_above, s_below = lax.ppermute(s_down, "ty", downward), lax.ppermute(s_up, "ty", upward)
    w_above, w_below = lax.ppermute(w_down, "ty", downward), lax.ppermute(w_up, "ty", upward)

    tall = rows + 2 * HALF
    col_taps = taps(np.arange(2 * LANES)[None, :] - np.arange(4 * LANES)[:, None] + LANES, 0)
    ring = np.where(np.arange(LANES) < 64, cols, -LANES) + np.arange(LANES)
    near = np.concatenate([np.arange(cols - LANES, cols), ring, np.arange(LANES)])
    edge_taps = taps(ring[None, :] - near[:, None], 0)
    tile = (rows, cols)
    inside = np.arange(rows)
    border_rows = np.concatenate(
        [np.arange(-HALF, HALF), np.arange(rows - HALF, rows + HALF)]
    )
    early_rows = np.concatenate([border_rows, inside[HALF : rows - HALF]])
    far_rows = np.concatenate([np.arange(-2 * HALF, 0), np.arange(rows, rows + 2 * HALF)])
    early_taps = taps(early_rows[:, None] - inside[None, :], 0)
    first_taps = taps(border_rows[:, None] - far_rows[None, :], 0)
    part, deep, root, r0, early = call(
        early_kernel,
        [(4 * HALF, wide), (rows - 2 * HALF, wide), tile, tile, (16, LANES)],
        s,
        w,
        early_taps,
        col_taps,
        edge_taps,
        scratch=[pltpu.VMEM((rows - 2 * HALF, wide), F32)],
        flops=5 * 2 * tall * wide * 3 * LANES,
        name="early",
    )
    y0, early = call(
        functools.partial(first_kernel, n_ty),
        [(tall, wide), (16, LANES)],
        s,
        s_above,
        s_below,
        part,
        deep,
        early,
        first_taps,
        col_taps,
        edge_taps,
        scratch=[pltpu.VMEM((4 * HALF, wide), F32), pltpu.VMEM((4 * HALF, wide), F32)],
        flops=5 * 2 * rows * wide * 6 * LANES,
        name="first",
    )
    own_taps = taps(inside[:, None] - inside[None, :], 0)
    border = np.concatenate([inside[:HALF], inside[rows - HALF :]])
    outside = np.concatenate([np.arange(-HALF, 0), np.arange(rows, rows + HALF)])
    halo_taps = taps(border[:, None] - outside[None, :], 0)
    b0, inner, part, sums = call(
        second_kernel,
        [tile, (rows - 2 * HALF, cols), (rows, wide), (24, LANES)],
        w,
        y0,
        root,
        r0,
        early,
        own_taps,
        col_taps,
        flops=5 * 2 * rows * wide * 3 * LANES,
        name="second",
    )
    b1, moments = call(
        functools.partial(third_kernel, n_ty),
        [tile, (devices, LANES)],
        w_above,
        w_below,
        y0,
        root,
        r0,
        b0,
        part,
        inner,
        sums,
        halo_taps,
        col_taps,
        scratch=[pltpu.VMEM((2 * HALF, wide), F32)],
        flops=5 * 2 * rows * wide * 3 * LANES,
        name="third",
    )
    moments = lax.all_to_all(
        moments.reshape(devices, 1, LANES), TY_TX, split_axis=0, concat_axis=0, tiled=True
    ).reshape(devices, LANES)
    return tuple(
        call(
            final_kernel,
            [tile, tile],
            moments,
            r0,
            b0,
            b1,
            outs=[HBM, HBM],
            scratch=[
                pltpu.VMEM(tile, F32),
                pltpu.VMEM(tile, F32),
                pltpu.SemaphoreType.DMA((CHUNKS, 2)),
            ],
            name="combine",
        )
    )


def solution(mesh):
    split = Mesh(mesh.devices.reshape(mesh.shape["ty"], 4, 4, 2), ("ty", "tx_0", "tx_1", "tx_2"))
    in_specs = (P(TY_TX, None, None), P(TY_TX, None, None), P(TY_TX, None), P(TY_TX), P("ty", TX))
    out_specs = (P("ty", TX), P("ty", TX))
    return jax.shard_map(
        shards, mesh=split, in_specs=in_specs, out_specs=out_specs, check_vma=False
    )
```

```python
import functools

import jax
import jax.numpy as jnp
import numpy as np
from jax import lax
from jax.experimental import pallas as pl
from jax.experimental.pallas import tpu as pltpu
from jax.sharding import Mesh
from jax.sharding import PartitionSpec as P

HALF = 32
LANES = 128
SLOTS = 2
GROUPS = 2
CHUNKS = 4
TY_TX = ("ty", "tx_0", "tx_1", "tx_2")
TX = ("tx_0", "tx_1", "tx_2")
F32 = jnp.float32
BF16 = jnp.bfloat16


def taps(offset, axis):
    def raw(d):
        scaled = np.abs(d) / (HALF + 1.0)
        return np.where(np.abs(d) <= HALF, (1.0 - scaled) ** 4 * (1.0 + 4.0 * scaled), 0.0)

    values = raw(offset) / raw(np.arange(-HALF, HALF + 1)).sum()
    head = values.astype(BF16)
    tail = (values - head.astype(np.float64)).astype(BF16)
    return jnp.asarray(np.concatenate([head, tail], axis=axis))


def split3(x):
    head = x.astype(BF16)
    rest = x - head.astype(F32)
    mid = rest.astype(BF16)
    return head, mid, (rest - mid.astype(F32)).astype(BF16)


def mm(a, b):
    return jnp.dot(a, b, preferred_element_type=F32)


def pick(select, x):
    head, mid, tail = split3(x)
    return mm(select, tail) + mm(select, mid) + mm(select, head)


def taps_times(taps_ref, x):
    rows = taps_ref.shape[0] // 2
    xh, xm, xl = split3(x)
    low = mm(taps_ref[:rows, :], xl)
    mid = mm(taps_ref[...], xm)
    high = mm(taps_ref[...], xh)
    return low + mid[rows:] + high[rows:] + mid[:rows] + high[:rows]


def times_taps(pieces, taps_ref):
    xh, xm, xl = pieces
    depth = taps_ref.shape[0] // 2
    head, tail = taps_ref[:depth, :], taps_ref[depth:, :]
    return mm(xl, head) + mm(xm, tail) + mm(xh, tail) + mm(xm, head) + mm(xh, head)


def spans(wide):
    cols = wide - LANES
    return [slice(c, c + 2 * LANES) for c in range(0, cols, 2 * LANES)] + [slice(cols, wide)]


def iota(shape, dim):
    return lax.broadcasted_iota(jnp.int32, shape, dim)


def pack_kernel(
    n_tx, parts, length, tile_hbm, row_hbm, sums_hbm, weights_hbm, out_hbm,
    tile_ref, row_ref, sums_ref, weights_ref, split_ref, out_ref, in_sem, out_sem
):
    fetches = [
        pltpu.make_async_copy(src, dst, in_sem.at[i])
        for i, (src, dst) in enumerate(
            (
                (tile_hbm, tile_ref),
                (row_hbm, row_ref),
                (sums_hbm, sums_ref),
                (weights_hbm, weights_ref),
            )
        )
    ]
    for fetch in fetches:
        fetch.start()
    fetches[0].wait()
    fetches[1].wait()
    count = tile_ref.shape[1]
    devices = out_ref.shape[0] // length
    group = devices // GROUPS
    tile = tile_ref[...]
    t = iota((devices, count), 0)
    same = tile == t
    earlier = iota((count, count), 0) < iota((count, count), 1)
    before = mm(same.astype(F32).astype(BF16), earlier.astype(F32).astype(BF16))
    rank = jnp.sum(jnp.where(same, before, 0.0), axis=0, keepdims=True)
    column = lax.rem(t, n_tx)
    from_left = (tile + 1 == t) & (column != 0)
    from_right = (tile - 1 == t) & (column != n_tx - 1)

    def onehot(mask, k):
        return jnp.where(mask & (rank == float(k)), 1.0, 0.0)

    own = [onehot(same, k) for k in range(SLOTS)]
    left = [onehot(from_left, k) for k in range(SLOTS)]
    right = [
        jnp.concatenate([onehot(from_right, k), own[k]], axis=1) for k in range(SLOTS)
    ]

    def of_group(masks, g):
        part = slice(g * group, (g + 1) * group)
        return jnp.concatenate([m[part] for m in masks], axis=0).astype(BF16)

    lane = iota((count, LANES), 1)
    number = jnp.transpose(jnp.broadcast_to(row_ref[...].astype(F32) + 1.0, (count, count)))
    for which, ref in enumerate((sums_ref, weights_ref)):
        fetches[2 + which].wait()
        for c in range(parts):
            at = slice((which * parts + c) * LANES, (which * parts + c + 1) * LANES)
            for i, piece in enumerate(split3(ref[pl.ds(c, count, stride=parts), :])):
                split_ref[i, :, at] = piece

    last = parts - 1
    s_last = sums_ref[pl.ds(last, count, stride=parts), :]
    w_last = pltpu.roll(weights_ref[pl.ds(last, count, stride=parts), :], 64, 1)
    s_first = sums_ref[pl.ds(0, count, stride=parts), :]
    w_first = pltpu.roll(weights_ref[pl.ds(0, count, stride=parts), :], 64, 1)
    left_rows = jnp.where(
        lane >= 64, s_last, jnp.where(lane >= 32, w_last, jnp.where(lane == 0, number, 0.0))
    )
    right_rows = jnp.where(
        lane < 64, s_first, jnp.where(lane < 96, w_first, jnp.where(lane == 96, number, 0.0))
    )
    own_rows = jnp.where(lane == 97, number, 0.0)
    both_rows = jnp.concatenate([right_rows, own_rows], axis=0)

    base = 2 * SLOTS * parts
    sends = []
    for g in range(GROUPS):
        first = g * group * length
        own_all = of_group(own, g)
        for c in range(0, 2 * parts, 2):
            at = slice(c * LANES, (c + 2) * LANES)
            y = (
                mm(own_all, split_ref[2, :, at])
                + mm(own_all, split_ref[1, :, at])
                + mm(own_all, split_ref[0, :, at])
            )
            which, chunk = divmod(c, parts)
            for k in range(SLOTS):
                for i in range(2):
                    to = first + (which * SLOTS + k) * parts + chunk + i
                    out_ref[pl.ds(to, group, stride=length), :] = y[
                        k * group : (k + 1) * group, i * LANES : (i + 1) * LANES
                    ]
        to_left = pick(of_group(left, g), left_rows)
        to_right = pick(of_group(right, g), both_rows)
        for k in range(SLOTS):
            part = slice(k * group, (k + 1) * group)
            out_ref[pl.ds(first + base + k, group, stride=length), :] = to_left[part]
            out_ref[pl.ds(first + base + SLOTS + k, group, stride=length), :] = to_right[part]
        span = pl.ds(first, group * length)
        send = pltpu.make_async_copy(out_ref.at[span], out_hbm.at[span], out_sem.at[g])
        send.start()
        sends.append(send)
    for send in sends:
        send.wait()


def slot_rows(got_ref, length, at, devices):
    return got_ref[pl.ds(at, devices, stride=length), :]


def odd_row():
    return lax.rem(lax.axis_index("ty"), 2)


def to_partners(ref, near_ref, next_ref):
    rows, count = ref.shape[0], near_ref.shape[0]
    bottom = (rows - count) * (1 - odd_row())
    near_ref[...] = ref[pl.ds(pl.multiple_of(bottom, 8), count), :]
    next_ref[...] = ref[pl.ds(pl.multiple_of(rows - count - bottom, 8), count), :]


def from_partners(n_ty, near_ref, next_ref, at):
    row_at, odd = lax.axis_index("ty"), odd_row() == 1
    near, far = near_ref[:, at], next_ref[:, at]
    above = jnp.where(odd, near, far) * jnp.where(row_at > 0, 1.0, 0.0)
    below = jnp.where(odd, far, near) * jnp.where(row_at < n_ty - 1, 1.0, 0.0)
    return above, below


def gather_tile(got_ref, parts, length, which, select, dst, extra):
    devices = got_ref.shape[0] // length
    for c in range(0, parts, 2):
        x = jnp.concatenate(
            [
                jnp.concatenate(
                    [
                        slot_rows(got_ref, length, (which * SLOTS + k) * parts + c + i, devices)
                        for i in range(2)
                    ],
                    axis=1,
                )
                for k in range(SLOTS)
            ],
            axis=0,
        )
        at = slice(c * LANES, (c + 2) * LANES)
        y = pick(select, x)
        dst[:, at] = y if extra is None else y + extra[:, at]


def sums_kernel(parts, length, got_ref, s_ref, near_ref, next_ref, select_ref, strip_ref):
    rows, wide = s_ref.shape
    cols = wide - LANES
    devices = got_ref.shape[0] // length
    base = 2 * SLOTS * parts
    from_left = [slot_rows(got_ref, length, base + k, devices) for k in range(SLOTS)]
    from_right = [slot_rows(got_ref, length, base + SLOTS + k, devices) for k in range(SLOTS)]
    left_t = [jnp.transpose(x) for x in from_left]
    right_t = [jnp.transpose(x) for x in from_right]
    wanted = (iota((rows, devices), 0) + 1).astype(F32)

    def chooser(lists, at):
        return jnp.concatenate(
            [jnp.where(x[at : at + 1, :] == wanted, 1.0, 0.0) for x in lists], axis=1
        ).astype(BF16)

    own = chooser(right_t, 97)
    select_ref[...] = own
    gather_tile(got_ref, parts, length, 0, own, s_ref, None)
    left = pick(chooser(left_t, 0), jnp.concatenate(from_left, axis=0))
    right = pick(chooser(right_t, 96), jnp.concatenate(from_right, axis=0))
    lane = iota((rows, LANES), 1)
    s_ref[:, cols:] = jnp.where(lane < 64, right, left)
    strip_ref[...] = jnp.where(lane < 64, pltpu.roll(right, 64, 1), pltpu.roll(left, 64, 1))
    to_partners(s_ref, near_ref, next_ref)


def weights_kernel(
    parts, length, n_tx, got_ref, prior_ref, prior_halo_ref, select_ref, strip_ref,
    w_ref, near_ref, next_ref
):
    rows, wide = w_ref.shape
    cols = wide - LANES
    gather_tile(got_ref, parts, length, 1, select_ref[...], w_ref, prior_ref)
    lane = iota((rows, LANES), 1)
    column = lax.axis_index(TX)
    has_left = jnp.where(column > 0, 1.0, 0.0)
    has_right = jnp.where(column < n_tx - 1, 1.0, 0.0)
    prior_halo = prior_halo_ref[...]
    strip = strip_ref[...]
    w_ref[:, cols:] = jnp.where(
        lane < HALF,
        prior_halo * has_right + strip,
        jnp.where(lane >= LANES - HALF, prior_halo * has_left + strip, 0.0),
    )
    to_partners(w_ref, near_ref, next_ref)


def along_columns(pieces, taps_ref):
    height, wide = pieces[0].shape
    cols = wide - LANES

    def stacked(x):
        first = jnp.concatenate([x[:, cols:], x[:, : 3 * LANES]], axis=1)
        rest = [
            x[:, (c - 1) * LANES : (c + 3) * LANES] for c in range(2, cols // LANES, 2)
        ]
        return jnp.concatenate([first] + rest, axis=0)

    half = [stacked(x) for x in pieces]
    out = []
    for r in range(0, half[0].shape[0], 2 * height):
        y = times_taps([x[r : r + 2 * height] for x in half], taps_ref)
        out += [y[:height], y[height:]]
    return out


def all_columns(mid, y0_ref, at, col_ref, edge_ref):
    wide = mid.shape[1]
    cols = wide - LANES
    pieces = split3(mid)
    for c, y in enumerate(along_columns(pieces, col_ref)):
        y0_ref[at, 2 * c * LANES : 2 * (c + 1) * LANES] = y
    near = [jnp.concatenate([x[:, cols - LANES :], x[:, :LANES]], axis=1) for x in pieces]
    y0_ref[at, cols:] = times_taps(near, edge_ref)


def early_kernel(
    s_ref,
    w_ref,
    own_ref,
    col_ref,
    edge_ref,
    part_ref,
    deep_ref,
    root_ref,
    r0_ref,
    sums_ref,
    mid_ref,
):
    rows, wide = s_ref.shape
    cols = wide - LANES
    edge = 4 * HALF
    for at in spans(wide):
        mid = taps_times(own_ref, s_ref[:, at])
        part_ref[:, at] = mid[:edge]
        mid_ref[:, at] = mid[edge:]
    all_columns(mid_ref[...], deep_ref, slice(None), col_ref, edge_ref)
    total_rr = total_rb = jnp.zeros((8, cols), F32)
    for r in range(0, rows, 8):
        at = slice(r, r + 8)
        root = jnp.sqrt(w_ref[at, :cols])
        s = s_ref[at, :cols]
        r0 = s / root
        root_ref[at, :] = root
        r0_ref[at, :] = r0
        total_rr += r0 * r0
        if HALF <= r < rows - HALF:
            total_rb += s * deep_ref[r - HALF : r - HALF + 8, :cols]
    sums_ref[0:8, :] = folded(total_rr)
    sums_ref[8:16, :] = folded(total_rb)


def first_kernel(
    n_ty,
    s_ref,
    near_ref,
    next_ref,
    part_ref,
    deep_ref,
    early_ref,
    halo_ref,
    col_ref,
    edge_ref,
    y0_ref,
    sums_ref,
    mid_ref,
    border_ref,
):
    rows, wide = s_ref.shape
    cols = wide - LANES
    for at in spans(wide):
        halo = jnp.concatenate(from_partners(n_ty, near_ref, next_ref, at), axis=0)
        mid_ref[:, at] = part_ref[:, at] + taps_times(halo_ref, halo)
    all_columns(mid_ref[...], border_ref, slice(None), col_ref, edge_ref)
    two = 2 * HALF
    y0_ref[:two, :] = border_ref[:two, :]
    y0_ref[two:rows, :] = deep_ref[...]
    y0_ref[rows:, :] = border_ref[two:, :]
    top = s_ref[:HALF, :cols] * border_ref[HALF:two, :cols]
    bottom = s_ref[rows - HALF :, :cols] * border_ref[two : two + HALF, :cols]
    sums_ref[0:8, :] = early_ref[0:8, :]
    sums_ref[8:16, :] = early_ref[8:16, :] + folded(top) + folded(bottom)


def folded(total):
    rows, cols = total.shape
    total = sum(total[r : r + 8] for r in range(0, rows, 8))
    return sum(total[:, c : c + LANES] for c in range(0, cols, LANES))


def whole(total):
    return jnp.sum(jnp.sum(total, axis=0, keepdims=True), axis=1, keepdims=True)


def centred(r0, b0, b1, c):
    v, q = b0 - c * r0, b1 - c * b0
    return v * q, v * b0 + r0 * q


def second_kernel(
    w_ref,
    y0_ref,
    root_ref,
    r0_ref,
    first_ref,
    own_ref,
    col_ref,
    b0_ref,
    inner_ref,
    mid_ref,
    sums_ref,
):
    rows, wide = w_ref.shape
    cols = wide - LANES
    tile = slice(HALF, HALF + rows)
    deep = slice(HALF, rows - HALF)
    m0, n1 = whole(first_ref[0:8, :]), whole(first_ref[8:16, :])
    c0 = n1 / jnp.where(m0 > 0.0, m0, 1.0)
    for at in spans(wide):
        mid_ref[:, at] = taps_times(own_ref, w_ref[:, at] * y0_ref[tile, at])
    total_vv = total_rv = total_vq = total_mix = jnp.zeros((8, LANES), F32)
    for c, y1 in enumerate(along_columns(split3(mid_ref[deep, :]), col_ref)):
        at = slice(2 * c * LANES, 2 * (c + 1) * LANES)
        r0 = r0_ref[:, at]
        b0 = root_ref[:, at] * y0_ref[tile, at]
        b0_ref[:, at] = b0
        v = b0 - c0 * r0
        total_vv += folded(v * v)
        total_rv += folded(r0 * v)
        b1 = root_ref[deep, at] * y1
        inner_ref[:, at] = b1
        vq, mix = centred(r0[deep], b0[deep], b1, c0)
        total_vq += folded(vq)
        total_mix += folded(mix)
    lane = iota((8, LANES), 1)
    known = jnp.zeros((8, LANES), F32)
    for i, value in enumerate((m0, n1, c0, whole(total_vv), whole(total_rv))):
        known = jnp.where(lane == i, value, known)
    sums_ref[0:8, :] = known
    sums_ref[8:16, :] = total_vq
    sums_ref[16:24, :] = total_mix


def third_kernel(
    n_ty,
    near_ref,
    next_ref,
    y0_ref,
    root_ref,
    r0_ref,
    b0_ref,
    part_ref,
    inner_ref,
    sums_ref,
    halo_ref,
    col_ref,
    b1_ref,
    moments_ref,
    mid_ref,
):
    rows, wide = part_ref.shape
    cols = wide - LANES
    top, bottom = slice(0, HALF), slice(rows - HALF, rows)
    b1_ref[HALF : rows - HALF, :] = inner_ref[...]
    known = sums_ref[0:1, :]
    lane = iota(known.shape, 1)
    c0 = jnp.sum(jnp.where(lane == 2, known, 0.0), axis=1, keepdims=True)

    def border(ref, at):
        return jnp.concatenate([ref[top, at], ref[bottom, at]], axis=0)

    for at in spans(wide):
        above, below = from_partners(n_ty, near_ref, next_ref, at)
        z = jnp.concatenate(
            [above * y0_ref[:HALF, at], below * y0_ref[rows + HALF :, at]], axis=0
        )
        mid_ref[:, at] = border(part_ref, at) + taps_times(halo_ref, z)
    total_vq, total_mix = sums_ref[8:16, :], sums_ref[16:24, :]
    for c, y1 in enumerate(along_columns(split3(mid_ref[...]), col_ref)):
        at = slice(2 * c * LANES, 2 * (c + 1) * LANES)
        b1 = border(root_ref, at) * y1
        b1_ref[top, at] = b1[:HALF]
        b1_ref[bottom, at] = b1[HALF:]
        vq, mix = centred(border(r0_ref, at), border(b0_ref, at), b1, c0)
        total_vq += folded(vq)
        total_mix += folded(mix)
    known = jnp.where(lane == 5, whole(total_vq), known)
    known = jnp.where(lane == 6, whole(total_mix), known)
    moments_ref[...] = jnp.broadcast_to(known, moments_ref.shape)


def final_kernel(moments_ref, r0_ref, b0_ref, b1_ref, x_hbm, r_hbm, x_ref, r_ref, sem):
    parts = jnp.transpose(moments_ref[...])
    m0_at, n1_at, c_at, vv_at, rv_at, vq_at, mix_at = (parts[i : i + 1, :] for i in range(7))

    def total(x):
        return jnp.sum(x, axis=1, keepdims=True)

    m0, n1 = total(m0_at), total(n1_at)
    mu = n1 / m0
    shift = c_at - mu
    vv = total(vv_at + shift * (2.0 * rv_at + shift * m0_at))
    vbv = total(vq_at + shift * (mix_at + shift * n1_at))
    a = m0 / (0.5 * m0 + n1)
    ratio = vv / m0
    beta = a * a * ratio
    step = vv / (0.5 * vv + vbv - a * vv * ratio)
    x_r0 = a + step * beta + step * a * mu
    x_b0 = -step * a
    r_r0 = a * mu - step * (0.5 * a * mu + 0.5 * beta)
    r_b0 = -a - step * (a * mu - 0.5 * a + beta)
    r_b1 = step * a
    sends = []
    step_rows = r0_ref.shape[0] // CHUNKS
    for c in range(CHUNKS):
        at = slice(c * step_rows, (c + 1) * step_rows)
        r0 = r0_ref[at, :]
        b0 = b0_ref[at, :]
        x_ref[at, :] = x_r0 * r0 + x_b0 * b0
        r_ref[at, :] = r_r0 * r0 + r_b0 * b0 + r_b1 * b1_ref[at, :]
        for i, (src, dst) in enumerate(((x_ref, x_hbm), (r_ref, r_hbm))):
            send = pltpu.make_async_copy(src.at[at], dst.at[at], sem.at[c, i])
            send.start()
            sends.append(send)
    for send in sends:
        send.wait()


VMEM = pl.BlockSpec(memory_space=pltpu.VMEM)
ANY = pl.BlockSpec(memory_space=pl.ANY)
HBM = pl.BlockSpec(memory_space=pltpu.HBM)


def call(kernel, shapes, *args, ins=None, outs=None, scratch=(), name, limit=24, flops=0):
    moved = sum(int(np.prod(x.shape)) * x.dtype.itemsize for x in args)
    return pl.pallas_call(
        kernel,
        out_shape=[
            jax.ShapeDtypeStruct(s, F32) if isinstance(s, tuple) else s for s in shapes
        ],
        in_specs=ins or [VMEM] * len(args),
        out_specs=outs or [VMEM] * len(shapes),
        scratch_shapes=list(scratch),
        compiler_params=pltpu.CompilerParams(vmem_limit_bytes=limit << 20),
        cost_estimate=pl.CostEstimate(flops=flops, bytes_accessed=moved, transcendentals=0),
        name=name,
    )(*args)


def neighbours(axes, step):
    count = int(np.prod([lax.axis_size(a) for a in axes]))
    return [(i, (i + step) % count) for i in range(count)]


def shards(block_sums, block_weights, block_tile, block_row, prior_weight):
    devices = lax.axis_size(TY_TX)
    n_tx = lax.axis_size(TX)
    blocks, _, cols = block_sums.shape
    rows = prior_weight.shape[0]
    parts = cols // LANES
    length = 2 * SLOTS * parts + 2 * SLOTS
    wide = cols + LANES

    prior_right = lax.ppermute(prior_weight[:, :LANES], TX, neighbours(TX, -1))
    prior_left = lax.ppermute(prior_weight[:, cols - LANES :], TX, neighbours(TX, 1))
    lane = jnp.arange(LANES)[None, :]
    prior_halo = jnp.where(lane < HALF, prior_right, jnp.where(lane >= LANES - HALF, prior_left, 0.0))

    (message,) = call(
        functools.partial(pack_kernel, n_tx, parts, length),
        [(devices * length, LANES)],
        block_tile.reshape(1, blocks),
        block_row.reshape(1, blocks),
        block_sums.reshape(blocks * parts, LANES),
        block_weights.reshape(blocks * parts, LANES),
        ins=[HBM] * 4,
        outs=[HBM],
        scratch=[
            pltpu.VMEM((1, blocks), jnp.int32),
            pltpu.VMEM((1, blocks), jnp.int32),
            pltpu.VMEM((blocks * parts, LANES), F32),
            pltpu.VMEM((blocks * parts, LANES), F32),
            pltpu.VMEM((3, blocks, 2 * cols), BF16),
            pltpu.VMEM((devices * length, LANES), F32),
            pltpu.SemaphoreType.DMA((4,)),
            pltpu.SemaphoreType.DMA((GROUPS,)),
        ],
        name="pack",
        limit=63,
    )
    got = lax.all_to_all(
        message.reshape(devices, 1, length * LANES), TY_TX, split_axis=0, concat_axis=0, tiled=True
    ).reshape(devices * length, LANES)
    s_slab, w_slab = (2 * HALF, wide), (HALF, wide)
    s, s_near, s_next, chosen, strip = call(
        functools.partial(sums_kernel, parts, length),
        [
            (rows, wide),
            s_slab,
            s_slab,
            jax.ShapeDtypeStruct((rows, SLOTS * devices), BF16),
            (rows, LANES),
        ],
        got,
        flops=3 * 2 * rows * wide * SLOTS * devices,
        name="sums",
    )
    w, w_near, w_next = call(
        functools.partial(weights_kernel, parts, length, n_tx),
        [(rows, wide), w_slab, w_slab],
        got,
        prior_weight,
        prior_halo,
        chosen,
        strip,
        flops=3 * 2 * rows * wide * SLOTS * devices,
        name="weights",
    )
    n_ty = lax.axis_size("ty")
    near = [(i, i ^ 1) for i in range(n_ty)]
    far = [((i + 1) % n_ty, ((i ^ 1) + 1) % n_ty) for i in range(n_ty)]
    s_near, s_next = lax.ppermute(s_near, "ty", near), lax.ppermute(s_next, "ty", far)
    w_near, w_next = lax.ppermute(w_near, "ty", near), lax.ppermute(w_next, "ty", far)

    tall = rows + 2 * HALF
    col_taps = taps(np.arange(2 * LANES)[None, :] - np.arange(4 * LANES)[:, None] + LANES, 0)
    ring = np.where(np.arange(LANES) < 64, cols, -LANES) + np.arange(LANES)
    near = np.concatenate([np.arange(cols - LANES, cols), ring, np.arange(LANES)])
    edge_taps = taps(ring[None, :] - near[:, None], 0)
    tile = (rows, cols)
    inside = np.arange(rows)
    border_rows = np.concatenate(
        [np.arange(-HALF, HALF), np.arange(rows - HALF, rows + HALF)]
    )
    early_rows = np.concatenate([border_rows, inside[HALF : rows - HALF]])
    far_rows = np.concatenate([np.arange(-2 * HALF, 0), np.arange(rows, rows + 2 * HALF)])
    early_taps = taps(early_rows[:, None] - inside[None, :], 0)
    first_taps = taps(border_rows[:, None] - far_rows[None, :], 0)
    part, deep, root, r0, early = call(
        early_kernel,
        [(4 * HALF, wide), (rows - 2 * HALF, wide), tile, tile, (16, LANES)],
        s,
        w,
        early_taps,
        col_taps,
        edge_taps,
        scratch=[pltpu.VMEM((rows - 2 * HALF, wide), F32)],
        flops=5 * 2 * tall * wide * 3 * LANES,
        name="early",
    )
    y0, early = call(
        functools.partial(first_kernel, n_ty),
        [(tall, wide), (16, LANES)],
        s,
        s_near,
        s_next,
        part,
        deep,
        early,
        first_taps,
        col_taps,
        edge_taps,
        scratch=[pltpu.VMEM((4 * HALF, wide), F32), pltpu.VMEM((4 * HALF, wide), F32)],
        flops=5 * 2 * rows * wide * 6 * LANES,
        name="first",
    )
    own_taps = taps(inside[:, None] - inside[None, :], 0)
    border = np.concatenate([inside[:HALF], inside[rows - HALF :]])
    outside = np.concatenate([np.arange(-HALF, 0), np.arange(rows, rows + HALF)])
    halo_taps = taps(border[:, None] - outside[None, :], 0)
    b0, inner, part, sums = call(
        second_kernel,
        [tile, (rows - 2 * HALF, cols), (rows, wide), (24, LANES)],
        w,
        y0,
        root,
        r0,
        early,
        own_taps,
        col_taps,
        flops=5 * 2 * rows * wide * 3 * LANES,
        name="second",
    )
    b1, moments = call(
        functools.partial(third_kernel, n_ty),
        [tile, (devices, LANES)],
        w_near,
        w_next,
        y0,
        root,
        r0,
        b0,
        part,
        inner,
        sums,
        halo_taps,
        col_taps,
        scratch=[pltpu.VMEM((2 * HALF, wide), F32)],
        flops=5 * 2 * rows * wide * 3 * LANES,
        name="third",
    )
    moments = lax.all_to_all(
        moments.reshape(devices, 1, LANES), TY_TX, split_axis=0, concat_axis=0, tiled=True
    ).reshape(devices, LANES)
    return tuple(
        call(
            final_kernel,
            [tile, tile],
            moments,
            r0,
            b0,
            b1,
            outs=[HBM, HBM],
            scratch=[
                pltpu.VMEM(tile, F32),
                pltpu.VMEM(tile, F32),
                pltpu.SemaphoreType.DMA((CHUNKS, 2)),
            ],
            name="combine",
        )
    )


def solution(mesh):
    split = Mesh(mesh.devices.reshape(mesh.shape["ty"], 4, 4, 2), ("ty", "tx_0", "tx_1", "tx_2"))
    in_specs = (P(TY_TX, None, None), P(TY_TX, None, None), P(TY_TX, None), P(TY_TX), P("ty", TX))
    out_specs = (P("ty", TX), P("ty", TX))
    return jax.shard_map(
        shards, mesh=split, in_specs=in_specs, out_specs=out_specs, check_vma=False
    )
```

```python
import functools

import jax
import jax.numpy as jnp
import numpy as np
from jax import lax
from jax.experimental import pallas as pl
from jax.experimental.pallas import tpu as pltpu
from jax.sharding import Mesh
from jax.sharding import PartitionSpec as P

HALF = 32
LANES = 128
SLOTS = 2
GROUPS = 2
CHUNKS = 4
TY_TX = ("ty", "tx_0", "tx_1", "tx_2")
TX = ("tx_0", "tx_1", "tx_2")
F32 = jnp.float32
BF16 = jnp.bfloat16


def taps(offset, axis):
    def raw(d):
        scaled = np.abs(d) / (HALF + 1.0)
        return np.where(np.abs(d) <= HALF, (1.0 - scaled) ** 4 * (1.0 + 4.0 * scaled), 0.0)

    values = raw(offset) / raw(np.arange(-HALF, HALF + 1)).sum()
    head = values.astype(BF16)
    tail = (values - head.astype(np.float64)).astype(BF16)
    return jnp.asarray(np.concatenate([head, tail], axis=axis))


def split3(x):
    head = x.astype(BF16)
    rest = x - head.astype(F32)
    mid = rest.astype(BF16)
    return head, mid, (rest - mid.astype(F32)).astype(BF16)


def mm(a, b):
    return jnp.dot(a, b, preferred_element_type=F32)


def pick(select, x):
    head, mid, tail = split3(x)
    return mm(select, tail) + mm(select, mid) + mm(select, head)


def taps_times(taps_ref, x):
    rows = taps_ref.shape[0] // 2
    xh, xm, xl = split3(x)
    low = mm(taps_ref[:rows, :], xl)
    mid = mm(taps_ref[...], xm)
    high = mm(taps_ref[...], xh)
    return low + mid[rows:] + high[rows:] + mid[:rows] + high[:rows]


def times_taps(pieces, taps_ref):
    xh, xm, xl = pieces
    depth = taps_ref.shape[0] // 2
    head, tail = taps_ref[:depth, :], taps_ref[depth:, :]
    return mm(xl, head) + mm(xm, tail) + mm(xh, tail) + mm(xm, head) + mm(xh, head)


def spans(wide):
    cols = wide - LANES
    return [slice(c, c + 2 * LANES) for c in range(0, cols, 2 * LANES)] + [slice(cols, wide)]


def iota(shape, dim):
    return lax.broadcasted_iota(jnp.int32, shape, dim)


def pack_kernel(
    n_tx, parts, length, tile_hbm, row_hbm, sums_hbm, weights_hbm, out_hbm,
    tile_ref, row_ref, sums_ref, weights_ref, split_ref, out_ref, in_sem, out_sem
):
    fetches = [
        pltpu.make_async_copy(src, dst, in_sem.at[i])
        for i, (src, dst) in enumerate(
            (
                (tile_hbm, tile_ref),
                (row_hbm, row_ref),
                (sums_hbm, sums_ref),
                (weights_hbm, weights_ref),
            )
        )
    ]
    for fetch in fetches:
        fetch.start()
    fetches[0].wait()
    fetches[1].wait()
    count = tile_ref.shape[1]
    devices = out_ref.shape[0] // length
    group = devices // GROUPS
    tile = tile_ref[...]
    t = iota((devices, count), 0)
    same = tile == t
    earlier = iota((count, count), 0) < iota((count, count), 1)
    before = mm(same.astype(F32).astype(BF16), earlier.astype(F32).astype(BF16))
    rank = jnp.sum(jnp.where(same, before, 0.0), axis=0, keepdims=True)
    column = lax.rem(t, n_tx)
    from_left = (tile + 1 == t) & (column != 0)
    from_right = (tile - 1 == t) & (column != n_tx - 1)

    def onehot(mask, k):
        return jnp.where(mask & (rank == float(k)), 1.0, 0.0)

    own = [onehot(same, k) for k in range(SLOTS)]
    left = [onehot(from_left, k) for k in range(SLOTS)]
    right = [
        jnp.concatenate([onehot(from_right, k), own[k]], axis=1) for k in range(SLOTS)
    ]

    def of_group(masks, g):
        part = slice(g * group, (g + 1) * group)
        return jnp.concatenate([m[part] for m in masks], axis=0).astype(BF16)

    lane = iota((count, LANES), 1)
    number = jnp.transpose(jnp.broadcast_to(row_ref[...].astype(F32) + 1.0, (count, count)))
    for which, ref in enumerate((sums_ref, weights_ref)):
        fetches[2 + which].wait()
        for c in range(parts):
            at = slice((which * parts + c) * LANES, (which * parts + c + 1) * LANES)
            for i, piece in enumerate(split3(ref[pl.ds(c, count, stride=parts), :])):
                split_ref[i, :, at] = piece

    last = parts - 1
    s_last = sums_ref[pl.ds(last, count, stride=parts), :]
    w_last = pltpu.roll(weights_ref[pl.ds(last, count, stride=parts), :], 64, 1)
    s_first = sums_ref[pl.ds(0, count, stride=parts), :]
    w_first = pltpu.roll(weights_ref[pl.ds(0, count, stride=parts), :], 64, 1)
    left_rows = jnp.where(
        lane >= 64, s_last, jnp.where(lane >= 32, w_last, jnp.where(lane == 0, number, 0.0))
    )
    right_rows = jnp.where(
        lane < 64, s_first, jnp.where(lane < 96, w_first, jnp.where(lane == 96, number, 0.0))
    )
    own_rows = jnp.where(lane == 97, number, 0.0)
    both_rows = jnp.concatenate([right_rows, own_rows], axis=0)

    base = 2 * SLOTS * parts
    sends = []
    for g in range(GROUPS):
        first = g * group * length
        own_all = of_group(own, g)
        for c in range(0, 2 * parts, 2):
            at = slice(c * LANES, (c + 2) * LANES)
            y = (
                mm(own_all, split_ref[2, :, at])
                + mm(own_all, split_ref[1, :, at])
                + mm(own_all, split_ref[0, :, at])
            )
            which, chunk = divmod(c, parts)
            for k in range(SLOTS):
                for i in range(2):
                    to = first + (which * SLOTS + k) * parts + chunk + i
                    out_ref[pl.ds(to, group, stride=length), :] = y[
                        k * group : (k + 1) * group, i * LANES : (i + 1) * LANES
                    ]
        to_left = pick(of_group(left, g), left_rows)
        to_right = pick(of_group(right, g), both_rows)
        for k in range(SLOTS):
            part = slice(k * group, (k + 1) * group)
            out_ref[pl.ds(first + base + k, group, stride=length), :] = to_left[part]
            out_ref[pl.ds(first + base + SLOTS + k, group, stride=length), :] = to_right[part]
        span = pl.ds(first, group * length)
        send = pltpu.make_async_copy(out_ref.at[span], out_hbm.at[span], out_sem.at[g])
        send.start()
        sends.append(send)
    for send in sends:
        send.wait()


def slot_rows(got_ref, length, at, devices):
    return got_ref[pl.ds(at, devices, stride=length), :]


def odd_row():
    return lax.rem(lax.axis_index("ty"), 2)


def to_partners(ref, near_ref, next_ref):
    rows, count = ref.shape[0], near_ref.shape[0]
    bottom = (rows - count) * (1 - odd_row())
    near_ref[...] = ref[pl.ds(pl.multiple_of(bottom, 8), count), :]
    next_ref[...] = ref[pl.ds(pl.multiple_of(rows - count - bottom, 8), count), :]


def from_partners(n_ty, near_ref, next_ref, at):
    row_at, odd = lax.axis_index("ty"), odd_row() == 1
    near, far = near_ref[:, at], next_ref[:, at]
    above = jnp.where(odd, near, far) * jnp.where(row_at > 0, 1.0, 0.0)
    below = jnp.where(odd, far, near) * jnp.where(row_at < n_ty - 1, 1.0, 0.0)
    return above, below


def gather_tile(got_ref, parts, length, which, select, dst, extra):
    devices = got_ref.shape[0] // length
    for c in range(0, parts, 2):
        x = jnp.concatenate(
            [
                jnp.concatenate(
                    [
                        slot_rows(got_ref, length, (which * SLOTS + k) * parts + c + i, devices)
                        for i in range(2)
                    ],
                    axis=1,
                )
                for k in range(SLOTS)
            ],
            axis=0,
        )
        at = slice(c * LANES, (c + 2) * LANES)
        y = pick(select, x)
        dst[:, at] = y if extra is None else y + extra[:, at]


def sums_kernel(parts, length, got_ref, s_ref, near_ref, next_ref, select_ref, strip_ref):
    rows, wide = s_ref.shape
    cols = wide - LANES
    devices = got_ref.shape[0] // length
    base = 2 * SLOTS * parts
    from_left = [slot_rows(got_ref, length, base + k, devices) for k in range(SLOTS)]
    from_right = [slot_rows(got_ref, length, base + SLOTS + k, devices) for k in range(SLOTS)]
    left_t = [jnp.transpose(x) for x in from_left]
    right_t = [jnp.transpose(x) for x in from_right]
    wanted = (iota((rows, devices), 0) + 1).astype(F32)

    def chooser(lists, at):
        return jnp.concatenate(
            [jnp.where(x[at : at + 1, :] == wanted, 1.0, 0.0) for x in lists], axis=1
        ).astype(BF16)

    own = chooser(right_t, 97)
    select_ref[...] = own
    gather_tile(got_ref, parts, length, 0, own, s_ref, None)
    left = pick(chooser(left_t, 0), jnp.concatenate(from_left, axis=0))
    right = pick(chooser(right_t, 96), jnp.concatenate(from_right, axis=0))
    lane = iota((rows, LANES), 1)
    s_ref[:, cols:] = jnp.where(lane < 64, right, left)
    strip_ref[...] = jnp.where(lane < 64, pltpu.roll(right, 64, 1), pltpu.roll(left, 64, 1))
    to_partners(s_ref, near_ref, next_ref)


def weights_kernel(
    parts, length, n_tx, got_ref, prior_ref, prior_halo_ref, select_ref, strip_ref,
    w_ref, near_ref, next_ref
):
    rows, wide = w_ref.shape
    cols = wide - LANES
    gather_tile(got_ref, parts, length, 1, select_ref[...], w_ref, prior_ref)
    lane = iota((rows, LANES), 1)
    column = lax.axis_index(TX)
    has_left = jnp.where(column > 0, 1.0, 0.0)
    has_right = jnp.where(column < n_tx - 1, 1.0, 0.0)
    prior_halo = prior_halo_ref[...]
    strip = strip_ref[...]
    w_ref[:, cols:] = jnp.where(
        lane < HALF,
        prior_halo * has_right + strip,
        jnp.where(lane >= LANES - HALF, prior_halo * has_left + strip, 0.0),
    )
    to_partners(w_ref, near_ref, next_ref)


def along_columns(pieces, taps_ref):
    height, wide = pieces[0].shape
    cols = wide - LANES

    def stacked(x):
        first = jnp.concatenate([x[:, cols:], x[:, : 3 * LANES]], axis=1)
        rest = [
            x[:, (c - 1) * LANES : (c + 3) * LANES] for c in range(2, cols // LANES, 2)
        ]
        return jnp.concatenate([first] + rest, axis=0)

    half = [stacked(x) for x in pieces]
    out = []
    for r in range(0, half[0].shape[0], 2 * height):
        y = times_taps([x[r : r + 2 * height] for x in half], taps_ref)
        out += [y[:height], y[height:]]
    return out


def all_columns(mid, y0_ref, at, col_ref, edge_ref):
    wide = mid.shape[1]
    cols = wide - LANES
    pieces = split3(mid)
    for c, y in enumerate(along_columns(pieces, col_ref)):
        y0_ref[at, 2 * c * LANES : 2 * (c + 1) * LANES] = y
    near = [jnp.concatenate([x[:, cols - LANES :], x[:, :LANES]], axis=1) for x in pieces]
    y0_ref[at, cols:] = times_taps(near, edge_ref)


def early_kernel(
    s_ref,
    w_ref,
    own_ref,
    col_ref,
    edge_ref,
    part_ref,
    deep_ref,
    root_ref,
    r0_ref,
    sums_ref,
    mid_ref,
):
    rows, wide = s_ref.shape
    cols = wide - LANES
    edge = 4 * HALF
    for at in spans(wide):
        mid = taps_times(own_ref, s_ref[:, at])
        part_ref[:, at] = mid[:edge]
        mid_ref[:, at] = mid[edge:]
    all_columns(mid_ref[...], deep_ref, slice(None), col_ref, edge_ref)
    total_rr = total_rb = jnp.zeros((8, cols), F32)
    for r in range(0, rows, 8):
        at = slice(r, r + 8)
        root = jnp.sqrt(w_ref[at, :cols])
        s = s_ref[at, :cols]
        r0 = s / root
        root_ref[at, :] = root
        r0_ref[at, :] = r0
        total_rr += r0 * r0
        if HALF <= r < rows - HALF:
            total_rb += s * deep_ref[r - HALF : r - HALF + 8, :cols]
    sums_ref[0:8, :] = folded(total_rr)
    sums_ref[8:16, :] = folded(total_rb)


def first_kernel(
    n_ty,
    s_ref,
    near_ref,
    next_ref,
    part_ref,
    early_ref,
    halo_ref,
    col_ref,
    edge_ref,
    border_ref,
    sums_ref,
    mid_ref,
):
    rows, wide = s_ref.shape
    cols = wide - LANES
    for at in spans(wide):
        halo = jnp.concatenate(from_partners(n_ty, near_ref, next_ref, at), axis=0)
        mid_ref[:, at] = part_ref[:, at] + taps_times(halo_ref, halo)
    all_columns(mid_ref[...], border_ref, slice(None), col_ref, edge_ref)
    two = 2 * HALF
    top = s_ref[:HALF, :cols] * border_ref[HALF:two, :cols]
    bottom = s_ref[rows - HALF :, :cols] * border_ref[two : two + HALF, :cols]
    sums_ref[0:8, :] = early_ref[0:8, :]
    sums_ref[8:16, :] = early_ref[8:16, :] + folded(top) + folded(bottom)


def folded(total):
    rows, cols = total.shape
    total = sum(total[r : r + 8] for r in range(0, rows, 8))
    return sum(total[:, c : c + LANES] for c in range(0, cols, LANES))


def whole(total):
    return jnp.sum(jnp.sum(total, axis=0, keepdims=True), axis=1, keepdims=True)


def second_kernel(
    n_ty,
    w_ref,
    near_ref,
    next_ref,
    deep_ref,
    border_ref,
    root_ref,
    r0_ref,
    first_ref,
    row_ref,
    col_ref,
    b0_ref,
    b1_ref,
    moments_ref,
    mid_ref,
):
    rows, wide = w_ref.shape
    cols = wide - LANES
    one, two, three = HALF, 2 * HALF, 3 * HALF
    m0, n1 = whole(first_ref[0:8, :]), whole(first_ref[8:16, :])
    c0 = n1 / jnp.where(m0 > 0.0, m0, 1.0)
    for at in spans(wide):
        above, below = from_partners(n_ty, near_ref, next_ref, at)
        z = jnp.concatenate(
            [
                above * border_ref[:one, at],
                w_ref[:one, at] * border_ref[one:two, at],
                w_ref[one : rows - one, at] * deep_ref[:, at],
                w_ref[rows - one :, at] * border_ref[two:three, at],
                below * border_ref[three:, at],
            ],
            axis=0,
        )
        mid_ref[:, at] = taps_times(row_ref, z)
    total_vv = total_rv = total_vq = total_mix = jnp.zeros((8, LANES), F32)
    for c, y1 in enumerate(along_columns(split3(mid_ref[...]), col_ref)):
        at = slice(2 * c * LANES, 2 * (c + 1) * LANES)
        y0 = jnp.concatenate(
            [border_ref[one:two, at], deep_ref[:, at], border_ref[two:three, at]], axis=0
        )
        r0, root = r0_ref[:, at], root_ref[:, at]
        b0, b1 = root * y0, root * y1
        b0_ref[:, at] = b0
        b1_ref[:, at] = b1
        v, q = b0 - c0 * r0, b1 - c0 * b0
        total_vv += folded(v * v)
        total_rv += folded(r0 * v)
        total_vq += folded(v * q)
        total_mix += folded(v * b0 + r0 * q)
    lane = iota((1, LANES), 1)
    known = jnp.zeros((1, LANES), F32)
    totals = (whole(x) for x in (total_vv, total_rv, total_vq, total_mix))
    for i, value in enumerate((m0, n1, c0, *totals)):
        known = jnp.where(lane == i, value, known)
    moments_ref[...] = jnp.broadcast_to(known, moments_ref.shape)


def final_kernel(moments_ref, r0_ref, b0_ref, b1_ref, x_hbm, r_hbm, x_ref, r_ref, sem):
    parts = jnp.transpose(moments_ref[...])
    m0_at, n1_at, c_at, vv_at, rv_at, vq_at, mix_at = (parts[i : i + 1, :] for i in range(7))

    def total(x):
        return jnp.sum(x, axis=1, keepdims=True)

    m0, n1 = total(m0_at), total(n1_at)
    mu = n1 / m0
    shift = c_at - mu
    vv = total(vv_at + shift * (2.0 * rv_at + shift * m0_at))
    vbv = total(vq_at + shift * (mix_at + shift * n1_at))
    a = m0 / (0.5 * m0 + n1)
    ratio = vv / m0
    beta = a * a * ratio
    step = vv / (0.5 * vv + vbv - a * vv * ratio)
    x_r0 = a + step * beta + step * a * mu
    x_b0 = -step * a
    r_r0 = a * mu - step * (0.5 * a * mu + 0.5 * beta)
    r_b0 = -a - step * (a * mu - 0.5 * a + beta)
    r_b1 = step * a
    sends = []
    step_rows = r0_ref.shape[0] // CHUNKS
    for c in range(CHUNKS):
        at = slice(c * step_rows, (c + 1) * step_rows)
        r0 = r0_ref[at, :]
        b0 = b0_ref[at, :]
        x_ref[at, :] = x_r0 * r0 + x_b0 * b0
        r_ref[at, :] = r_r0 * r0 + r_b0 * b0 + r_b1 * b1_ref[at, :]
        for i, (src, dst) in enumerate(((x_ref, x_hbm), (r_ref, r_hbm))):
            send = pltpu.make_async_copy(src.at[at], dst.at[at], sem.at[c, i])
            send.start()
            sends.append(send)
    for send in sends:
        send.wait()


VMEM = pl.BlockSpec(memory_space=pltpu.VMEM)
ANY = pl.BlockSpec(memory_space=pl.ANY)
HBM = pl.BlockSpec(memory_space=pltpu.HBM)


def call(kernel, shapes, *args, ins=None, outs=None, scratch=(), name, limit=24, flops=0):
    moved = sum(int(np.prod(x.shape)) * x.dtype.itemsize for x in args)
    return pl.pallas_call(
        kernel,
        out_shape=[
            jax.ShapeDtypeStruct(s, F32) if isinstance(s, tuple) else s for s in shapes
        ],
        in_specs=ins or [VMEM] * len(args),
        out_specs=outs or [VMEM] * len(shapes),
        scratch_shapes=list(scratch),
        compiler_params=pltpu.CompilerParams(vmem_limit_bytes=limit << 20),
        cost_estimate=pl.CostEstimate(flops=flops, bytes_accessed=moved, transcendentals=0),
        name=name,
    )(*args)


def neighbours(axes, step):
    count = int(np.prod([lax.axis_size(a) for a in axes]))
    return [(i, (i + step) % count) for i in range(count)]


def shards(block_sums, block_weights, block_tile, block_row, prior_weight):
    devices = lax.axis_size(TY_TX)
    n_tx = lax.axis_size(TX)
    blocks, _, cols = block_sums.shape
    rows = prior_weight.shape[0]
    parts = cols // LANES
    length = 2 * SLOTS * parts + 2 * SLOTS
    wide = cols + LANES

    prior_right = lax.ppermute(prior_weight[:, :LANES], TX, neighbours(TX, -1))
    prior_left = lax.ppermute(prior_weight[:, cols - LANES :], TX, neighbours(TX, 1))
    lane = jnp.arange(LANES)[None, :]
    prior_halo = jnp.where(lane < HALF, prior_right, jnp.where(lane >= LANES - HALF, prior_left, 0.0))

    (message,) = call(
        functools.partial(pack_kernel, n_tx, parts, length),
        [(devices * length, LANES)],
        block_tile.reshape(1, blocks),
        block_row.reshape(1, blocks),
        block_sums.reshape(blocks * parts, LANES),
        block_weights.reshape(blocks * parts, LANES),
        ins=[HBM] * 4,
        outs=[HBM],
        scratch=[
            pltpu.VMEM((1, blocks), jnp.int32),
            pltpu.VMEM((1, blocks), jnp.int32),
            pltpu.VMEM((blocks * parts, LANES), F32),
            pltpu.VMEM((blocks * parts, LANES), F32),
            pltpu.VMEM((3, blocks, 2 * cols), BF16),
            pltpu.VMEM((devices * length, LANES), F32),
            pltpu.SemaphoreType.DMA((4,)),
            pltpu.SemaphoreType.DMA((GROUPS,)),
        ],
        name="pack",
        limit=63,
    )
    got = lax.all_to_all(
        message.reshape(devices, 1, length * LANES), TY_TX, split_axis=0, concat_axis=0, tiled=True
    ).reshape(devices * length, LANES)
    s_slab, w_slab = (2 * HALF, wide), (HALF, wide)
    s, s_near, s_next, chosen, strip = call(
        functools.partial(sums_kernel, parts, length),
        [
            (rows, wide),
            s_slab,
            s_slab,
            jax.ShapeDtypeStruct((rows, SLOTS * devices), BF16),
            (rows, LANES),
        ],
        got,
        flops=3 * 2 * rows * wide * SLOTS * devices,
        name="sums",
    )
    w, w_near, w_next = call(
        functools.partial(weights_kernel, parts, length, n_tx),
        [(rows, wide), w_slab, w_slab],
        got,
        prior_weight,
        prior_halo,
        chosen,
        strip,
        flops=3 * 2 * rows * wide * SLOTS * devices,
        name="weights",
    )
    n_ty = lax.axis_size("ty")
    near = [(i, i ^ 1) for i in range(n_ty)]
    far = [((i + 1) % n_ty, ((i ^ 1) + 1) % n_ty) for i in range(n_ty)]
    s_near, s_next = lax.ppermute(s_near, "ty", near), lax.ppermute(s_next, "ty", far)
    w_near, w_next = lax.ppermute(w_near, "ty", near), lax.ppermute(w_next, "ty", far)

    tall = rows + 2 * HALF
    col_taps = taps(np.arange(2 * LANES)[None, :] - np.arange(4 * LANES)[:, None] + LANES, 0)
    ring = np.where(np.arange(LANES) < 64, cols, -LANES) + np.arange(LANES)
    near = np.concatenate([np.arange(cols - LANES, cols), ring, np.arange(LANES)])
    edge_taps = taps(ring[None, :] - near[:, None], 0)
    tile = (rows, cols)
    inside = np.arange(rows)
    border_rows = np.concatenate(
        [np.arange(-HALF, HALF), np.arange(rows - HALF, rows + HALF)]
    )
    early_rows = np.concatenate([border_rows, inside[HALF : rows - HALF]])
    far_rows = np.concatenate([np.arange(-2 * HALF, 0), np.arange(rows, rows + 2 * HALF)])
    early_taps = taps(early_rows[:, None] - inside[None, :], 0)
    first_taps = taps(border_rows[:, None] - far_rows[None, :], 0)
    part, deep, root, r0, early = call(
        early_kernel,
        [(4 * HALF, wide), (rows - 2 * HALF, wide), tile, tile, (16, LANES)],
        s,
        w,
        early_taps,
        col_taps,
        edge_taps,
        scratch=[pltpu.VMEM((rows - 2 * HALF, wide), F32)],
        flops=5 * 2 * tall * wide * 3 * LANES,
        name="early",
    )
    border, early = call(
        functools.partial(first_kernel, n_ty),
        [(4 * HALF, wide), (16, LANES)],
        s,
        s_near,
        s_next,
        part,
        early,
        first_taps,
        col_taps,
        edge_taps,
        scratch=[pltpu.VMEM((4 * HALF, wide), F32)],
        flops=5 * 2 * rows * wide * 6 * LANES,
        name="first",
    )
    second_taps = taps(inside[:, None] - np.arange(-HALF, rows + HALF)[None, :], 0)
    b0, b1, moments = call(
        functools.partial(second_kernel, n_ty),
        [tile, tile, (devices, LANES)],
        w,
        w_near,
        w_next,
        deep,
        border,
        root,
        r0,
        early,
        second_taps,
        col_taps,
        scratch=[pltpu.VMEM((rows, wide), F32)],
        flops=5 * 2 * rows * wide * 6 * LANES,
        name="second",
    )
    moments = lax.all_to_all(
        moments.reshape(devices, 1, LANES), TY_TX, split_axis=0, concat_axis=0, tiled=True
    ).reshape(devices, LANES)
    return tuple(
        call(
            final_kernel,
            [tile, tile],
            moments,
            r0,
            b0,
            b1,
            outs=[HBM, HBM],
            scratch=[
                pltpu.VMEM(tile, F32),
                pltpu.VMEM(tile, F32),
                pltpu.SemaphoreType.DMA((CHUNKS, 2)),
            ],
            name="combine",
        )
    )


def solution(mesh):
    split = Mesh(mesh.devices.reshape(mesh.shape["ty"], 4, 4, 2), ("ty", "tx_0", "tx_1", "tx_2"))
    in_specs = (P(TY_TX, None, None), P(TY_TX, None, None), P(TY_TX, None), P(TY_TX), P("ty", TX))
    out_specs = (P("ty", TX), P("ty", TX))
    return jax.shard_map(
        shards, mesh=split, in_specs=in_specs, out_specs=out_specs, check_vma=False
    )
```

```python
import functools

import jax
import jax.numpy as jnp
import numpy as np
from jax import lax
from jax.experimental import pallas as pl
from jax.experimental.pallas import tpu as pltpu
from jax.sharding import Mesh
from jax.sharding import PartitionSpec as P

HALF = 32
LANES = 128
SLOTS = 2
GROUPS = 2
CHUNKS = 4
TY_TX = ("ty", "tx_0", "tx_1", "tx_2")
TX = ("tx_0", "tx_1", "tx_2")
F32 = jnp.float32
BF16 = jnp.bfloat16


def taps(offset, axis):
    def raw(d):
        scaled = np.abs(d) / (HALF + 1.0)
        return np.where(np.abs(d) <= HALF, (1.0 - scaled) ** 4 * (1.0 + 4.0 * scaled), 0.0)

    values = raw(offset) / raw(np.arange(-HALF, HALF + 1)).sum()
    head = values.astype(BF16)
    tail = (values - head.astype(np.float64)).astype(BF16)
    return jnp.asarray(np.concatenate([head, tail], axis=axis))


def split3(x):
    head = x.astype(BF16)
    rest = x - head.astype(F32)
    mid = rest.astype(BF16)
    return head, mid, (rest - mid.astype(F32)).astype(BF16)


def mm(a, b):
    return jnp.dot(a, b, preferred_element_type=F32)


def pick(select, x):
    head, mid, tail = split3(x)
    return mm(select, tail) + mm(select, mid) + mm(select, head)


def taps_times(taps_ref, x):
    rows = taps_ref.shape[0] // 2
    xh, xm, xl = split3(x)
    low = mm(taps_ref[:rows, :], xl)
    mid = mm(taps_ref[...], xm)
    high = mm(taps_ref[...], xh)
    return low + mid[rows:] + high[rows:] + mid[:rows] + high[:rows]


def times_taps(pieces, taps_ref):
    xh, xm, xl = pieces
    depth = taps_ref.shape[0] // 2
    head, tail = taps_ref[:depth, :], taps_ref[depth:, :]
    return mm(xl, head) + mm(xm, tail) + mm(xh, tail) + mm(xm, head) + mm(xh, head)


def spans(wide):
    cols = wide - LANES
    return [slice(c, c + 2 * LANES) for c in range(0, cols, 2 * LANES)] + [slice(cols, wide)]


def iota(shape, dim):
    return lax.broadcasted_iota(jnp.int32, shape, dim)


def pack_kernel(
    n_tx, parts, length, tile_hbm, row_hbm, sums_hbm, weights_hbm, out_hbm,
    tile_ref, row_ref, sums_ref, weights_ref, split_ref, out_ref, in_sem, out_sem
):
    fetches = [
        pltpu.make_async_copy(src, dst, in_sem.at[i])
        for i, (src, dst) in enumerate(
            (
                (tile_hbm, tile_ref),
                (row_hbm, row_ref),
                (sums_hbm, sums_ref),
                (weights_hbm, weights_ref),
            )
        )
    ]
    for fetch in fetches:
        fetch.start()
    fetches[0].wait()
    fetches[1].wait()
    count = tile_ref.shape[1]
    devices = out_ref.shape[0] // length
    group = devices // GROUPS
    tile = tile_ref[...]
    t = iota((devices, count), 0)
    same = tile == t
    earlier = iota((count, count), 0) < iota((count, count), 1)
    before = mm(same.astype(F32).astype(BF16), earlier.astype(F32).astype(BF16))
    rank = jnp.sum(jnp.where(same, before, 0.0), axis=0, keepdims=True)
    column = lax.rem(t, n_tx)
    from_left = (tile + 1 == t) & (column != 0)
    from_right = (tile - 1 == t) & (column != n_tx - 1)

    def onehot(mask, k):
        return jnp.where(mask & (rank == float(k)), 1.0, 0.0)

    own = [onehot(same, k) for k in range(SLOTS)]
    left = [onehot(from_left, k) for k in range(SLOTS)]
    right = [
        jnp.concatenate([onehot(from_right, k), own[k]], axis=1) for k in range(SLOTS)
    ]

    def of_group(masks, g):
        part = slice(g * group, (g + 1) * group)
        return jnp.concatenate([m[part] for m in masks], axis=0).astype(BF16)

    lane = iota((count, LANES), 1)
    number = jnp.transpose(jnp.broadcast_to(row_ref[...].astype(F32) + 1.0, (count, count)))
    for which, ref in enumerate((sums_ref, weights_ref)):
        fetches[2 + which].wait()
        for c in range(parts):
            at = slice((which * parts + c) * LANES, (which * parts + c + 1) * LANES)
            for i, piece in enumerate(split3(ref[pl.ds(c, count, stride=parts), :])):
                split_ref[i, :, at] = piece

    last = parts - 1
    s_last = sums_ref[pl.ds(last, count, stride=parts), :]
    w_last = pltpu.roll(weights_ref[pl.ds(last, count, stride=parts), :], 64, 1)
    s_first = sums_ref[pl.ds(0, count, stride=parts), :]
    w_first = pltpu.roll(weights_ref[pl.ds(0, count, stride=parts), :], 64, 1)
    left_rows = jnp.where(
        lane >= 64, s_last, jnp.where(lane >= 32, w_last, jnp.where(lane == 0, number, 0.0))
    )
    right_rows = jnp.where(
        lane < 64, s_first, jnp.where(lane < 96, w_first, jnp.where(lane == 96, number, 0.0))
    )
    own_rows = jnp.where(lane == 97, number, 0.0)
    both_rows = jnp.concatenate([right_rows, own_rows], axis=0)

    base = 2 * SLOTS * parts
    sends = []
    for g in range(GROUPS):
        first = g * group * length
        own_all = of_group(own, g)
        for c in range(0, 2 * parts, 2):
            at = slice(c * LANES, (c + 2) * LANES)
            y = (
                mm(own_all, split_ref[2, :, at])
                + mm(own_all, split_ref[1, :, at])
                + mm(own_all, split_ref[0, :, at])
            )
            which, chunk = divmod(c, parts)
            for k in range(SLOTS):
                for i in range(2):
                    to = first + (which * SLOTS + k) * parts + chunk + i
                    out_ref[pl.ds(to, group, stride=length), :] = y[
                        k * group : (k + 1) * group, i * LANES : (i + 1) * LANES
                    ]
        to_left = pick(of_group(left, g), left_rows)
        to_right = pick(of_group(right, g), both_rows)
        for k in range(SLOTS):
            part = slice(k * group, (k + 1) * group)
            out_ref[pl.ds(first + base + k, group, stride=length), :] = to_left[part]
            out_ref[pl.ds(first + base + SLOTS + k, group, stride=length), :] = to_right[part]
        span = pl.ds(first, group * length)
        send = pltpu.make_async_copy(out_ref.at[span], out_hbm.at[span], out_sem.at[g])
        send.start()
        sends.append(send)
    for send in sends:
        send.wait()


def slot_rows(got_ref, length, at, devices):
    return got_ref[pl.ds(at, devices, stride=length), :]


def odd_row():
    return lax.rem(lax.axis_index("ty"), 2)


def to_partners(ref, near_ref, next_ref):
    rows, count = ref.shape[0], near_ref.shape[0]
    bottom = (rows - count) * (1 - odd_row())
    near_ref[...] = ref[pl.ds(pl.multiple_of(bottom, 8), count), :]
    next_ref[...] = ref[pl.ds(pl.multiple_of(rows - count - bottom, 8), count), :]


def from_partners(n_ty, near_ref, next_ref, at):
    row_at, odd = lax.axis_index("ty"), odd_row() == 1
    near, far = near_ref[:, at], next_ref[:, at]
    above = jnp.where(odd, near, far) * jnp.where(row_at > 0, 1.0, 0.0)
    below = jnp.where(odd, far, near) * jnp.where(row_at < n_ty - 1, 1.0, 0.0)
    return above, below


def gather_tile(got_ref, parts, length, which, select, dst, extra):
    devices = got_ref.shape[0] // length
    for c in range(0, parts, 2):
        x = jnp.concatenate(
            [
                jnp.concatenate(
                    [
                        slot_rows(got_ref, length, (which * SLOTS + k) * parts + c + i, devices)
                        for i in range(2)
                    ],
                    axis=1,
                )
                for k in range(SLOTS)
            ],
            axis=0,
        )
        at = slice(c * LANES, (c + 2) * LANES)
        y = pick(select, x)
        dst[:, at] = y if extra is None else y + extra[:, at]


def sums_kernel(parts, length, got_ref, s_ref, near_ref, next_ref, select_ref, strip_ref):
    rows, wide = s_ref.shape
    cols = wide - LANES
    devices = got_ref.shape[0] // length
    base = 2 * SLOTS * parts
    from_left = [slot_rows(got_ref, length, base + k, devices) for k in range(SLOTS)]
    from_right = [slot_rows(got_ref, length, base + SLOTS + k, devices) for k in range(SLOTS)]
    left_t = [jnp.transpose(x) for x in from_left]
    right_t = [jnp.transpose(x) for x in from_right]
    wanted = (iota((rows, devices), 0) + 1).astype(F32)

    def chooser(lists, at):
        return jnp.concatenate(
            [jnp.where(x[at : at + 1, :] == wanted, 1.0, 0.0) for x in lists], axis=1
        ).astype(BF16)

    own = chooser(right_t, 97)
    select_ref[...] = own
    gather_tile(got_ref, parts, length, 0, own, s_ref, None)
    left = pick(chooser(left_t, 0), jnp.concatenate(from_left, axis=0))
    right = pick(chooser(right_t, 96), jnp.concatenate(from_right, axis=0))
    lane = iota((rows, LANES), 1)
    s_ref[:, cols:] = jnp.where(lane < 64, right, left)
    strip_ref[...] = jnp.where(lane < 64, pltpu.roll(right, 64, 1), pltpu.roll(left, 64, 1))
    to_partners(s_ref, near_ref, next_ref)


def weights_kernel(
    parts, length, n_tx, got_ref, prior_ref, prior_halo_ref, select_ref, strip_ref,
    w_ref
):
    rows, wide = w_ref.shape
    cols = wide - LANES
    gather_tile(got_ref, parts, length, 1, select_ref[...], w_ref, prior_ref)
    lane = iota((rows, LANES), 1)
    column = lax.axis_index(TX)
    has_left = jnp.where(column > 0, 1.0, 0.0)
    has_right = jnp.where(column < n_tx - 1, 1.0, 0.0)
    prior_halo = prior_halo_ref[...]
    strip = strip_ref[...]
    w_ref[:, cols:] = jnp.where(
        lane < HALF,
        prior_halo * has_right + strip,
        jnp.where(lane >= LANES - HALF, prior_halo * has_left + strip, 0.0),
    )


def along_columns(pieces, taps_ref):
    height, wide = pieces[0].shape
    cols = wide - LANES

    def stacked(x):
        first = jnp.concatenate([x[:, cols:], x[:, : 3 * LANES]], axis=1)
        rest = [
            x[:, (c - 1) * LANES : (c + 3) * LANES] for c in range(2, cols // LANES, 2)
        ]
        return jnp.concatenate([first] + rest, axis=0)

    half = [stacked(x) for x in pieces]
    out = []
    for r in range(0, half[0].shape[0], 2 * height):
        y = times_taps([x[r : r + 2 * height] for x in half], taps_ref)
        out += [y[:height], y[height:]]
    return out


def all_columns(mid, y0_ref, at, col_ref, edge_ref):
    wide = mid.shape[1]
    cols = wide - LANES
    pieces = split3(mid)
    for c, y in enumerate(along_columns(pieces, col_ref)):
        y0_ref[at, 2 * c * LANES : 2 * (c + 1) * LANES] = y
    near = [jnp.concatenate([x[:, cols - LANES :], x[:, :LANES]], axis=1) for x in pieces]
    y0_ref[at, cols:] = times_taps(near, edge_ref)


def early_kernel(
    s_ref,
    w_ref,
    own_ref,
    col_ref,
    edge_ref,
    part_ref,
    deep_ref,
    root_ref,
    r0_ref,
    sums_ref,
    near_ref,
    next_ref,
    mid_ref,
):
    rows, wide = s_ref.shape
    cols = wide - LANES
    edge = 4 * HALF
    to_partners(w_ref, near_ref, next_ref)
    for at in spans(wide):
        mid = taps_times(own_ref, s_ref[:, at])
        part_ref[:, at] = mid[:edge]
        mid_ref[:, at] = mid[edge:]
    all_columns(mid_ref[...], deep_ref, slice(None), col_ref, edge_ref)
    total_rr = total_rb = jnp.zeros((8, cols), F32)
    for r in range(0, rows, 8):
        at = slice(r, r + 8)
        root = jnp.sqrt(w_ref[at, :cols])
        s = s_ref[at, :cols]
        r0 = s / root
        root_ref[at, :] = root
        r0_ref[at, :] = r0
        total_rr += r0 * r0
        if HALF <= r < rows - HALF:
            total_rb += s * deep_ref[r - HALF : r - HALF + 8, :cols]
    sums_ref[0:8, :] = folded(total_rr)
    sums_ref[8:16, :] = folded(total_rb)


def first_kernel(
    n_ty,
    s_ref,
    near_ref,
    next_ref,
    part_ref,
    early_ref,
    halo_ref,
    col_ref,
    edge_ref,
    border_ref,
    sums_ref,
    mid_ref,
):
    rows, wide = s_ref.shape
    cols = wide - LANES
    for at in spans(wide):
        halo = jnp.concatenate(from_partners(n_ty, near_ref, next_ref, at), axis=0)
        mid_ref[:, at] = part_ref[:, at] + taps_times(halo_ref, halo)
    all_columns(mid_ref[...], border_ref, slice(None), col_ref, edge_ref)
    two = 2 * HALF
    top = s_ref[:HALF, :cols] * border_ref[HALF:two, :cols]
    bottom = s_ref[rows - HALF :, :cols] * border_ref[two : two + HALF, :cols]
    sums_ref[0:8, :] = early_ref[0:8, :]
    sums_ref[8:16, :] = early_ref[8:16, :] + folded(top) + folded(bottom)


def folded(total):
    rows, cols = total.shape
    total = sum(total[r : r + 8] for r in range(0, rows, 8))
    return sum(total[:, c : c + LANES] for c in range(0, cols, LANES))


def whole(total):
    return jnp.sum(jnp.sum(total, axis=0, keepdims=True), axis=1, keepdims=True)


def second_kernel(
    n_ty,
    w_ref,
    near_ref,
    next_ref,
    deep_ref,
    border_ref,
    root_ref,
    r0_ref,
    first_ref,
    row_ref,
    col_ref,
    b0_ref,
    b1_ref,
    moments_ref,
    mid_ref,
):
    rows, wide = w_ref.shape
    cols = wide - LANES
    one, two, three = HALF, 2 * HALF, 3 * HALF
    m0, n1 = whole(first_ref[0:8, :]), whole(first_ref[8:16, :])
    c0 = n1 / jnp.where(m0 > 0.0, m0, 1.0)
    for at in spans(wide):
        above, below = from_partners(n_ty, near_ref, next_ref, at)
        z = jnp.concatenate(
            [
                above * border_ref[:one, at],
                w_ref[:one, at] * border_ref[one:two, at],
                w_ref[one : rows - one, at] * deep_ref[:, at],
                w_ref[rows - one :, at] * border_ref[two:three, at],
                below * border_ref[three:, at],
            ],
            axis=0,
        )
        mid_ref[:, at] = taps_times(row_ref, z)
    total_vv = total_rv = total_vq = total_mix = jnp.zeros((8, LANES), F32)
    for c, y1 in enumerate(along_columns(split3(mid_ref[...]), col_ref)):
        at = slice(2 * c * LANES, 2 * (c + 1) * LANES)
        y0 = jnp.concatenate(
            [border_ref[one:two, at], deep_ref[:, at], border_ref[two:three, at]], axis=0
        )
        r0, root = r0_ref[:, at], root_ref[:, at]
        b0, b1 = root * y0, root * y1
        b0_ref[:, at] = b0
        b1_ref[:, at] = b1
        v, q = b0 - c0 * r0, b1 - c0 * b0
        total_vv += folded(v * v)
        total_rv += folded(r0 * v)
        total_vq += folded(v * q)
        total_mix += folded(v * b0 + r0 * q)
    lane = iota((1, LANES), 1)
    known = jnp.zeros((1, LANES), F32)
    totals = (whole(x) for x in (total_vv, total_rv, total_vq, total_mix))
    for i, value in enumerate((m0, n1, c0, *totals)):
        known = jnp.where(lane == i, value, known)
    moments_ref[...] = jnp.broadcast_to(known, moments_ref.shape)


def final_kernel(moments_ref, r0_ref, b0_ref, b1_ref, x_hbm, r_hbm, x_ref, r_ref, sem):
    parts = jnp.transpose(moments_ref[...])
    m0_at, n1_at, c_at, vv_at, rv_at, vq_at, mix_at = (parts[i : i + 1, :] for i in range(7))

    def total(x):
        return jnp.sum(x, axis=1, keepdims=True)

    m0, n1 = total(m0_at), total(n1_at)
    mu = n1 / m0
    shift = c_at - mu
    vv = total(vv_at + shift * (2.0 * rv_at + shift * m0_at))
    vbv = total(vq_at + shift * (mix_at + shift * n1_at))
    a = m0 / (0.5 * m0 + n1)
    ratio = vv / m0
    beta = a * a * ratio
    step = vv / (0.5 * vv + vbv - a * vv * ratio)
    x_r0 = a + step * beta + step * a * mu
    x_b0 = -step * a
    r_r0 = a * mu - step * (0.5 * a * mu + 0.5 * beta)
    r_b0 = -a - step * (a * mu - 0.5 * a + beta)
    r_b1 = step * a
    sends = []
    step_rows = r0_ref.shape[0] // CHUNKS
    for c in range(CHUNKS):
        at = slice(c * step_rows, (c + 1) * step_rows)
        r0 = r0_ref[at, :]
        b0 = b0_ref[at, :]
        x_ref[at, :] = x_r0 * r0 + x_b0 * b0
        r_ref[at, :] = r_r0 * r0 + r_b0 * b0 + r_b1 * b1_ref[at, :]
        for i, (src, dst) in enumerate(((x_ref, x_hbm), (r_ref, r_hbm))):
            send = pltpu.make_async_copy(src.at[at], dst.at[at], sem.at[c, i])
            send.start()
            sends.append(send)
    for send in sends:
        send.wait()


VMEM = pl.BlockSpec(memory_space=pltpu.VMEM)
ANY = pl.BlockSpec(memory_space=pl.ANY)
HBM = pl.BlockSpec(memory_space=pltpu.HBM)


def call(kernel, shapes, *args, ins=None, outs=None, scratch=(), name, limit=24, flops=0):
    moved = sum(int(np.prod(x.shape)) * x.dtype.itemsize for x in args)
    return pl.pallas_call(
        kernel,
        out_shape=[
            jax.ShapeDtypeStruct(s, F32) if isinstance(s, tuple) else s for s in shapes
        ],
        in_specs=ins or [VMEM] * len(args),
        out_specs=outs or [VMEM] * len(shapes),
        scratch_shapes=list(scratch),
        compiler_params=pltpu.CompilerParams(vmem_limit_bytes=limit << 20),
        cost_estimate=pl.CostEstimate(flops=flops, bytes_accessed=moved, transcendentals=0),
        name=name,
    )(*args)


def neighbours(axes, step):
    count = int(np.prod([lax.axis_size(a) for a in axes]))
    return [(i, (i + step) % count) for i in range(count)]


def shards(block_sums, block_weights, block_tile, block_row, prior_weight):
    devices = lax.axis_size(TY_TX)
    n_tx = lax.axis_size(TX)
    blocks, _, cols = block_sums.shape
    rows = prior_weight.shape[0]
    parts = cols // LANES
    length = 2 * SLOTS * parts + 2 * SLOTS
    wide = cols + LANES

    prior_right = lax.ppermute(prior_weight[:, :LANES], TX, neighbours(TX, -1))
    prior_left = lax.ppermute(prior_weight[:, cols - LANES :], TX, neighbours(TX, 1))
    lane = jnp.arange(LANES)[None, :]
    prior_halo = jnp.where(lane < HALF, prior_right, jnp.where(lane >= LANES - HALF, prior_left, 0.0))

    (message,) = call(
        functools.partial(pack_kernel, n_tx, parts, length),
        [(devices * length, LANES)],
        block_tile.reshape(1, blocks),
        block_row.reshape(1, blocks),
        block_sums.reshape(blocks * parts, LANES),
        block_weights.reshape(blocks * parts, LANES),
        ins=[HBM] * 4,
        outs=[HBM],
        scratch=[
            pltpu.VMEM((1, blocks), jnp.int32),
            pltpu.VMEM((1, blocks), jnp.int32),
            pltpu.VMEM((blocks * parts, LANES), F32),
            pltpu.VMEM((blocks * parts, LANES), F32),
            pltpu.VMEM((3, blocks, 2 * cols), BF16),
            pltpu.VMEM((devices * length, LANES), F32),
            pltpu.SemaphoreType.DMA((4,)),
            pltpu.SemaphoreType.DMA((GROUPS,)),
        ],
        name="pack",
        limit=63,
    )
    got = lax.all_to_all(
        message.reshape(devices, 1, length * LANES), TY_TX, split_axis=0, concat_axis=0, tiled=True
    ).reshape(devices * length, LANES)
    s_slab, w_slab = (2 * HALF, wide), (HALF, wide)
    s, s_near, s_next, chosen, strip = call(
        functools.partial(sums_kernel, parts, length),
        [
            (rows, wide),
            s_slab,
            s_slab,
            jax.ShapeDtypeStruct((rows, SLOTS * devices), BF16),
            (rows, LANES),
        ],
        got,
        flops=3 * 2 * rows * wide * SLOTS * devices,
        name="sums",
    )
    (w,) = call(
        functools.partial(weights_kernel, parts, length, n_tx),
        [(rows, wide)],
        got,
        prior_weight,
        prior_halo,
        chosen,
        strip,
        flops=3 * 2 * rows * wide * SLOTS * devices,
        name="weights",
    )
    n_ty = lax.axis_size("ty")
    swaps = [(i, i ^ 1) for i in range(n_ty)]
    far = [((i + 1) % n_ty, ((i ^ 1) + 1) % n_ty) for i in range(n_ty)]
    s_near, s_next = lax.ppermute(s_near, "ty", swaps), lax.ppermute(s_next, "ty", far)

    tall = rows + 2 * HALF
    col_taps = taps(np.arange(2 * LANES)[None, :] - np.arange(4 * LANES)[:, None] + LANES, 0)
    ring = np.where(np.arange(LANES) < 64, cols, -LANES) + np.arange(LANES)
    near = np.concatenate([np.arange(cols - LANES, cols), ring, np.arange(LANES)])
    edge_taps = taps(ring[None, :] - near[:, None], 0)
    tile = (rows, cols)
    inside = np.arange(rows)
    border_rows = np.concatenate(
        [np.arange(-HALF, HALF), np.arange(rows - HALF, rows + HALF)]
    )
    early_rows = np.concatenate([border_rows, inside[HALF : rows - HALF]])
    far_rows = np.concatenate([np.arange(-2 * HALF, 0), np.arange(rows, rows + 2 * HALF)])
    early_taps = taps(early_rows[:, None] - inside[None, :], 0)
    first_taps = taps(border_rows[:, None] - far_rows[None, :], 0)
    part, deep, root, r0, early, w_near, w_next = call(
        early_kernel,
        [(4 * HALF, wide), (rows - 2 * HALF, wide), tile, tile, (16, LANES), w_slab, w_slab],
        s,
        w,
        early_taps,
        col_taps,
        edge_taps,
        scratch=[pltpu.VMEM((rows - 2 * HALF, wide), F32)],
        flops=5 * 2 * tall * wide * 3 * LANES,
        name="early",
    )
    w_near, w_next = lax.ppermute(w_near, "ty", swaps), lax.ppermute(w_next, "ty", far)
    border, early = call(
        functools.partial(first_kernel, n_ty),
        [(4 * HALF, wide), (16, LANES)],
        s,
        s_near,
        s_next,
        part,
        early,
        first_taps,
        col_taps,
        edge_taps,
        scratch=[pltpu.VMEM((4 * HALF, wide), F32)],
        flops=5 * 2 * rows * wide * 6 * LANES,
        name="first",
    )
    second_taps = taps(inside[:, None] - np.arange(-HALF, rows + HALF)[None, :], 0)
    b0, b1, moments = call(
        functools.partial(second_kernel, n_ty),
        [tile, tile, (devices, LANES)],
        w,
        w_near,
        w_next,
        deep,
        border,
        root,
        r0,
        early,
        second_taps,
        col_taps,
        scratch=[pltpu.VMEM((rows, wide), F32)],
        flops=5 * 2 * rows * wide * 6 * LANES,
        name="second",
    )
    moments = lax.all_to_all(
        moments.reshape(devices, 1, LANES), TY_TX, split_axis=0, concat_axis=0, tiled=True
    ).reshape(devices, LANES)
    return tuple(
        call(
            final_kernel,
            [tile, tile],
            moments,
            r0,
            b0,
            b1,
            outs=[HBM, HBM],
            scratch=[
                pltpu.VMEM(tile, F32),
                pltpu.VMEM(tile, F32),
                pltpu.SemaphoreType.DMA((CHUNKS, 2)),
            ],
            name="combine",
        )
    )


def solution(mesh):
    split = Mesh(mesh.devices.reshape(mesh.shape["ty"], 4, 4, 2), ("ty", "tx_0", "tx_1", "tx_2"))
    in_specs = (P(TY_TX, None, None), P(TY_TX, None, None), P(TY_TX, None), P(TY_TX), P("ty", TX))
    out_specs = (P("ty", TX), P("ty", TX))
    return jax.shard_map(
        shards, mesh=split, in_specs=in_specs, out_specs=out_specs, check_vma=False
    )
```

```python
import functools

import jax
import jax.numpy as jnp
import numpy as np
from jax import lax
from jax.experimental import pallas as pl
from jax.experimental.pallas import tpu as pltpu
from jax.sharding import Mesh
from jax.sharding import PartitionSpec as P

HALF = 32
LANES = 128
SLOTS = 2
GROUPS = 2
CHUNKS = 4
TY_TX = ("ty", "tx_0", "tx_1", "tx_2")
TX = ("tx_0", "tx_1", "tx_2")
F32 = jnp.float32
BF16 = jnp.bfloat16


def taps(offset, axis):
    def raw(d):
        scaled = np.abs(d) / (HALF + 1.0)
        return np.where(np.abs(d) <= HALF, (1.0 - scaled) ** 4 * (1.0 + 4.0 * scaled), 0.0)

    values = raw(offset) / raw(np.arange(-HALF, HALF + 1)).sum()
    head = values.astype(BF16)
    tail = (values - head.astype(np.float64)).astype(BF16)
    return jnp.asarray(np.concatenate([head, tail], axis=axis))


def split3(x):
    head = x.astype(BF16)
    rest = x - head.astype(F32)
    mid = rest.astype(BF16)
    return head, mid, (rest - mid.astype(F32)).astype(BF16)


def mm(a, b):
    return jnp.dot(a, b, preferred_element_type=F32)


def pick(select, x):
    head, mid, tail = split3(x)
    return mm(select, tail) + mm(select, mid) + mm(select, head)


def taps_times(taps_ref, x):
    rows = taps_ref.shape[0] // 2
    xh, xm, xl = split3(x)
    low = mm(taps_ref[:rows, :], xl)
    mid = mm(taps_ref[...], xm)
    high = mm(taps_ref[...], xh)
    return low + mid[rows:] + high[rows:] + mid[:rows] + high[:rows]


def times_taps(pieces, taps_ref):
    xh, xm, xl = pieces
    depth = taps_ref.shape[0] // 2
    head, tail = taps_ref[:depth, :], taps_ref[depth:, :]
    return mm(xl, head) + mm(xm, tail) + mm(xh, tail) + mm(xm, head) + mm(xh, head)


def spans(wide):
    cols = wide - LANES
    return [slice(c, c + 2 * LANES) for c in range(0, cols, 2 * LANES)] + [slice(cols, wide)]


def iota(shape, dim):
    return lax.broadcasted_iota(jnp.int32, shape, dim)


def pack_kernel(
    n_tx, parts, length, tile_hbm, row_hbm, sums_hbm, weights_hbm, out_hbm,
    tile_ref, row_ref, sums_ref, weights_ref, split_ref, out_ref, in_sem, out_sem
):
    fetches = [
        pltpu.make_async_copy(src, dst, in_sem.at[i])
        for i, (src, dst) in enumerate(
            (
                (tile_hbm, tile_ref),
                (row_hbm, row_ref),
                (sums_hbm, sums_ref),
                (weights_hbm, weights_ref),
            )
        )
    ]
    for fetch in fetches:
        fetch.start()
    fetches[0].wait()
    fetches[1].wait()
    count = tile_ref.shape[1]
    devices = out_ref.shape[0] // length
    group = devices // GROUPS
    tile = tile_ref[...]
    t = iota((devices, count), 0)
    same = tile == t
    earlier = iota((count, count), 0) < iota((count, count), 1)
    before = mm(same.astype(F32).astype(BF16), earlier.astype(F32).astype(BF16))
    rank = jnp.sum(jnp.where(same, before, 0.0), axis=0, keepdims=True)
    column = lax.rem(t, n_tx)
    from_left = (tile + 1 == t) & (column != 0)
    from_right = (tile - 1 == t) & (column != n_tx - 1)

    def onehot(mask, k):
        return jnp.where(mask & (rank == float(k)), 1.0, 0.0)

    own = [onehot(same, k) for k in range(SLOTS)]
    left = [onehot(from_left, k) for k in range(SLOTS)]
    right = [
        jnp.concatenate([onehot(from_right, k), own[k]], axis=1) for k in range(SLOTS)
    ]

    def of_group(masks, g):
        part = slice(g * group, (g + 1) * group)
        return jnp.concatenate([m[part] for m in masks], axis=0).astype(BF16)

    lane = iota((count, LANES), 1)
    number = jnp.transpose(jnp.broadcast_to(row_ref[...].astype(F32) + 1.0, (count, count)))
    for which, ref in enumerate((sums_ref, weights_ref)):
        fetches[2 + which].wait()
        for c in range(parts):
            at = slice((which * parts + c) * LANES, (which * parts + c + 1) * LANES)
            for i, piece in enumerate(split3(ref[pl.ds(c, count, stride=parts), :])):
                split_ref[i, :, at] = piece

    last = parts - 1
    s_last = sums_ref[pl.ds(last, count, stride=parts), :]
    w_last = pltpu.roll(weights_ref[pl.ds(last, count, stride=parts), :], 64, 1)
    s_first = sums_ref[pl.ds(0, count, stride=parts), :]
    w_first = pltpu.roll(weights_ref[pl.ds(0, count, stride=parts), :], 64, 1)
    left_rows = jnp.where(
        lane >= 64, s_last, jnp.where(lane >= 32, w_last, jnp.where(lane == 0, number, 0.0))
    )
    right_rows = jnp.where(
        lane < 64, s_first, jnp.where(lane < 96, w_first, jnp.where(lane == 96, number, 0.0))
    )
    own_rows = jnp.where(lane == 97, number, 0.0)
    both_rows = jnp.concatenate([right_rows, own_rows], axis=0)

    base = 2 * SLOTS * parts
    sends = []
    for g in range(GROUPS):
        first = g * group * length
        own_all = of_group(own, g)
        for c in range(0, 2 * parts, 2):
            at = slice(c * LANES, (c + 2) * LANES)
            y = (
                mm(own_all, split_ref[2, :, at])
                + mm(own_all, split_ref[1, :, at])
                + mm(own_all, split_ref[0, :, at])
            )
            which, chunk = divmod(c, parts)
            for k in range(SLOTS):
                for i in range(2):
                    to = first + (which * SLOTS + k) * parts + chunk + i
                    out_ref[pl.ds(to, group, stride=length), :] = y[
                        k * group : (k + 1) * group, i * LANES : (i + 1) * LANES
                    ]
        to_left = pick(of_group(left, g), left_rows)
        to_right = pick(of_group(right, g), both_rows)
        for k in range(SLOTS):
            part = slice(k * group, (k + 1) * group)
            out_ref[pl.ds(first + base + k, group, stride=length), :] = to_left[part]
            out_ref[pl.ds(first + base + SLOTS + k, group, stride=length), :] = to_right[part]
        span = pl.ds(first, group * length)
        send = pltpu.make_async_copy(out_ref.at[span], out_hbm.at[span], out_sem.at[g])
        send.start()
        sends.append(send)
    for send in sends:
        send.wait()


def slot_rows(got_ref, length, at, devices):
    return got_ref[pl.ds(at, devices, stride=length), :]


def odd_row():
    return lax.rem(lax.axis_index("ty") + 1 - lax.axis_index("tx_2"), 2)


def to_partners(ref, near_ref, next_ref):
    rows, count = ref.shape[0], near_ref.shape[0]
    bottom = (rows - count) * (1 - odd_row())
    near_ref[...] = ref[pl.ds(pl.multiple_of(bottom, 8), count), :]
    next_ref[...] = ref[pl.ds(pl.multiple_of(rows - count - bottom, 8), count), :]


def from_partners(n_ty, near_ref, next_ref, at):
    row_at, odd = lax.axis_index("ty"), odd_row() == 1
    near, far = near_ref[:, at], next_ref[:, at]
    above = jnp.where(odd, near, far) * jnp.where(row_at > 0, 1.0, 0.0)
    below = jnp.where(odd, far, near) * jnp.where(row_at < n_ty - 1, 1.0, 0.0)
    return above, below


def gather_tile(got_ref, parts, length, which, select, dst, extra):
    devices = got_ref.shape[0] // length
    for c in range(0, parts, 2):
        x = jnp.concatenate(
            [
                jnp.concatenate(
                    [
                        slot_rows(got_ref, length, (which * SLOTS + k) * parts + c + i, devices)
                        for i in range(2)
                    ],
                    axis=1,
                )
                for k in range(SLOTS)
            ],
            axis=0,
        )
        at = slice(c * LANES, (c + 2) * LANES)
        y = pick(select, x)
        dst[:, at] = y if extra is None else y + extra[:, at]


def sums_kernel(parts, length, got_ref, s_ref, near_ref, next_ref, select_ref, strip_ref):
    rows, wide = s_ref.shape
    cols = wide - LANES
    devices = got_ref.shape[0] // length
    base = 2 * SLOTS * parts
    from_left = [slot_rows(got_ref, length, base + k, devices) for k in range(SLOTS)]
    from_right = [slot_rows(got_ref, length, base + SLOTS + k, devices) for k in range(SLOTS)]
    left_t = [jnp.transpose(x) for x in from_left]
    right_t = [jnp.transpose(x) for x in from_right]
    wanted = (iota((rows, devices), 0) + 1).astype(F32)

    def chooser(lists, at):
        return jnp.concatenate(
            [jnp.where(x[at : at + 1, :] == wanted, 1.0, 0.0) for x in lists], axis=1
        ).astype(BF16)

    own = chooser(right_t, 97)
    select_ref[...] = own
    gather_tile(got_ref, parts, length, 0, own, s_ref, None)
    left = pick(chooser(left_t, 0), jnp.concatenate(from_left, axis=0))
    right = pick(chooser(right_t, 96), jnp.concatenate(from_right, axis=0))
    lane = iota((rows, LANES), 1)
    s_ref[:, cols:] = jnp.where(lane < 64, right, left)
    strip_ref[...] = jnp.where(lane < 64, pltpu.roll(right, 64, 1), pltpu.roll(left, 64, 1))
    to_partners(s_ref, near_ref, next_ref)


def weights_kernel(
    parts, length, n_tx, got_ref, prior_ref, prior_halo_ref, select_ref, strip_ref,
    w_ref
):
    rows, wide = w_ref.shape
    cols = wide - LANES
    gather_tile(got_ref, parts, length, 1, select_ref[...], w_ref, prior_ref)
    lane = iota((rows, LANES), 1)
    column = lax.axis_index(TX)
    has_left = jnp.where(column > 0, 1.0, 0.0)
    has_right = jnp.where(column < n_tx - 1, 1.0, 0.0)
    prior_halo = prior_halo_ref[...]
    strip = strip_ref[...]
    w_ref[:, cols:] = jnp.where(
        lane < HALF,
        prior_halo * has_right + strip,
        jnp.where(lane >= LANES - HALF, prior_halo * has_left + strip, 0.0),
    )


def along_columns(pieces, taps_ref):
    height, wide = pieces[0].shape
    cols = wide - LANES

    def stacked(x):
        first = jnp.concatenate([x[:, cols:], x[:, : 3 * LANES]], axis=1)
        rest = [
            x[:, (c - 1) * LANES : (c + 3) * LANES] for c in range(2, cols // LANES, 2)
        ]
        return jnp.concatenate([first] + rest, axis=0)

    half = [stacked(x) for x in pieces]
    out = []
    for r in range(0, half[0].shape[0], 2 * height):
        y = times_taps([x[r : r + 2 * height] for x in half], taps_ref)
        out += [y[:height], y[height:]]
    return out


def all_columns(mid, y0_ref, at, col_ref, edge_ref):
    wide = mid.shape[1]
    cols = wide - LANES
    pieces = split3(mid)
    for c, y in enumerate(along_columns(pieces, col_ref)):
        y0_ref[at, 2 * c * LANES : 2 * (c + 1) * LANES] = y
    near = [jnp.concatenate([x[:, cols - LANES :], x[:, :LANES]], axis=1) for x in pieces]
    y0_ref[at, cols:] = times_taps(near, edge_ref)


def early_kernel(
    s_ref,
    w_ref,
    own_ref,
    col_ref,
    edge_ref,
    part_ref,
    deep_ref,
    root_ref,
    r0_ref,
    sums_ref,
    near_ref,
    next_ref,
    mid_ref,
):
    rows, wide = s_ref.shape
    cols = wide - LANES
    edge = 4 * HALF
    to_partners(w_ref, near_ref, next_ref)
    for at in spans(wide):
        mid = taps_times(own_ref, s_ref[:, at])
        part_ref[:, at] = mid[:edge]
        mid_ref[:, at] = mid[edge:]
    all_columns(mid_ref[...], deep_ref, slice(None), col_ref, edge_ref)
    total_rr = total_rb = jnp.zeros((8, cols), F32)
    for r in range(0, rows, 8):
        at = slice(r, r + 8)
        root = jnp.sqrt(w_ref[at, :cols])
        s = s_ref[at, :cols]
        r0 = s / root
        root_ref[at, :] = root
        r0_ref[at, :] = r0
        total_rr += r0 * r0
        if HALF <= r < rows - HALF:
            total_rb += s * deep_ref[r - HALF : r - HALF + 8, :cols]
    sums_ref[0:8, :] = folded(total_rr)
    sums_ref[8:16, :] = folded(total_rb)


def first_kernel(
    n_ty,
    s_ref,
    near_ref,
    next_ref,
    part_ref,
    early_ref,
    halo_ref,
    col_ref,
    edge_ref,
    border_ref,
    sums_ref,
    mid_ref,
):
    rows, wide = s_ref.shape
    cols = wide - LANES
    for at in spans(wide):
        halo = jnp.concatenate(from_partners(n_ty, near_ref, next_ref, at), axis=0)
        mid_ref[:, at] = part_ref[:, at] + taps_times(halo_ref, halo)
    all_columns(mid_ref[...], border_ref, slice(None), col_ref, edge_ref)
    two = 2 * HALF
    top = s_ref[:HALF, :cols] * border_ref[HALF:two, :cols]
    bottom = s_ref[rows - HALF :, :cols] * border_ref[two : two + HALF, :cols]
    sums_ref[0:8, :] = early_ref[0:8, :]
    sums_ref[8:16, :] = early_ref[8:16, :] + folded(top) + folded(bottom)


def folded(total):
    rows, cols = total.shape
    total = sum(total[r : r + 8] for r in range(0, rows, 8))
    return sum(total[:, c : c + LANES] for c in range(0, cols, LANES))


def whole(total):
    return jnp.sum(jnp.sum(total, axis=0, keepdims=True), axis=1, keepdims=True)


def second_kernel(
    n_ty,
    w_ref,
    near_ref,
    next_ref,
    deep_ref,
    border_ref,
    root_ref,
    r0_ref,
    first_ref,
    row_ref,
    col_ref,
    b0_ref,
    b1_ref,
    moments_ref,
    mid_ref,
):
    rows, wide = w_ref.shape
    cols = wide - LANES
    one, two, three = HALF, 2 * HALF, 3 * HALF
    m0, n1 = whole(first_ref[0:8, :]), whole(first_ref[8:16, :])
    c0 = n1 / jnp.where(m0 > 0.0, m0, 1.0)
    for at in spans(wide):
        above, below = from_partners(n_ty, near_ref, next_ref, at)
        z = jnp.concatenate(
            [
                above * border_ref[:one, at],
                w_ref[:one, at] * border_ref[one:two, at],
                w_ref[one : rows - one, at] * deep_ref[:, at],
                w_ref[rows - one :, at] * border_ref[two:three, at],
                below * border_ref[three:, at],
            ],
            axis=0,
        )
        mid_ref[:, at] = taps_times(row_ref, z)
    total_vv = total_rv = total_vq = total_mix = jnp.zeros((8, LANES), F32)
    for c, y1 in enumerate(along_columns(split3(mid_ref[...]), col_ref)):
        at = slice(2 * c * LANES, 2 * (c + 1) * LANES)
        y0 = jnp.concatenate(
            [border_ref[one:two, at], deep_ref[:, at], border_ref[two:three, at]], axis=0
        )
        r0, root = r0_ref[:, at], root_ref[:, at]
        b0, b1 = root * y0, root * y1
        b0_ref[:, at] = b0
        b1_ref[:, at] = b1
        v, q = b0 - c0 * r0, b1 - c0 * b0
        total_vv += folded(v * v)
        total_rv += folded(r0 * v)
        total_vq += folded(v * q)
        total_mix += folded(v * b0 + r0 * q)
    lane = iota((1, LANES), 1)
    known = jnp.zeros((1, LANES), F32)
    totals = (whole(x) for x in (total_vv, total_rv, total_vq, total_mix))
    for i, value in enumerate((m0, n1, c0, *totals)):
        known = jnp.where(lane == i, value, known)
    moments_ref[...] = jnp.broadcast_to(known, moments_ref.shape)


def final_kernel(moments_ref, r0_ref, b0_ref, b1_ref, x_hbm, r_hbm, x_ref, r_ref, sem):
    parts = jnp.transpose(moments_ref[...])
    m0_at, n1_at, c_at, vv_at, rv_at, vq_at, mix_at = (parts[i : i + 1, :] for i in range(7))

    def total(x):
        return jnp.sum(x, axis=1, keepdims=True)

    m0, n1 = total(m0_at), total(n1_at)
    mu = n1 / m0
    shift = c_at - mu
    vv = total(vv_at + shift * (2.0 * rv_at + shift * m0_at))
    vbv = total(vq_at + shift * (mix_at + shift * n1_at))
    a = m0 / (0.5 * m0 + n1)
    ratio = vv / m0
    beta = a * a * ratio
    step = vv / (0.5 * vv + vbv - a * vv * ratio)
    x_r0 = a + step * beta + step * a * mu
    x_b0 = -step * a
    r_r0 = a * mu - step * (0.5 * a * mu + 0.5 * beta)
    r_b0 = -a - step * (a * mu - 0.5 * a + beta)
    r_b1 = step * a
    sends = []
    step_rows = r0_ref.shape[0] // CHUNKS
    for c in range(CHUNKS):
        at = slice(c * step_rows, (c + 1) * step_rows)
        r0 = r0_ref[at, :]
        b0 = b0_ref[at, :]
        x_ref[at, :] = x_r0 * r0 + x_b0 * b0
        r_ref[at, :] = r_r0 * r0 + r_b0 * b0 + r_b1 * b1_ref[at, :]
        for i, (src, dst) in enumerate(((x_ref, x_hbm), (r_ref, r_hbm))):
            send = pltpu.make_async_copy(src.at[at], dst.at[at], sem.at[c, i])
            send.start()
            sends.append(send)
    for send in sends:
        send.wait()


VMEM = pl.BlockSpec(memory_space=pltpu.VMEM)
ANY = pl.BlockSpec(memory_space=pl.ANY)
HBM = pl.BlockSpec(memory_space=pltpu.HBM)


def call(kernel, shapes, *args, ins=None, outs=None, scratch=(), name, limit=24, flops=0):
    moved = sum(int(np.prod(x.shape)) * x.dtype.itemsize for x in args)
    return pl.pallas_call(
        kernel,
        out_shape=[
            jax.ShapeDtypeStruct(s, F32) if isinstance(s, tuple) else s for s in shapes
        ],
        in_specs=ins or [VMEM] * len(args),
        out_specs=outs or [VMEM] * len(shapes),
        scratch_shapes=list(scratch),
        compiler_params=pltpu.CompilerParams(vmem_limit_bytes=limit << 20),
        cost_estimate=pl.CostEstimate(flops=flops, bytes_accessed=moved, transcendentals=0),
        name=name,
    )(*args)


def neighbours(axes, step):
    count = int(np.prod([lax.axis_size(a) for a in axes]))
    return [(i, (i + step) % count) for i in range(count)]


def shards(block_sums, block_weights, block_tile, block_row, prior_weight):
    devices = lax.axis_size(TY_TX)
    n_tx = lax.axis_size(TX)
    blocks, _, cols = block_sums.shape
    rows = prior_weight.shape[0]
    parts = cols // LANES
    length = 2 * SLOTS * parts + 2 * SLOTS
    wide = cols + LANES

    prior_right = lax.ppermute(prior_weight[:, :LANES], TX, neighbours(TX, -1))
    prior_left = lax.ppermute(prior_weight[:, cols - LANES :], TX, neighbours(TX, 1))
    lane = jnp.arange(LANES)[None, :]
    prior_halo = jnp.where(lane < HALF, prior_right, jnp.where(lane >= LANES - HALF, prior_left, 0.0))

    (message,) = call(
        functools.partial(pack_kernel, n_tx, parts, length),
        [(devices * length, LANES)],
        block_tile.reshape(1, blocks),
        block_row.reshape(1, blocks),
        block_sums.reshape(blocks * parts, LANES),
        block_weights.reshape(blocks * parts, LANES),
        ins=[HBM] * 4,
        outs=[HBM],
        scratch=[
            pltpu.VMEM((1, blocks), jnp.int32),
            pltpu.VMEM((1, blocks), jnp.int32),
            pltpu.VMEM((blocks * parts, LANES), F32),
            pltpu.VMEM((blocks * parts, LANES), F32),
            pltpu.VMEM((3, blocks, 2 * cols), BF16),
            pltpu.VMEM((devices * length, LANES), F32),
            pltpu.SemaphoreType.DMA((4,)),
            pltpu.SemaphoreType.DMA((GROUPS,)),
        ],
        name="pack",
        limit=63,
    )
    got = lax.all_to_all(
        message.reshape(devices, 1, length * LANES), TY_TX, split_axis=0, concat_axis=0, tiled=True
    ).reshape(devices * length, LANES)
    s_slab, w_slab = (2 * HALF, wide), (HALF, wide)
    s, s_near, s_next, chosen, strip = call(
        functools.partial(sums_kernel, parts, length),
        [
            (rows, wide),
            s_slab,
            s_slab,
            jax.ShapeDtypeStruct((rows, SLOTS * devices), BF16),
            (rows, LANES),
        ],
        got,
        flops=3 * 2 * rows * wide * SLOTS * devices,
        name="sums",
    )
    (w,) = call(
        functools.partial(weights_kernel, parts, length, n_tx),
        [(rows, wide)],
        got,
        prior_weight,
        prior_halo,
        chosen,
        strip,
        flops=3 * 2 * rows * wide * SLOTS * devices,
        name="weights",
    )
    n_ty = lax.axis_size("ty")
    swaps = [(i, i ^ 1) for i in range(n_ty)]
    others = [((i + 1) % n_ty, ((i ^ 1) + 1) % n_ty) for i in range(n_ty)]
    columns = ("ty", "tx_2")

    def in_turn(first_core, second_core):
        return [(2 * a, 2 * b) for a, b in first_core] + [
            (2 * a + 1, 2 * b + 1) for a, b in second_core
        ]

    near, far = in_turn(others, swaps), in_turn(swaps, others)
    s_near, s_next = lax.ppermute(s_near, columns, near), lax.ppermute(s_next, columns, far)

    tall = rows + 2 * HALF
    col_taps = taps(np.arange(2 * LANES)[None, :] - np.arange(4 * LANES)[:, None] + LANES, 0)
    ring = np.where(np.arange(LANES) < 64, cols, -LANES) + np.arange(LANES)
    beside = np.concatenate([np.arange(cols - LANES, cols), ring, np.arange(LANES)])
    edge_taps = taps(ring[None, :] - beside[:, None], 0)
    tile = (rows, cols)
    inside = np.arange(rows)
    border_rows = np.concatenate(
        [np.arange(-HALF, HALF), np.arange(rows - HALF, rows + HALF)]
    )
    early_rows = np.concatenate([border_rows, inside[HALF : rows - HALF]])
    far_rows = np.concatenate([np.arange(-2 * HALF, 0), np.arange(rows, rows + 2 * HALF)])
    early_taps = taps(early_rows[:, None] - inside[None, :], 0)
    first_taps = taps(border_rows[:, None] - far_rows[None, :], 0)
    part, deep, root, r0, early, w_near, w_next = call(
        early_kernel,
        [(4 * HALF, wide), (rows - 2 * HALF, wide), tile, tile, (16, LANES), w_slab, w_slab],
        s,
        w,
        early_taps,
        col_taps,
        edge_taps,
        scratch=[pltpu.VMEM((rows - 2 * HALF, wide), F32)],
        flops=5 * 2 * tall * wide * 3 * LANES,
        name="early",
    )
    w_near, w_next = lax.ppermute(w_near, columns, near), lax.ppermute(w_next, columns, far)
    border, early = call(
        functools.partial(first_kernel, n_ty),
        [(4 * HALF, wide), (16, LANES)],
        s,
        s_near,
        s_next,
        part,
        early,
        first_taps,
        col_taps,
        edge_taps,
        scratch=[pltpu.VMEM((4 * HALF, wide), F32)],
        flops=5 * 2 * rows * wide * 6 * LANES,
        name="first",
    )
    second_taps = taps(inside[:, None] - np.arange(-HALF, rows + HALF)[None, :], 0)
    b0, b1, moments = call(
        functools.partial(second_kernel, n_ty),
        [tile, tile, (devices, LANES)],
        w,
        w_near,
        w_next,
        deep,
        border,
        root,
        r0,
        early,
        second_taps,
        col_taps,
        scratch=[pltpu.VMEM((rows, wide), F32)],
        flops=5 * 2 * rows * wide * 6 * LANES,
        name="second",
    )
    moments = lax.all_to_all(
        moments.reshape(devices, 1, LANES), TY_TX, split_axis=0, concat_axis=0, tiled=True
    ).reshape(devices, LANES)
    return tuple(
        call(
            final_kernel,
            [tile, tile],
            moments,
            r0,
            b0,
            b1,
            outs=[HBM, HBM],
            scratch=[
                pltpu.VMEM(tile, F32),
                pltpu.VMEM(tile, F32),
                pltpu.SemaphoreType.DMA((CHUNKS, 2)),
            ],
            name="combine",
        )
    )


def solution(mesh):
    split = Mesh(mesh.devices.reshape(mesh.shape["ty"], 4, 4, 2), ("ty", "tx_0", "tx_1", "tx_2"))
    in_specs = (P(TY_TX, None, None), P(TY_TX, None, None), P(TY_TX, None), P(TY_TX), P("ty", TX))
    out_specs = (P("ty", TX), P("ty", TX))
    return jax.shard_map(
        shards, mesh=split, in_specs=in_specs, out_specs=out_specs, check_vma=False
    )
```

```python
import functools

import jax
import jax.numpy as jnp
import numpy as np
from jax import lax
from jax.experimental import pallas as pl
from jax.experimental.pallas import tpu as pltpu
from jax.sharding import Mesh
from jax.sharding import PartitionSpec as P

HALF = 32
LANES = 128
SLOTS = 2
GROUPS = 2
CHUNKS = 4
TY_TX = ("ty", "tx_0", "tx_1", "tx_2")
TX = ("tx_0", "tx_1", "tx_2")
F32 = jnp.float32
BF16 = jnp.bfloat16


def taps(offset, axis):
    def raw(d):
        scaled = np.abs(d) / (HALF + 1.0)
        return np.where(np.abs(d) <= HALF, (1.0 - scaled) ** 4 * (1.0 + 4.0 * scaled), 0.0)

    values = raw(offset) / raw(np.arange(-HALF, HALF + 1)).sum()
    head = values.astype(BF16)
    tail = (values - head.astype(np.float64)).astype(BF16)
    return jnp.asarray(np.concatenate([head, tail], axis=axis))


def split3(x):
    head = x.astype(BF16)
    rest = x - head.astype(F32)
    mid = rest.astype(BF16)
    return head, mid, (rest - mid.astype(F32)).astype(BF16)


def mm(a, b):
    return jnp.dot(a, b, preferred_element_type=F32)


def pick(select, x):
    head, mid, tail = split3(x)
    return mm(select, tail) + mm(select, mid) + mm(select, head)


def taps_times(taps_ref, x):
    rows = taps_ref.shape[0] // 2
    xh, xm, xl = split3(x)
    low = mm(taps_ref[:rows, :], xl)
    mid = mm(taps_ref[...], xm)
    high = mm(taps_ref[...], xh)
    return low + mid[rows:] + high[rows:] + mid[:rows] + high[:rows]


def times_taps(pieces, taps_ref):
    xh, xm, xl = pieces
    depth = taps_ref.shape[0] // 2
    head, tail = taps_ref[:depth, :], taps_ref[depth:, :]
    return mm(xl, head) + mm(xm, tail) + mm(xh, tail) + mm(xm, head) + mm(xh, head)


def spans(wide):
    cols = wide - LANES
    return [slice(c, c + 2 * LANES) for c in range(0, cols, 2 * LANES)] + [slice(cols, wide)]


def iota(shape, dim):
    return lax.broadcasted_iota(jnp.int32, shape, dim)


def pack_kernel(
    n_tx, parts, length, tile_hbm, row_hbm, sums_hbm, weights_hbm, out_hbm,
    tile_ref, row_ref, sums_ref, weights_ref, split_ref, out_ref, in_sem, out_sem
):
    fetches = [
        pltpu.make_async_copy(src, dst, in_sem.at[i])
        for i, (src, dst) in enumerate(
            (
                (tile_hbm, tile_ref),
                (row_hbm, row_ref),
                (sums_hbm, sums_ref),
                (weights_hbm, weights_ref),
            )
        )
    ]
    for fetch in fetches:
        fetch.start()
    fetches[0].wait()
    fetches[1].wait()
    count = tile_ref.shape[1]
    devices = out_ref.shape[0] // length
    group = devices // GROUPS
    tile = tile_ref[...]
    t = iota((devices, count), 0)
    same = tile == t
    earlier = iota((count, count), 0) < iota((count, count), 1)
    before = mm(same.astype(F32).astype(BF16), earlier.astype(F32).astype(BF16))
    rank = jnp.sum(jnp.where(same, before, 0.0), axis=0, keepdims=True)
    column = lax.rem(t, n_tx)
    from_left = (tile + 1 == t) & (column != 0)
    from_right = (tile - 1 == t) & (column != n_tx - 1)

    def onehot(mask, k):
        return jnp.where(mask & (rank == float(k)), 1.0, 0.0)

    own = [onehot(same, k) for k in range(SLOTS)]
    left = [onehot(from_left, k) for k in range(SLOTS)]
    right = [
        jnp.concatenate([onehot(from_right, k), own[k]], axis=1) for k in range(SLOTS)
    ]

    def of_group(masks, g):
        part = slice(g * group, (g + 1) * group)
        return jnp.concatenate([m[part] for m in masks], axis=0).astype(BF16)

    lane = iota((count, LANES), 1)
    number = jnp.transpose(jnp.broadcast_to(row_ref[...].astype(F32) + 1.0, (count, count)))
    for which, ref in enumerate((sums_ref, weights_ref)):
        fetches[2 + which].wait()
        for c in range(parts):
            at = slice((which * parts + c) * LANES, (which * parts + c + 1) * LANES)
            for i, piece in enumerate(split3(ref[pl.ds(c, count, stride=parts), :])):
                split_ref[i, :, at] = piece

    last = parts - 1
    s_last = sums_ref[pl.ds(last, count, stride=parts), :]
    w_last = pltpu.roll(weights_ref[pl.ds(last, count, stride=parts), :], 64, 1)
    s_first = sums_ref[pl.ds(0, count, stride=parts), :]
    w_first = pltpu.roll(weights_ref[pl.ds(0, count, stride=parts), :], 64, 1)
    left_rows = jnp.where(
        lane >= 64, s_last, jnp.where(lane >= 32, w_last, jnp.where(lane == 0, number, 0.0))
    )
    right_rows = jnp.where(
        lane < 64, s_first, jnp.where(lane < 96, w_first, jnp.where(lane == 96, number, 0.0))
    )
    own_rows = jnp.where(lane == 97, number, 0.0)
    both_rows = jnp.concatenate([right_rows, own_rows], axis=0)

    base = 2 * SLOTS * parts
    sends = []
    for g in range(GROUPS):
        first = g * group * length
        own_all = of_group(own, g)
        for c in range(0, 2 * parts, 2):
            at = slice(c * LANES, (c + 2) * LANES)
            y = (
                mm(own_all, split_ref[2, :, at])
                + mm(own_all, split_ref[1, :, at])
                + mm(own_all, split_ref[0, :, at])
            )
            which, chunk = divmod(c, parts)
            for k in range(SLOTS):
                for i in range(2):
                    to = first + (which * SLOTS + k) * parts + chunk + i
                    out_ref[pl.ds(to, group, stride=length), :] = y[
                        k * group : (k + 1) * group, i * LANES : (i + 1) * LANES
                    ]
        to_left = pick(of_group(left, g), left_rows)
        to_right = pick(of_group(right, g), both_rows)
        for k in range(SLOTS):
            part = slice(k * group, (k + 1) * group)
            out_ref[pl.ds(first + base + k, group, stride=length), :] = to_left[part]
            out_ref[pl.ds(first + base + SLOTS + k, group, stride=length), :] = to_right[part]
        span = pl.ds(first, group * length)
        send = pltpu.make_async_copy(out_ref.at[span], out_hbm.at[span], out_sem.at[g])
        send.start()
        sends.append(send)
    for send in sends:
        send.wait()


def slot_rows(got_ref, length, at, devices):
    return got_ref[pl.ds(at, devices, stride=length), :]


def odd_row():
    return lax.rem(lax.axis_index("ty"), 2)


def to_partners(ref, near_ref, next_ref):
    rows, count = ref.shape[0], near_ref.shape[0]
    bottom = (rows - count) * (1 - odd_row())
    near_ref[...] = ref[pl.ds(pl.multiple_of(bottom, 8), count), :]
    next_ref[...] = ref[pl.ds(pl.multiple_of(rows - count - bottom, 8), count), :]


def from_partners(n_ty, near_ref, next_ref, at):
    row_at, odd = lax.axis_index("ty"), odd_row() == 1
    near, far = near_ref[:, at], next_ref[:, at]
    above = jnp.where(odd, near, far) * jnp.where(row_at > 0, 1.0, 0.0)
    below = jnp.where(odd, far, near) * jnp.where(row_at < n_ty - 1, 1.0, 0.0)
    return above, below


def gather_tile(got_ref, parts, length, which, select, dst, extra):
    devices = got_ref.shape[0] // length
    for c in range(0, parts, 2):
        x = jnp.concatenate(
            [
                jnp.concatenate(
                    [
                        slot_rows(got_ref, length, (which * SLOTS + k) * parts + c + i, devices)
                        for i in range(2)
                    ],
                    axis=1,
                )
                for k in range(SLOTS)
            ],
            axis=0,
        )
        at = slice(c * LANES, (c + 2) * LANES)
        y = pick(select, x)
        dst[:, at] = y if extra is None else y + extra[:, at]


def sums_kernel(parts, length, got_ref, s_ref, near_ref, next_ref, select_ref, strip_ref):
    rows, wide = s_ref.shape
    cols = wide - LANES
    devices = got_ref.shape[0] // length
    base = 2 * SLOTS * parts
    from_left = [slot_rows(got_ref, length, base + k, devices) for k in range(SLOTS)]
    from_right = [slot_rows(got_ref, length, base + SLOTS + k, devices) for k in range(SLOTS)]
    first_lane = iota((devices, LANES), 1) == 0
    numbers = [
        jnp.transpose(jnp.where(first_lane, x, y)) for x, y in zip(from_left, from_right)
    ]
    wanted = (iota((rows, devices), 0) + 1).astype(F32)

    def chooser(lists, at):
        return jnp.concatenate(
            [jnp.where(x[at : at + 1, :] == wanted, 1.0, 0.0) for x in lists], axis=1
        ).astype(BF16)

    own = chooser(numbers, 97)
    select_ref[...] = own
    gather_tile(got_ref, parts, length, 0, own, s_ref, None)
    left = pick(chooser(numbers, 0), jnp.concatenate(from_left, axis=0))
    right = pick(chooser(numbers, 96), jnp.concatenate(from_right, axis=0))
    lane = iota((rows, LANES), 1)
    s_ref[:, cols:] = jnp.where(lane < 64, right, left)
    strip_ref[...] = jnp.where(lane < 64, pltpu.roll(right, 64, 1), pltpu.roll(left, 64, 1))
    to_partners(s_ref, near_ref, next_ref)


def weights_kernel(
    parts, length, n_tx, got_ref, prior_ref, prior_halo_ref, select_ref, strip_ref,
    w_ref
):
    rows, wide = w_ref.shape
    cols = wide - LANES
    gather_tile(got_ref, parts, length, 1, select_ref[...], w_ref, prior_ref)
    lane = iota((rows, LANES), 1)
    column = lax.axis_index(TX)
    has_left = jnp.where(column > 0, 1.0, 0.0)
    has_right = jnp.where(column < n_tx - 1, 1.0, 0.0)
    prior_halo = prior_halo_ref[...]
    strip = strip_ref[...]
    w_ref[:, cols:] = jnp.where(
        lane < HALF,
        prior_halo * has_right + strip,
        jnp.where(lane >= LANES - HALF, prior_halo * has_left + strip, 0.0),
    )


def along_columns(pieces, taps_ref):
    height, wide = pieces[0].shape
    cols = wide - LANES

    def stacked(x):
        first = jnp.concatenate([x[:, cols:], x[:, : 3 * LANES]], axis=1)
        rest = [
            x[:, (c - 1) * LANES : (c + 3) * LANES] for c in range(2, cols // LANES, 2)
        ]
        return jnp.concatenate([first] + rest, axis=0)

    half = [stacked(x) for x in pieces]
    out = []
    for r in range(0, half[0].shape[0], 2 * height):
        y = times_taps([x[r : r + 2 * height] for x in half], taps_ref)
        out += [y[:height], y[height:]]
    return out


def all_columns(mid, y0_ref, at, col_ref, edge_ref):
    wide = mid.shape[1]
    cols = wide - LANES
    pieces = split3(mid)
    for c, y in enumerate(along_columns(pieces, col_ref)):
        y0_ref[at, 2 * c * LANES : 2 * (c + 1) * LANES] = y
    near = [jnp.concatenate([x[:, cols - LANES :], x[:, :LANES]], axis=1) for x in pieces]
    y0_ref[at, cols:] = times_taps(near, edge_ref)


def early_kernel(
    s_ref,
    w_ref,
    own_ref,
    col_ref,
    edge_ref,
    part_ref,
    deep_ref,
    root_ref,
    r0_ref,
    sums_ref,
    near_ref,
    next_ref,
    mid_ref,
):
    rows, wide = s_ref.shape
    cols = wide - LANES
    edge = 4 * HALF
    to_partners(w_ref, near_ref, next_ref)
    for at in spans(wide):
        mid = taps_times(own_ref, s_ref[:, at])
        part_ref[:, at] = mid[:edge]
        mid_ref[:, at] = mid[edge:]
    all_columns(mid_ref[...], deep_ref, slice(None), col_ref, edge_ref)
    total_rr = total_rb = jnp.zeros((8, cols), F32)
    for r in range(0, rows, 8):
        at = slice(r, r + 8)
        root = jnp.sqrt(w_ref[at, :cols])
        s = s_ref[at, :cols]
        r0 = s / root
        root_ref[at, :] = root
        r0_ref[at, :] = r0
        total_rr += r0 * r0
        if HALF <= r < rows - HALF:
            total_rb += s * deep_ref[r - HALF : r - HALF + 8, :cols]
    sums_ref[0:8, :] = folded(total_rr)
    sums_ref[8:16, :] = folded(total_rb)


def first_kernel(
    n_ty,
    s_ref,
    near_ref,
    next_ref,
    part_ref,
    early_ref,
    halo_ref,
    col_ref,
    edge_ref,
    border_ref,
    sums_ref,
    mid_ref,
):
    rows, wide = s_ref.shape
    cols = wide - LANES
    for at in spans(wide):
        halo = jnp.concatenate(from_partners(n_ty, near_ref, next_ref, at), axis=0)
        mid_ref[:, at] = part_ref[:, at] + taps_times(halo_ref, halo)
    all_columns(mid_ref[...], border_ref, slice(None), col_ref, edge_ref)
    two = 2 * HALF
    top = s_ref[:HALF, :cols] * border_ref[HALF:two, :cols]
    bottom = s_ref[rows - HALF :, :cols] * border_ref[two : two + HALF, :cols]
    sums_ref[0:8, :] = early_ref[0:8, :]
    sums_ref[8:16, :] = early_ref[8:16, :] + folded(top) + folded(bottom)


def folded(total):
    rows, cols = total.shape
    total = sum(total[r : r + 8] for r in range(0, rows, 8))
    return sum(total[:, c : c + LANES] for c in range(0, cols, LANES))


def whole(total):
    return jnp.sum(jnp.sum(total, axis=0, keepdims=True), axis=1, keepdims=True)


def second_kernel(
    n_ty,
    w_ref,
    near_ref,
    next_ref,
    deep_ref,
    border_ref,
    root_ref,
    r0_ref,
    first_ref,
    row_ref,
    col_ref,
    b0_ref,
    b1_ref,
    moments_ref,
    mid_ref,
):
    rows, wide = w_ref.shape
    cols = wide - LANES
    one, two, three = HALF, 2 * HALF, 3 * HALF
    m0, n1 = whole(first_ref[0:8, :]), whole(first_ref[8:16, :])
    c0 = n1 / jnp.where(m0 > 0.0, m0, 1.0)
    for at in spans(wide):
        above, below = from_partners(n_ty, near_ref, next_ref, at)
        z = jnp.concatenate(
            [
                above * border_ref[:one, at],
                w_ref[:one, at] * border_ref[one:two, at],
                w_ref[one : rows - one, at] * deep_ref[:, at],
                w_ref[rows - one :, at] * border_ref[two:three, at],
                below * border_ref[three:, at],
            ],
            axis=0,
        )
        mid_ref[:, at] = taps_times(row_ref, z)
    total_vv = total_rv = total_vq = total_mix = jnp.zeros((8, LANES), F32)
    for c, y1 in enumerate(along_columns(split3(mid_ref[...]), col_ref)):
        at = slice(2 * c * LANES, 2 * (c + 1) * LANES)
        y0 = jnp.concatenate(
            [border_ref[one:two, at], deep_ref[:, at], border_ref[two:three, at]], axis=0
        )
        r0, root = r0_ref[:, at], root_ref[:, at]
        b0, b1 = root * y0, root * y1
        b0_ref[:, at] = b0
        b1_ref[:, at] = b1
        v, q = b0 - c0 * r0, b1 - c0 * b0
        total_vv += folded(v * v)
        total_rv += folded(r0 * v)
        total_vq += folded(v * q)
        total_mix += folded(v * b0 + r0 * q)
    lane = iota((1, LANES), 1)
    known = jnp.zeros((1, LANES), F32)
    totals = (whole(x) for x in (total_vv, total_rv, total_vq, total_mix))
    for i, value in enumerate((m0, n1, c0, *totals)):
        known = jnp.where(lane == i, value, known)
    moments_ref[...] = jnp.broadcast_to(known, moments_ref.shape)


def final_kernel(moments_ref, r0_ref, b0_ref, b1_ref, x_hbm, r_hbm, x_ref, r_ref, sem):
    parts = jnp.transpose(moments_ref[...])
    m0_at, n1_at, c_at, vv_at, rv_at, vq_at, mix_at = (parts[i : i + 1, :] for i in range(7))

    def total(x):
        return jnp.sum(x, axis=1, keepdims=True)

    m0, n1 = total(m0_at), total(n1_at)
    mu = n1 / m0
    shift = c_at - mu
    vv = total(vv_at + shift * (2.0 * rv_at + shift * m0_at))
    vbv = total(vq_at + shift * (mix_at + shift * n1_at))
    a = m0 / (0.5 * m0 + n1)
    ratio = vv / m0
    beta = a * a * ratio
    step = vv / (0.5 * vv + vbv - a * vv * ratio)
    x_r0 = a + step * beta + step * a * mu
    x_b0 = -step * a
    r_r0 = a * mu - step * (0.5 * a * mu + 0.5 * beta)
    r_b0 = -a - step * (a * mu - 0.5 * a + beta)
    r_b1 = step * a
    sends = []
    step_rows = r0_ref.shape[0] // CHUNKS
    for c in range(CHUNKS):
        at = slice(c * step_rows, (c + 1) * step_rows)
        r0 = r0_ref[at, :]
        b0 = b0_ref[at, :]
        x_ref[at, :] = x_r0 * r0 + x_b0 * b0
        r_ref[at, :] = r_r0 * r0 + r_b0 * b0 + r_b1 * b1_ref[at, :]
        for i, (src, dst) in enumerate(((x_ref, x_hbm), (r_ref, r_hbm))):
            send = pltpu.make_async_copy(src.at[at], dst.at[at], sem.at[c, i])
            send.start()
            sends.append(send)
    for send in sends:
        send.wait()


VMEM = pl.BlockSpec(memory_space=pltpu.VMEM)
ANY = pl.BlockSpec(memory_space=pl.ANY)
HBM = pl.BlockSpec(memory_space=pltpu.HBM)


def call(kernel, shapes, *args, ins=None, outs=None, scratch=(), name, limit=24, flops=0):
    moved = sum(int(np.prod(x.shape)) * x.dtype.itemsize for x in args)
    return pl.pallas_call(
        kernel,
        out_shape=[
            jax.ShapeDtypeStruct(s, F32) if isinstance(s, tuple) else s for s in shapes
        ],
        in_specs=ins or [VMEM] * len(args),
        out_specs=outs or [VMEM] * len(shapes),
        scratch_shapes=list(scratch),
        compiler_params=pltpu.CompilerParams(vmem_limit_bytes=limit << 20),
        cost_estimate=pl.CostEstimate(flops=flops, bytes_accessed=moved, transcendentals=0),
        name=name,
    )(*args)


def neighbours(axes, step):
    count = int(np.prod([lax.axis_size(a) for a in axes]))
    return [(i, (i + step) % count) for i in range(count)]


def shards(block_sums, block_weights, block_tile, block_row, prior_weight):
    devices = lax.axis_size(TY_TX)
    n_tx = lax.axis_size(TX)
    blocks, _, cols = block_sums.shape
    rows = prior_weight.shape[0]
    parts = cols // LANES
    length = 2 * SLOTS * parts + 2 * SLOTS
    wide = cols + LANES

    prior_right = lax.ppermute(prior_weight[:, :LANES], TX, neighbours(TX, -1))
    prior_left = lax.ppermute(prior_weight[:, cols - LANES :], TX, neighbours(TX, 1))
    lane = jnp.arange(LANES)[None, :]
    prior_halo = jnp.where(lane < HALF, prior_right, jnp.where(lane >= LANES - HALF, prior_left, 0.0))

    (message,) = call(
        functools.partial(pack_kernel, n_tx, parts, length),
        [(devices * length, LANES)],
        block_tile.reshape(1, blocks),
        block_row.reshape(1, blocks),
        block_sums.reshape(blocks * parts, LANES),
        block_weights.reshape(blocks * parts, LANES),
        ins=[HBM] * 4,
        outs=[HBM],
        scratch=[
            pltpu.VMEM((1, blocks), jnp.int32),
            pltpu.VMEM((1, blocks), jnp.int32),
            pltpu.VMEM((blocks * parts, LANES), F32),
            pltpu.VMEM((blocks * parts, LANES), F32),
            pltpu.VMEM((3, blocks, 2 * cols), BF16),
            pltpu.VMEM((devices * length, LANES), F32),
            pltpu.SemaphoreType.DMA((4,)),
            pltpu.SemaphoreType.DMA((GROUPS,)),
        ],
        name="pack",
        limit=63,
    )
    got = lax.all_to_all(
        message.reshape(devices, 1, length * LANES), TY_TX, split_axis=0, concat_axis=0, tiled=True
    ).reshape(devices * length, LANES)
    s_slab, w_slab = (2 * HALF, wide), (HALF, wide)
    s, s_near, s_next, chosen, strip = call(
        functools.partial(sums_kernel, parts, length),
        [
            (rows, wide),
            s_slab,
            s_slab,
            jax.ShapeDtypeStruct((rows, SLOTS * devices), BF16),
            (rows, LANES),
        ],
        got,
        flops=3 * 2 * rows * wide * SLOTS * devices,
        name="sums",
    )
    (w,) = call(
        functools.partial(weights_kernel, parts, length, n_tx),
        [(rows, wide)],
        got,
        prior_weight,
        prior_halo,
        chosen,
        strip,
        flops=3 * 2 * rows * wide * SLOTS * devices,
        name="weights",
    )
    n_ty = lax.axis_size("ty")
    swaps = [(i, i ^ 1) for i in range(n_ty)]
    far = [((i + 1) % n_ty, ((i ^ 1) + 1) % n_ty) for i in range(n_ty)]
    s_near, s_next = lax.ppermute(s_near, "ty", swaps), lax.ppermute(s_next, "ty", far)

    tall = rows + 2 * HALF
    col_taps = taps(np.arange(2 * LANES)[None, :] - np.arange(4 * LANES)[:, None] + LANES, 0)
    ring = np.where(np.arange(LANES) < 64, cols, -LANES) + np.arange(LANES)
    near = np.concatenate([np.arange(cols - LANES, cols), ring, np.arange(LANES)])
    edge_taps = taps(ring[None, :] - near[:, None], 0)
    tile = (rows, cols)
    inside = np.arange(rows)
    border_rows = np.concatenate(
        [np.arange(-HALF, HALF), np.arange(rows - HALF, rows + HALF)]
    )
    early_rows = np.concatenate([border_rows, inside[HALF : rows - HALF]])
    far_rows = np.concatenate([np.arange(-2 * HALF, 0), np.arange(rows, rows + 2 * HALF)])
    early_taps = taps(early_rows[:, None] - inside[None, :], 0)
    first_taps = taps(border_rows[:, None] - far_rows[None, :], 0)
    part, deep, root, r0, early, w_near, w_next = call(
        early_kernel,
        [(4 * HALF, wide), (rows - 2 * HALF, wide), tile, tile, (16, LANES), w_slab, w_slab],
        s,
        w,
        early_taps,
        col_taps,
        edge_taps,
        scratch=[pltpu.VMEM((rows - 2 * HALF, wide), F32)],
        flops=5 * 2 * tall * wide * 3 * LANES,
        name="early",
    )
    w_near, w_next = lax.ppermute(w_near, "ty", swaps), lax.ppermute(w_next, "ty", far)
    border, early = call(
        functools.partial(first_kernel, n_ty),
        [(4 * HALF, wide), (16, LANES)],
        s,
        s_near,
        s_next,
        part,
        early,
        first_taps,
        col_taps,
        edge_taps,
        scratch=[pltpu.VMEM((4 * HALF, wide), F32)],
        flops=5 * 2 * rows * wide * 6 * LANES,
        name="first",
    )
    second_taps = taps(inside[:, None] - np.arange(-HALF, rows + HALF)[None, :], 0)
    b0, b1, moments = call(
        functools.partial(second_kernel, n_ty),
        [tile, tile, (devices, LANES)],
        w,
        w_near,
        w_next,
        deep,
        border,
        root,
        r0,
        early,
        second_taps,
        col_taps,
        scratch=[pltpu.VMEM((rows, wide), F32)],
        flops=5 * 2 * rows * wide * 6 * LANES,
        name="second",
    )
    moments = lax.all_to_all(
        moments.reshape(devices, 1, LANES), TY_TX, split_axis=0, concat_axis=0, tiled=True
    ).reshape(devices, LANES)
    return tuple(
        call(
            final_kernel,
            [tile, tile],
            moments,
            r0,
            b0,
            b1,
            outs=[HBM, HBM],
            scratch=[
                pltpu.VMEM(tile, F32),
                pltpu.VMEM(tile, F32),
                pltpu.SemaphoreType.DMA((CHUNKS, 2)),
            ],
            name="combine",
        )
    )


def solution(mesh):
    split = Mesh(mesh.devices.reshape(mesh.shape["ty"], 4, 4, 2), ("ty", "tx_0", "tx_1", "tx_2"))
    in_specs = (P(TY_TX, None, None), P(TY_TX, None, None), P(TY_TX, None), P(TY_TX), P("ty", TX))
    out_specs = (P("ty", TX), P("ty", TX))
    return jax.shard_map(
        shards, mesh=split, in_specs=in_specs, out_specs=out_specs, check_vma=False
    )
```

```python
import functools

import jax
import jax.numpy as jnp
import numpy as np
from jax import lax
from jax.experimental import pallas as pl
from jax.experimental.pallas import tpu as pltpu
from jax.sharding import Mesh
from jax.sharding import PartitionSpec as P

HALF = 32
LANES = 128
SLOTS = 2
GROUPS = 2
CHUNKS = 4
TY_TX = ("ty", "tx_0", "tx_1", "tx_2")
TX = ("tx_0", "tx_1", "tx_2")
F32 = jnp.float32
BF16 = jnp.bfloat16


def taps(offset, axis):
    def raw(d):
        scaled = np.abs(d) / (HALF + 1.0)
        return np.where(np.abs(d) <= HALF, (1.0 - scaled) ** 4 * (1.0 + 4.0 * scaled), 0.0)

    values = raw(offset) / raw(np.arange(-HALF, HALF + 1)).sum()
    head = values.astype(BF16)
    tail = (values - head.astype(np.float64)).astype(BF16)
    return jnp.asarray(np.concatenate([head, tail], axis=axis))


def split3(x):
    head = x.astype(BF16)
    rest = x - head.astype(F32)
    mid = rest.astype(BF16)
    return head, mid, (rest - mid.astype(F32)).astype(BF16)


def mm(a, b):
    return jnp.dot(a, b, preferred_element_type=F32)


def pick(select, x):
    head, mid, tail = split3(x)
    return mm(select, tail) + mm(select, mid) + mm(select, head)


def taps_times(taps_ref, x):
    rows = taps_ref.shape[0] // 2
    xh, xm, xl = split3(x)
    low = mm(taps_ref[:rows, :], xl)
    mid = mm(taps_ref[...], xm)
    high = mm(taps_ref[...], xh)
    return low + mid[rows:] + high[rows:] + mid[:rows] + high[:rows]


def times_taps(pieces, taps_ref):
    xh, xm, xl = pieces
    depth = taps_ref.shape[0] // 2
    head, tail = taps_ref[:depth, :], taps_ref[depth:, :]
    return mm(xl, head) + mm(xm, tail) + mm(xh, tail) + mm(xm, head) + mm(xh, head)


def spans(wide):
    cols = wide - LANES
    return [slice(c, c + 2 * LANES) for c in range(0, cols, 2 * LANES)] + [slice(cols, wide)]


def iota(shape, dim):
    return lax.broadcasted_iota(jnp.int32, shape, dim)


def pack_kernel(
    n_tx, parts, length, tile_hbm, row_hbm, sums_hbm, weights_hbm, out_hbm,
    tile_ref, row_ref, sums_ref, weights_ref, split_ref, out_ref, in_sem, out_sem
):
    fetches = [
        pltpu.make_async_copy(src, dst, in_sem.at[i])
        for i, (src, dst) in enumerate(
            (
                (tile_hbm, tile_ref),
                (row_hbm, row_ref),
                (sums_hbm, sums_ref),
                (weights_hbm, weights_ref),
            )
        )
    ]
    for fetch in fetches:
        fetch.start()
    fetches[0].wait()
    fetches[1].wait()
    count = tile_ref.shape[1]
    devices = out_ref.shape[0] // length
    group = devices // GROUPS
    tile = tile_ref[...]
    t = iota((devices, count), 0)
    same = tile == t
    earlier = iota((count, count), 0) < iota((count, count), 1)
    before = mm(same.astype(F32).astype(BF16), earlier.astype(F32).astype(BF16))
    rank = jnp.sum(jnp.where(same, before, 0.0), axis=0, keepdims=True)
    column = lax.rem(t, n_tx)
    from_left = (tile + 1 == t) & (column != 0)
    from_right = (tile - 1 == t) & (column != n_tx - 1)

    def onehot(mask, k):
        return jnp.where(mask & (rank == float(k)), 1.0, 0.0)

    own = [onehot(same, k) for k in range(SLOTS)]
    left = [onehot(from_left, k) for k in range(SLOTS)]
    right = [
        jnp.concatenate([onehot(from_right, k), own[k]], axis=1) for k in range(SLOTS)
    ]

    def of_group(masks, g):
        part = slice(g * group, (g + 1) * group)
        return jnp.concatenate([m[part] for m in masks], axis=0).astype(BF16)

    lane = iota((count, LANES), 1)
    number = jnp.transpose(jnp.broadcast_to(row_ref[...].astype(F32) + 1.0, (count, count)))
    for which, ref in enumerate((sums_ref, weights_ref)):
        fetches[2 + which].wait()
        for c in range(parts):
            at = slice((which * parts + c) * LANES, (which * parts + c + 1) * LANES)
            for i, piece in enumerate(split3(ref[pl.ds(c, count, stride=parts), :])):
                split_ref[i, :, at] = piece

    last = parts - 1
    s_last = sums_ref[pl.ds(last, count, stride=parts), :]
    w_last = pltpu.roll(weights_ref[pl.ds(last, count, stride=parts), :], 64, 1)
    s_first = sums_ref[pl.ds(0, count, stride=parts), :]
    w_first = pltpu.roll(weights_ref[pl.ds(0, count, stride=parts), :], 64, 1)
    left_rows = jnp.where(
        lane >= 64, s_last, jnp.where(lane >= 32, w_last, jnp.where(lane == 0, number, 0.0))
    )
    right_rows = jnp.where(
        lane < 64, s_first, jnp.where(lane < 96, w_first, jnp.where(lane == 96, number, 0.0))
    )
    own_rows = jnp.where(lane == 97, number, 0.0)
    both_rows = jnp.concatenate([right_rows, own_rows], axis=0)

    base = 2 * SLOTS * parts
    sends = []
    for g in range(GROUPS):
        first = g * group * length
        own_all = of_group(own, g)
        for c in range(0, 2 * parts, 2):
            at = slice(c * LANES, (c + 2) * LANES)
            y = (
                mm(own_all, split_ref[2, :, at])
                + mm(own_all, split_ref[1, :, at])
                + mm(own_all, split_ref[0, :, at])
            )
            which, chunk = divmod(c, parts)
            for k in range(SLOTS):
                for i in range(2):
                    to = first + (which * SLOTS + k) * parts + chunk + i
                    out_ref[pl.ds(to, group, stride=length), :] = y[
                        k * group : (k + 1) * group, i * LANES : (i + 1) * LANES
                    ]
        to_left = pick(of_group(left, g), left_rows)
        to_right = pick(of_group(right, g), both_rows)
        for k in range(SLOTS):
            part = slice(k * group, (k + 1) * group)
            out_ref[pl.ds(first + base + k, group, stride=length), :] = to_left[part]
            out_ref[pl.ds(first + base + SLOTS + k, group, stride=length), :] = to_right[part]
        span = pl.ds(first, group * length)
        send = pltpu.make_async_copy(out_ref.at[span], out_hbm.at[span], out_sem.at[g])
        send.start()
        sends.append(send)
    for send in sends:
        send.wait()


def slot_rows(got_ref, length, at, devices):
    return got_ref[pl.ds(at, devices, stride=length), :]


def odd_row():
    return lax.rem(lax.axis_index("ty"), 2)


def to_partners(ref, near_ref, next_ref):
    rows, count = ref.shape[0], near_ref.shape[0]
    bottom = (rows - count) * (1 - odd_row())
    near_ref[...] = ref[pl.ds(pl.multiple_of(bottom, 8), count), :]
    next_ref[...] = ref[pl.ds(pl.multiple_of(rows - count - bottom, 8), count), :]


def from_partners(n_ty, near_ref, next_ref, at):
    row_at, odd = lax.axis_index("ty"), odd_row() == 1
    near, far = near_ref[:, at], next_ref[:, at]
    above = jnp.where(odd, near, far) * jnp.where(row_at > 0, 1.0, 0.0)
    below = jnp.where(odd, far, near) * jnp.where(row_at < n_ty - 1, 1.0, 0.0)
    return above, below


def gather_tile(got_ref, parts, length, which, select, dst, extra):
    devices = got_ref.shape[0] // length
    for c in range(0, parts, 2):
        x = jnp.concatenate(
            [
                jnp.concatenate(
                    [
                        slot_rows(got_ref, length, (which * SLOTS + k) * parts + c + i, devices)
                        for i in range(2)
                    ],
                    axis=1,
                )
                for k in range(SLOTS)
            ],
            axis=0,
        )
        at = slice(c * LANES, (c + 2) * LANES)
        y = pick(select, x)
        dst[:, at] = y if extra is None else y + extra[:, at]


def sums_kernel(parts, length, got_ref, s_ref, near_ref, next_ref, select_ref, strip_ref):
    rows, wide = s_ref.shape
    cols = wide - LANES
    devices = got_ref.shape[0] // length
    base = 2 * SLOTS * parts
    from_left = [slot_rows(got_ref, length, base + k, devices) for k in range(SLOTS)]
    from_right = [slot_rows(got_ref, length, base + SLOTS + k, devices) for k in range(SLOTS)]
    left_t = [jnp.transpose(x) for x in from_left]
    right_t = [jnp.transpose(x) for x in from_right]
    wanted = (iota((rows, devices), 0) + 1).astype(F32)

    def chooser(lists, at):
        return jnp.concatenate(
            [jnp.where(x[at : at + 1, :] == wanted, 1.0, 0.0) for x in lists], axis=1
        ).astype(BF16)

    own = chooser(right_t, 97)
    select_ref[...] = own
    gather_tile(got_ref, parts, length, 0, own, s_ref, None)
    left = pick(chooser(left_t, 0), jnp.concatenate(from_left, axis=0))
    right = pick(chooser(right_t, 96), jnp.concatenate(from_right, axis=0))
    lane = iota((rows, LANES), 1)
    s_ref[:, cols:] = jnp.where(lane < 64, right, left)
    strip_ref[...] = jnp.where(lane < 64, pltpu.roll(right, 64, 1), pltpu.roll(left, 64, 1))
    to_partners(s_ref, near_ref, next_ref)


def weights_kernel(
    parts, length, n_tx, got_ref, prior_ref, prior_halo_ref, select_ref, strip_ref,
    w_ref
):
    rows, wide = w_ref.shape
    cols = wide - LANES
    gather_tile(got_ref, parts, length, 1, select_ref[...], w_ref, prior_ref)
    lane = iota((rows, LANES), 1)
    column = lax.axis_index(TX)
    has_left = jnp.where(column > 0, 1.0, 0.0)
    has_right = jnp.where(column < n_tx - 1, 1.0, 0.0)
    prior_halo = prior_halo_ref[...]
    strip = strip_ref[...]
    w_ref[:, cols:] = jnp.where(
        lane < HALF,
        prior_halo * has_right + strip,
        jnp.where(lane >= LANES - HALF, prior_halo * has_left + strip, 0.0),
    )


def along_columns(pieces, taps_ref, together=2):
    height, wide = pieces[0].shape
    cols = wide - LANES

    def stacked(x):
        first = jnp.concatenate([x[:, cols:], x[:, : 3 * LANES]], axis=1)
        rest = [
            x[:, (c - 1) * LANES : (c + 3) * LANES] for c in range(2, cols // LANES, 2)
        ]
        return jnp.concatenate([first] + rest, axis=0)

    half = [stacked(x) for x in pieces]
    out = []
    for r in range(0, half[0].shape[0], together * height):
        y = times_taps([x[r : r + together * height] for x in half], taps_ref)
        out += [y[i * height : (i + 1) * height] for i in range(together)]
    return out


def all_columns(mid, y0_ref, at, col_ref, edge_ref):
    wide = mid.shape[1]
    cols = wide - LANES
    pieces = split3(mid)
    for c, y in enumerate(along_columns(pieces, col_ref)):
        y0_ref[at, 2 * c * LANES : 2 * (c + 1) * LANES] = y
    near = [jnp.concatenate([x[:, cols - LANES :], x[:, :LANES]], axis=1) for x in pieces]
    y0_ref[at, cols:] = times_taps(near, edge_ref)


def early_kernel(
    s_ref,
    w_ref,
    own_ref,
    col_ref,
    edge_ref,
    part_ref,
    deep_ref,
    root_ref,
    r0_ref,
    sums_ref,
    near_ref,
    next_ref,
    mid_ref,
):
    rows, wide = s_ref.shape
    cols = wide - LANES
    edge = 4 * HALF
    to_partners(w_ref, near_ref, next_ref)
    for at in spans(wide):
        mid = taps_times(own_ref, s_ref[:, at])
        part_ref[:, at] = mid[:edge]
        mid_ref[:, at] = mid[edge:]
    all_columns(mid_ref[...], deep_ref, slice(None), col_ref, edge_ref)
    total_rr = total_rb = jnp.zeros((8, cols), F32)
    for r in range(0, rows, 8):
        at = slice(r, r + 8)
        root = jnp.sqrt(w_ref[at, :cols])
        s = s_ref[at, :cols]
        r0 = s / root
        root_ref[at, :] = root
        r0_ref[at, :] = r0
        total_rr += r0 * r0
        if HALF <= r < rows - HALF:
            total_rb += s * deep_ref[r - HALF : r - HALF + 8, :cols]
    sums_ref[0:8, :] = folded(total_rr)
    sums_ref[8:16, :] = folded(total_rb)


def first_kernel(
    n_ty,
    s_ref,
    near_ref,
    next_ref,
    part_ref,
    early_ref,
    halo_ref,
    col_ref,
    edge_ref,
    border_ref,
    sums_ref,
    mid_ref,
):
    rows, wide = s_ref.shape
    cols = wide - LANES
    for at in spans(wide):
        halo = jnp.concatenate(from_partners(n_ty, near_ref, next_ref, at), axis=0)
        mid_ref[:, at] = part_ref[:, at] + taps_times(halo_ref, halo)
    all_columns(mid_ref[...], border_ref, slice(None), col_ref, edge_ref)
    two = 2 * HALF
    top = s_ref[:HALF, :cols] * border_ref[HALF:two, :cols]
    bottom = s_ref[rows - HALF :, :cols] * border_ref[two : two + HALF, :cols]
    sums_ref[0:8, :] = early_ref[0:8, :]
    sums_ref[8:16, :] = early_ref[8:16, :] + folded(top) + folded(bottom)


def folded(total):
    rows, cols = total.shape
    total = sum(total[r : r + 8] for r in range(0, rows, 8))
    return sum(total[:, c : c + LANES] for c in range(0, cols, LANES))


def whole(total):
    return jnp.sum(jnp.sum(total, axis=0, keepdims=True), axis=1, keepdims=True)


def second_kernel(
    n_ty,
    w_ref,
    near_ref,
    next_ref,
    deep_ref,
    border_ref,
    root_ref,
    r0_ref,
    first_ref,
    row_ref,
    col_ref,
    b0_ref,
    b1_ref,
    moments_ref,
    mid_ref,
):
    rows, wide = w_ref.shape
    cols = wide - LANES
    one, two, three = HALF, 2 * HALF, 3 * HALF
    m0, n1 = whole(first_ref[0:8, :]), whole(first_ref[8:16, :])
    c0 = n1 / jnp.where(m0 > 0.0, m0, 1.0)
    for at in spans(wide):
        above, below = from_partners(n_ty, near_ref, next_ref, at)
        z = jnp.concatenate(
            [
                above * border_ref[:one, at],
                w_ref[:one, at] * border_ref[one:two, at],
                w_ref[one : rows - one, at] * deep_ref[:, at],
                w_ref[rows - one :, at] * border_ref[two:three, at],
                below * border_ref[three:, at],
            ],
            axis=0,
        )
        mid_ref[:, at] = taps_times(row_ref, z)
    total_vv = total_rv = total_vq = total_mix = jnp.zeros((8, LANES), F32)
    for c, y1 in enumerate(along_columns(split3(mid_ref[...]), col_ref, 1)):
        at = slice(2 * c * LANES, 2 * (c + 1) * LANES)
        y0 = jnp.concatenate(
            [border_ref[one:two, at], deep_ref[:, at], border_ref[two:three, at]], axis=0
        )
        r0, root = r0_ref[:, at], root_ref[:, at]
        b0, b1 = root * y0, root * y1
        b0_ref[:, at] = b0
        b1_ref[:, at] = b1
        v, q = b0 - c0 * r0, b1 - c0 * b0
        total_vv += folded(v * v)
        total_rv += folded(r0 * v)
        total_vq += folded(v * q)
        total_mix += folded(v * b0 + r0 * q)
    lane = iota((1, LANES), 1)
    known = jnp.zeros((1, LANES), F32)
    totals = (whole(x) for x in (total_vv, total_rv, total_vq, total_mix))
    for i, value in enumerate((m0, n1, c0, *totals)):
        known = jnp.where(lane == i, value, known)
    moments_ref[...] = jnp.broadcast_to(known, moments_ref.shape)


def final_kernel(moments_ref, r0_ref, b0_ref, b1_ref, x_hbm, r_hbm, x_ref, r_ref, sem):
    parts = jnp.transpose(moments_ref[...])
    m0_at, n1_at, c_at, vv_at, rv_at, vq_at, mix_at = (parts[i : i + 1, :] for i in range(7))

    def total(x):
        return jnp.sum(x, axis=1, keepdims=True)

    m0, n1 = total(m0_at), total(n1_at)
    mu = n1 / m0
    shift = c_at - mu
    vv = total(vv_at + shift * (2.0 * rv_at + shift * m0_at))
    vbv = total(vq_at + shift * (mix_at + shift * n1_at))
    a = m0 / (0.5 * m0 + n1)
    ratio = vv / m0
    beta = a * a * ratio
    step = vv / (0.5 * vv + vbv - a * vv * ratio)
    x_r0 = a + step * beta + step * a * mu
    x_b0 = -step * a
    r_r0 = a * mu - step * (0.5 * a * mu + 0.5 * beta)
    r_b0 = -a - step * (a * mu - 0.5 * a + beta)
    r_b1 = step * a
    sends = []
    step_rows = r0_ref.shape[0] // CHUNKS
    for c in range(CHUNKS):
        at = slice(c * step_rows, (c + 1) * step_rows)
        r0 = r0_ref[at, :]
        b0 = b0_ref[at, :]
        x_ref[at, :] = x_r0 * r0 + x_b0 * b0
        r_ref[at, :] = r_r0 * r0 + r_b0 * b0 + r_b1 * b1_ref[at, :]
        for i, (src, dst) in enumerate(((x_ref, x_hbm), (r_ref, r_hbm))):
            send = pltpu.make_async_copy(src.at[at], dst.at[at], sem.at[c, i])
            send.start()
            sends.append(send)
    for send in sends:
        send.wait()


VMEM = pl.BlockSpec(memory_space=pltpu.VMEM)
ANY = pl.BlockSpec(memory_space=pl.ANY)
HBM = pl.BlockSpec(memory_space=pltpu.HBM)


def call(kernel, shapes, *args, ins=None, outs=None, scratch=(), name, limit=24, flops=0):
    moved = sum(int(np.prod(x.shape)) * x.dtype.itemsize for x in args)
    return pl.pallas_call(
        kernel,
        out_shape=[
            jax.ShapeDtypeStruct(s, F32) if isinstance(s, tuple) else s for s in shapes
        ],
        in_specs=ins or [VMEM] * len(args),
        out_specs=outs or [VMEM] * len(shapes),
        scratch_shapes=list(scratch),
        compiler_params=pltpu.CompilerParams(vmem_limit_bytes=limit << 20),
        cost_estimate=pl.CostEstimate(flops=flops, bytes_accessed=moved, transcendentals=0),
        name=name,
    )(*args)


def neighbours(axes, step):
    count = int(np.prod([lax.axis_size(a) for a in axes]))
    return [(i, (i + step) % count) for i in range(count)]


def shards(block_sums, block_weights, block_tile, block_row, prior_weight):
    devices = lax.axis_size(TY_TX)
    n_tx = lax.axis_size(TX)
    blocks, _, cols = block_sums.shape
    rows = prior_weight.shape[0]
    parts = cols // LANES
    length = 2 * SLOTS * parts + 2 * SLOTS
    wide = cols + LANES

    prior_right = lax.ppermute(prior_weight[:, :LANES], TX, neighbours(TX, -1))
    prior_left = lax.ppermute(prior_weight[:, cols - LANES :], TX, neighbours(TX, 1))
    lane = jnp.arange(LANES)[None, :]
    prior_halo = jnp.where(lane < HALF, prior_right, jnp.where(lane >= LANES - HALF, prior_left, 0.0))

    (message,) = call(
        functools.partial(pack_kernel, n_tx, parts, length),
        [(devices * length, LANES)],
        block_tile.reshape(1, blocks),
        block_row.reshape(1, blocks),
        block_sums.reshape(blocks * parts, LANES),
        block_weights.reshape(blocks * parts, LANES),
        ins=[HBM] * 4,
        outs=[HBM],
        scratch=[
            pltpu.VMEM((1, blocks), jnp.int32),
            pltpu.VMEM((1, blocks), jnp.int32),
            pltpu.VMEM((blocks * parts, LANES), F32),
            pltpu.VMEM((blocks * parts, LANES), F32),
            pltpu.VMEM((3, blocks, 2 * cols), BF16),
            pltpu.VMEM((devices * length, LANES), F32),
            pltpu.SemaphoreType.DMA((4,)),
            pltpu.SemaphoreType.DMA((GROUPS,)),
        ],
        name="pack",
        limit=63,
    )
    got = lax.all_to_all(
        message.reshape(devices, 1, length * LANES), TY_TX, split_axis=0, concat_axis=0, tiled=True
    ).reshape(devices * length, LANES)
    s_slab, w_slab = (2 * HALF, wide), (HALF, wide)
    s, s_near, s_next, chosen, strip = call(
        functools.partial(sums_kernel, parts, length),
        [
            (rows, wide),
            s_slab,
            s_slab,
            jax.ShapeDtypeStruct((rows, SLOTS * devices), BF16),
            (rows, LANES),
        ],
        got,
        flops=3 * 2 * rows * wide * SLOTS * devices,
        name="sums",
    )
    (w,) = call(
        functools.partial(weights_kernel, parts, length, n_tx),
        [(rows, wide)],
        got,
        prior_weight,
        prior_halo,
        chosen,
        strip,
        flops=3 * 2 * rows * wide * SLOTS * devices,
        name="weights",
    )
    n_ty = lax.axis_size("ty")
    swaps = [(i, i ^ 1) for i in range(n_ty)]
    far = [((i + 1) % n_ty, ((i ^ 1) + 1) % n_ty) for i in range(n_ty)]
    s_near, s_next = lax.ppermute(s_near, "ty", swaps), lax.ppermute(s_next, "ty", far)

    tall = rows + 2 * HALF
    col_taps = taps(np.arange(2 * LANES)[None, :] - np.arange(4 * LANES)[:, None] + LANES, 0)
    ring = np.where(np.arange(LANES) < 64, cols, -LANES) + np.arange(LANES)
    near = np.concatenate([np.arange(cols - LANES, cols), ring, np.arange(LANES)])
    edge_taps = taps(ring[None, :] - near[:, None], 0)
    tile = (rows, cols)
    inside = np.arange(rows)
    border_rows = np.concatenate(
        [np.arange(-HALF, HALF), np.arange(rows - HALF, rows + HALF)]
    )
    early_rows = np.concatenate([border_rows, inside[HALF : rows - HALF]])
    far_rows = np.concatenate([np.arange(-2 * HALF, 0), np.arange(rows, rows + 2 * HALF)])
    early_taps = taps(early_rows[:, None] - inside[None, :], 0)
    first_taps = taps(border_rows[:, None] - far_rows[None, :], 0)
    part, deep, root, r0, early, w_near, w_next = call(
        early_kernel,
        [(4 * HALF, wide), (rows - 2 * HALF, wide), tile, tile, (16, LANES), w_slab, w_slab],
        s,
        w,
        early_taps,
        col_taps,
        edge_taps,
        scratch=[pltpu.VMEM((rows - 2 * HALF, wide), F32)],
        flops=5 * 2 * tall * wide * 3 * LANES,
        name="early",
    )
    w_near, w_next = lax.ppermute(w_near, "ty", swaps), lax.ppermute(w_next, "ty", far)
    border, early = call(
        functools.partial(first_kernel, n_ty),
        [(4 * HALF, wide), (16, LANES)],
        s,
        s_near,
        s_next,
        part,
        early,
        first_taps,
        col_taps,
        edge_taps,
        scratch=[pltpu.VMEM((4 * HALF, wide), F32)],
        flops=5 * 2 * rows * wide * 6 * LANES,
        name="first",
    )
    second_taps = taps(inside[:, None] - np.arange(-HALF, rows + HALF)[None, :], 0)
    b0, b1, moments = call(
        functools.partial(second_kernel, n_ty),
        [tile, tile, (devices, LANES)],
        w,
        w_near,
        w_next,
        deep,
        border,
        root,
        r0,
        early,
        second_taps,
        col_taps,
        scratch=[pltpu.VMEM((rows, wide), F32)],
        flops=5 * 2 * rows * wide * 6 * LANES,
        name="second",
    )
    moments = lax.all_to_all(
        moments.reshape(devices, 1, LANES), TY_TX, split_axis=0, concat_axis=0, tiled=True
    ).reshape(devices, LANES)
    return tuple(
        call(
            final_kernel,
            [tile, tile],
            moments,
            r0,
            b0,
            b1,
            outs=[HBM, HBM],
            scratch=[
                pltpu.VMEM(tile, F32),
                pltpu.VMEM(tile, F32),
                pltpu.SemaphoreType.DMA((CHUNKS, 2)),
            ],
            name="combine",
        )
    )


def solution(mesh):
    split = Mesh(mesh.devices.reshape(mesh.shape["ty"], 4, 4, 2), ("ty", "tx_0", "tx_1", "tx_2"))
    in_specs = (P(TY_TX, None, None), P(TY_TX, None, None), P(TY_TX, None), P(TY_TX), P("ty", TX))
    out_specs = (P("ty", TX), P("ty", TX))
    return jax.shard_map(
        shards, mesh=split, in_specs=in_specs, out_specs=out_specs, check_vma=False
    )
```
